512 devices in a mesh: head: 16 (over z), ctx: 32 (over x, y, core).
Axes of the slice: x: 4, y: 4, z: 16, core: 2. Of those that a mesh axis runs over, the one named last changes fastest.
Arguments:
- x_mant: bfloat16 [4096, 16384], P('ctx', 'head'), may hold values from -4 to 4
- x_codes: int32 [4096, 512], P('ctx', 'head'), may hold values from -2 to 2
- bc_raw: bfloat16 [4096, 2048], P('ctx'), may hold values from -5 to 5
- gate_z: bfloat16 [4096, 16384], P('ctx', 'head'), may hold values from -5 to 5
- conv_x: float32 [4, 16384], P(None, 'head'), may hold values from -3 to 3
- conv_bc: float32 [4, 2048], replicated, may hold values from -3 to 3
- dt_raw: float32 [4096, 256], P('ctx', 'head'), may hold values from -4 to 4
- a_log: float32 [256], P('head'), as said below
- d_skip: float32 [256], P('head'), may hold values from 0.5 to 1.5
- norm_gain: float32 [16384], P('head'), may hold values from 0.5 to 1.5
- prompt_lengths: int32 [4], replicated, may hold values from 1 to 2112, 4096 in all
- cache_slot: int32 [4], replicated, may hold values from 0 to 63, as said below
- prefix_state: bfloat16 [64, 16384, 128], P('ctx', 'head'), may hold values from -5 to 5
- tail_x: bfloat16 [64, 3, 16384], P('ctx', None, 'head'), may hold values from -5 to 5
- tail_bc: bfloat16 [64, 3, 2048], P('ctx'), may hold values from -5 to 5
Outputs:
- mixed: bfloat16 [4096, 16384], P('ctx', 'head')
The draws below stay inside these ranges and needn't reach their ends.
Inputs may be any that keep to these rules, and one draw needn't show every extreme that they name: `prompt_lengths`: the lengths sum to 4096, and the longest is exactly 2112. `cache_slot`: slot 63 is read by some prompt and slot 0 by another; prompts may share a slot. `a_log`: log of a positive rate per head.
All inputs are finite; a program needn't handle non-finite values.
Results may differ from the reference program's by a relative error of at most 0.0065.
Values may be sent and summed in bfloat16 or wider, within the bound.
No kernel may reach another device: no remote copies, remote signals or barrier semaphores. Data moves between devices by JAX's collectives and lax.ppermute only.
A program may use at most 64 MiB of HBM per device.

```python
import math
import jax
import jax.numpy as jnp
import numpy as np
from jax import lax

HEADS = 256
P_SIZE = 64
N = 128
GROUPS = 8
KW = 4
MXB = 32
PROMPTS = 4
TOK_DEV = 128
TOKENS = 4096
SLOTS = 64
N_CTX = 32


def draw_a_log(key, part):
    first_key, second_key, third_key = jax.random.split(key, 3)
    share = 0.5
    slow = jax.random.uniform(first_key, (HEADS,), jnp.float32) < share
    slow_log = jax.random.uniform(second_key, (HEADS,), jnp.float32, jnp.log(0.25 / TOKENS), jnp.log(2.0 / TOKENS))
    fast_log = jax.random.uniform(third_key, (HEADS,), jnp.float32, jnp.log(1.0 / 50.0), jnp.log(1.0 / 30.0))
    return jnp.where(slow, slow_log, fast_log).astype(jnp.float32)


def draw_cache_slot(key, part):
    first_key, second_key = jax.random.split(jax.random.fold_in(key, 7))
    slots = jax.random.randint(first_key, (PROMPTS,), 0, SLOTS).astype(jnp.int32)
    order = jax.random.permutation(second_key, PROMPTS)
    slots = slots.at[order[0]].set(0).at[order[1]].set(SLOTS - 1)
    return slots.astype(jnp.int32)


def place_ends(result, key, smallest, high):
    extent = result.shape
    index_at = [jax.random.randint(jax.random.fold_in(key, axis), (), 0, extent[axis]) for axis in range(len(extent))]
    result = result.at[tuple(index_at)].set(smallest)
    longest = extent.index(max(extent))
    index_at[longest] = (index_at[longest] + 1) % extent[longest]
    return result.at[tuple(index_at)].set(high)


def shard_levels(own_key, extent, shards, low, high):
    def one(axis_at, shards_of):
        heights = jax.random.uniform(jax.random.fold_in(jax.random.fold_in(own_key, 6), axis_at), (shards_of,), jnp.float32, low / len(shards), high / len(shards))
        return jnp.repeat(jnp.exp(heights), extent[axis_at] // shards_of).reshape((-1,) + (1,) * (len(extent) - axis_at - 1))

    gain = one(*shards[0])
    for cut in shards[1:]:
        gain = gain * one(*cut)
    return gain


def split_up(amount, total, reach, slope):
    loads = [(1 << 20) // math.isqrt(standing ** slope) + 1 for standing in range(2, amount + 1)]
    surplus, holding = total - reach - (amount - 1), [1] * (amount - 1)
    while surplus > 0:
        movable = [i for i in range(amount - 1) if holding[i] < reach]
        pool, remaining = sum([loads[i] for i in movable]), surplus
        for i in movable:
            addition = min(reach - holding[i], max(1, remaining * loads[i] // pool), surplus)
            holding[i] = holding[i] + addition
            surplus = surplus - addition
    return np.array([reach] + holding)


def ragged_sizes(own_key, amount, total, reach, slope):
    if amount == 2:
        one = jax.random.randint(own_key, (), max(1, total - reach), min(reach, total - 1) + 1)
        return jnp.stack([one, total - one])
    tallies = jnp.asarray(split_up(amount, total, reach, slope), jnp.int32)
    pairs = (amount - 1) // 2
    donor, taker = tallies[1:1 + 2 * pairs:2], tallies[2:2 + 2 * pairs:2]
    slack = jnp.minimum(donor - 1, reach - taker)
    passed = jax.random.randint(jax.random.fold_in(own_key, 1), (pairs,), 0, 1 << 20) % (slack + 1)
    tallies = tallies.at[1:1 + 2 * pairs:2].set(donor - passed).at[2:2 + 2 * pairs:2].set(taker + passed)
    return tallies[jax.random.permutation(jax.random.fold_in(own_key, 2), amount)]


def bell_draw(own_key, dims, scale, reach, cuts=(), kind=jnp.bfloat16):
    values = scale * jax.random.normal(own_key, dims, jnp.float32)
    if cuts:
        values = values * shard_levels(own_key, dims, cuts, -0.22, 0.18)
    return jnp.clip(values, -reach, reach).astype(kind)


def setup_inputs(seed: int = 0) -> dict:
    key_list = jax.random.split(jax.random.key(seed), 16)
    return {
        "x_mant": bell_draw(key_list[0], (TOKENS, HEADS * P_SIZE), 1.0, 4.0, ((0, 32), (1, 16))),
        "x_codes": place_ends(jax.random.randint(key_list[1], (TOKENS, HEADS * P_SIZE // MXB), -2, 3), jax.random.fold_in(key_list[1], 1), -2, 2).astype(jnp.int32),
        "bc_raw": bell_draw(key_list[2], (TOKENS, 2 * GROUPS * N), 1.0, 5.0, ((0, 32),)),
        "gate_z": bell_draw(key_list[3], (TOKENS, HEADS * P_SIZE), 1.0, 5.0, ((0, 32), (1, 16))),
        "conv_x": bell_draw(key_list[4], (KW, HEADS * P_SIZE), KW ** -0.5, 3.0, ((1, 16),), jnp.float32),
        "conv_bc": bell_draw(key_list[5], (KW, 2 * GROUPS * N), KW ** -0.5, 3.0, (), jnp.float32),
        "dt_raw": bell_draw(key_list[6], (TOKENS, HEADS), 1.0, 4.0, ((0, 32), (1, 16)), jnp.float32),
        "a_log": draw_a_log(jax.random.fold_in(key_list[15], 71), 0),
        "d_skip": jnp.clip(0.5 + 1.0 * jax.random.uniform(key_list[8], (HEADS,), jnp.float32) ** shard_levels(key_list[8], (HEADS,), ((0, 16),), -0.2, 0.2), 0.5, 1.5),
        "norm_gain": jnp.clip(1.0 + 0.1 * jax.random.normal(key_list[9], (HEADS * P_SIZE,), jnp.float32), 0.5, 1.5),
        "prompt_lengths": ragged_sizes(key_list[10], PROMPTS, TOKENS, TOKENS // 2 + TOK_DEV // 2, 0).astype(jnp.int32),
        "cache_slot": draw_cache_slot(jax.random.fold_in(key_list[15], 71), 0),
        "prefix_state": bell_draw(key_list[12], (SLOTS, HEADS * P_SIZE, N), 1.0, 5.0, ((0, 32), (1, 16))),
        "tail_x": bell_draw(key_list[13], (SLOTS, KW - 1, HEADS * P_SIZE), 1.0, 5.0, ((0, 32), (2, 16))),
        "tail_bc": bell_draw(key_list[14], (SLOTS, KW - 1, 2 * GROUPS * N), 1.0, 5.0, ((0, 32),)),
    }


eps_norm = 1e-05

def dequant(mantissa, codes):
    row_count, chan_count = mantissa.shape
    block_count = codes.shape[1]
    scaled = mantissa.astype(jnp.float32).reshape(row_count, block_count, chan_count // block_count)
    scaled = scaled * jnp.exp2(codes.astype(jnp.float32))[:, :, None]
    return scaled.reshape(row_count, chan_count)

def prompt_rows(starts, offset, row_count):
    position = jnp.arange(row_count, dtype=jnp.int32) + offset
    inside = (position[:, None] >= starts[None, :]).astype(jnp.int32)
    return (lax.optimization_barrier(jnp.sum(inside, axis=1)) - 1).astype(jnp.int32)

def pick_rows(table, prompt_id):
    hit = prompt_id[:, None] == jnp.arange(table.shape[0], dtype=jnp.int32)[None, :]
    return lax.optimization_barrier(jnp.sum(jnp.where(hit, table[None, :], 0), axis=1)).astype(jnp.int32)

def causal_conv(current, previous, tails, weights, prompt_id, start_loc):
    row_count, chan_count = current.shape
    lag_count = previous.shape[0]
    prompt_count = tails.shape[0]
    extended = jnp.concatenate([previous, current], axis=0)
    flat_tails = tails.reshape(prompt_count * lag_count, chan_count)
    row_start = pick_rows(start_loc, prompt_id)
    position = jnp.arange(row_count, dtype=jnp.int32)
    total = jnp.zeros((row_count, chan_count), jnp.float32)
    for shift_by in range(lag_count + 1):
        source = extended[lag_count - shift_by:lag_count - shift_by + row_count]
        earlier = position - shift_by
        index = (prompt_id * lag_count + jnp.clip(earlier - row_start + lag_count, 0, lag_count - 1)).astype(jnp.int32)
        tail_rows = jnp.take(flat_tails, index, axis=0)
        value = jnp.where((earlier < row_start)[:, None], tail_rows, source)
        total = total + weights[lag_count - shift_by][None, :] * value
    return total

def span_local(x_act, b_act, c_act, delta, log_decay, prompt_id, start_loc, prefixes):
    row_count, head_count, width = x_act.shape
    group_count, state = (b_act.shape[1], b_act.shape[2])
    per_group = head_count // group_count
    cumul = jnp.cumsum(log_decay, axis=0)
    before_sum = cumul - log_decay
    position = jnp.arange(row_count, dtype=jnp.int32)
    live = (prompt_id[:, None] == prompt_id[None, :]) & (position[:, None] >= position[None, :])
    scores = jnp.einsum('tgn,sgn->gts', c_act.astype(jnp.float32), b_act.astype(jnp.float32))

    def one_head(head):
        score = lax.dynamic_index_in_dim(scores, head // per_group, 0, keepdims=False)
        level = lax.dynamic_index_in_dim(cumul, head, 1, keepdims=False)
        stride = lax.dynamic_index_in_dim(delta, head, 1, keepdims=False)
        values = lax.dynamic_index_in_dim(x_act, head, 1, keepdims=False)
        spread = jnp.where(live, level[:, None] - level[None, :], 0.0)
        weights = jnp.where(live, score * jnp.exp(spread) * stride[None, :], 0.0).astype(jnp.bfloat16)
        return jnp.dot(weights, values, preferred_element_type=jnp.float32)
    intra = lax.map(one_head, jnp.arange(head_count, dtype=jnp.int32))
    intra = jnp.transpose(intra, (1, 0, 2))
    last_prompt = prompt_id[row_count - 1]
    final = cumul[row_count - 1]
    keep = (prompt_id == last_prompt)[:, None]
    fade = jnp.where(keep, jnp.exp(jnp.where(keep, final[None, :] - cumul, 0.0)), 0.0)
    inputs = (x_act.astype(jnp.float32) * (delta * fade)[:, :, None]).astype(jnp.bfloat16)
    grouped = inputs.reshape(row_count, group_count, per_group, width)
    ends = jnp.einsum('sgkp,sgn->gkpn', grouped.astype(jnp.float32), b_act.astype(jnp.float32))
    ends = ends.reshape(head_count, width, state)
    last_start = lax.dynamic_index_in_dim(start_loc, last_prompt, 0, keepdims=False)
    inside = last_start >= 0
    base = lax.dynamic_index_in_dim(before_sum, jnp.clip(last_start, 0, row_count - 1), 0, keepdims=False)
    carry_in = jnp.exp(jnp.where(inside, final - base, 0.0))
    prefix_last = lax.dynamic_index_in_dim(prefixes, last_prompt, 0, keepdims=False)
    ends = ends + jnp.where(inside, carry_in[:, None, None] * prefix_last, 0.0)
    opens = jnp.any((start_loc >= 0) & (start_loc < row_count))
    through = jnp.where(opens, 0.0, jnp.exp(final))
    return (intra, ends, through, cumul, before_sum)

def span_init(c_act, incoming, prefixes, prompt_id, start_loc, cumul, before_sum):
    row_count, group_count, state = c_act.shape
    prompt_count, head_count, width = (prefixes.shape[0], prefixes.shape[1], prefixes.shape[2])
    per_group = head_count // group_count
    c_wide = c_act.astype(jnp.float32)
    total = jnp.zeros((row_count, head_count, width), jnp.float32)
    for prompt in range(prompt_count):
        begin = start_loc[prompt]
        start_state = jnp.where(begin >= 0, prefixes[prompt], incoming)
        grouped = start_state.reshape(group_count, per_group, width, state)
        reads = jnp.einsum('tgn,gkpn->tgkp', c_wide, grouped, precision=lax.Precision.HIGHEST)
        reads = reads.reshape(row_count, head_count, width)
        base = lax.dynamic_index_in_dim(before_sum, jnp.clip(begin, 0, row_count - 1), 0, keepdims=False)
        member = (prompt_id == prompt)[:, None]
        fade = jnp.where(member, jnp.exp(jnp.where(member, cumul - base[None, :], 0.0)), 0.0)
        total = total + fade[:, :, None] * reads
    return total

def reference(x_mant, x_codes, bc_raw, gate_z, conv_x, conv_bc, dt_raw, a_log, d_skip, norm_gain, prompt_lengths, cache_slot, prefix_state, tail_x, tail_bc):
    lag_count = KW - 1
    heads_group = HEADS // GROUPS
    group_cols = GROUPS * N
    starts = (jnp.cumsum(prompt_lengths) - prompt_lengths).astype(jnp.int32)
    prefixes = jnp.take(prefix_state, cache_slot, axis=0).astype(jnp.float32).reshape(PROMPTS, HEADS, P_SIZE, N)
    tails_x = jnp.take(tail_x, cache_slot, axis=0).astype(jnp.float32)
    tails_bc = jnp.take(tail_bc, cache_slot, axis=0).astype(jnp.float32)
    rates = jnp.exp(a_log)

    def one_block(incoming, block):
        offset = (block * TOK_DEV).astype(jnp.int32)
        start_loc = (starts - offset).astype(jnp.int32)
        prompt_id = prompt_rows(starts, offset, TOK_DEV)
        back = jnp.maximum(offset - lag_count, 0).astype(jnp.int32)
        x_wide = dequant(lax.dynamic_slice_in_dim(x_mant, offset, TOK_DEV, 0), lax.dynamic_slice_in_dim(x_codes, offset, TOK_DEV, 0))
        prev_x = dequant(lax.dynamic_slice_in_dim(x_mant, back, lag_count, 0), lax.dynamic_slice_in_dim(x_codes, back, lag_count, 0))
        prev_x = jnp.where(block > 0, prev_x, 0.0)
        bc_rows = lax.dynamic_slice_in_dim(bc_raw, offset, TOK_DEV, 0).astype(jnp.float32)
        prev_bc = lax.dynamic_slice_in_dim(bc_raw, back, lag_count, 0).astype(jnp.float32)
        prev_bc = jnp.where(block > 0, prev_bc, 0.0)
        conv_out = causal_conv(x_wide, prev_x, tails_x, conv_x, prompt_id, start_loc)
        x_act = jax.nn.silu(conv_out).astype(jnp.bfloat16).reshape(TOK_DEV, HEADS, P_SIZE)
        bc_out = causal_conv(bc_rows, prev_bc, tails_bc, conv_bc, prompt_id, start_loc)
        bc_act = jax.nn.silu(bc_out).astype(jnp.bfloat16)
        b_act = bc_act[:, :group_cols].reshape(TOK_DEV, GROUPS, N)
        c_act = bc_act[:, group_cols:].reshape(TOK_DEV, GROUPS, N)
        delta = jax.nn.softplus(lax.dynamic_slice_in_dim(dt_raw, offset, TOK_DEV, 0))
        log_decay = -rates[None, :] * delta
        intra, ends, through, cumul, before_sum = span_local(x_act, b_act, c_act, delta, log_decay, prompt_id, start_loc, prefixes)
        init = span_init(c_act, incoming, prefixes, prompt_id, start_loc, cumul, before_sum)
        y_full = intra + init + d_skip[None, :, None] * x_act.astype(jnp.float32)
        gate_rows = lax.dynamic_slice_in_dim(gate_z, offset, TOK_DEV, 0).astype(jnp.float32).reshape(TOK_DEV, HEADS, P_SIZE)
        gated = y_full * jax.nn.silu(gate_rows)
        head_squares = lax.optimization_barrier(jnp.sum(gated * gated, axis=2))
        group_squares = lax.optimization_barrier(jnp.sum(head_squares.reshape(TOK_DEV, GROUPS, heads_group), axis=2))
        inverse = lax.rsqrt(group_squares / (heads_group * P_SIZE) + eps_norm)
        inverse = jnp.repeat(inverse, heads_group, axis=1)
        mixed_block = gated * inverse[:, :, None] * norm_gain.reshape(HEADS, P_SIZE)[None, :, :]
        following = through[:, None, None] * incoming + ends
        return (following, mixed_block.reshape(TOK_DEV, HEADS * P_SIZE).astype(jnp.bfloat16))
    _, blocks = lax.scan(one_block, jnp.zeros((HEADS, P_SIZE, N), jnp.float32), jnp.arange(N_CTX, dtype=jnp.int32))
    return blocks.reshape(TOKENS, HEADS * P_SIZE)
```

```python
import jax
import jax.numpy as jnp
from jax import lax
from jax.experimental import pallas as pl
from jax.experimental.pallas import tpu as pltpu
from jax.sharding import PartitionSpec as P

BF = jnp.bfloat16
F32 = jnp.float32
HIGH = lax.Precision.HIGHEST
INTERPRET = False

TOK = 128
WIDTH = 64
STATE = 128
MXB = 32
LAGS = 3
PROMPTS = 4
HEADS_GROUP = 32
SLOTS_HERE = 2
EPS = 1e-05
FAR = -1e30

TAIL_AT = 64
PREV_AT = 124
DECAY_AT = 154
ROWS0 = 160


def call(kernel, out_shape, **kw):
    return pl.pallas_call(
        kernel,
        out_shape=out_shape,
        interpret=INTERPRET,
        compiler_params=pltpu.CompilerParams(vmem_limit_bytes=48 * 1024 * 1024),
        **kw,
    )


def vmem():
    return pl.BlockSpec(memory_space=pltpu.VMEM)


def smem():
    return pl.BlockSpec(memory_space=pltpu.SMEM)


def starts_of(len_ref):
    found = [jnp.int32(0)]
    for p in range(PROMPTS - 1):
        found.append(found[-1] + len_ref[p])
    return found


def iota(shape, axis):
    return lax.broadcasted_iota(jnp.int32, shape, axis)


def row_starts(locs, token):
    first = jnp.full(token.shape, locs[0], jnp.int32)
    for p in range(1, PROMPTS):
        first = jnp.where(token >= locs[p], locs[p], first)
    return first


def softplus(v):
    return jnp.maximum(v, 0.0) + jnp.log1p(jnp.exp(-jnp.abs(v)))


def silu(v):
    return v / (1.0 + jnp.exp(-v))


def spread(per, count):
    shape = (count, count * per)
    return (iota(shape, 1) // per == iota(shape, 0)).astype(F32)


def wide_scale(codes):
    scale = jnp.exp2(codes.astype(F32)).astype(BF)
    return jnp.dot(scale, spread(MXB, codes.shape[1]).astype(BF), preferred_element_type=F32)


def group_cols(ref_load, group, groups):
    b_at = pl.multiple_of(group * STATE, STATE)
    c_at = pl.multiple_of((groups + group) * STATE, STATE)
    return jnp.concatenate([ref_load(b_at), ref_load(c_at)], axis=-1).astype(F32)


def pack_kernel(len_ref, dt_ref, alog_ref, prefix_ref, tx_ref, tbc_ref, xm_ref, xc_ref, bc_ref, out_ref):
    ctx = lax.axis_index("ctx")
    group = lax.axis_index("head") * dt_ref.shape[1] // HEADS_GROUP
    groups = bc_ref.shape[1] // (2 * STATE)
    devices, heads = out_ref.shape[0], dt_ref.shape[1]
    per_dev = prefix_ref.shape[1] // devices
    locs = [s - ctx * TOK for s in starts_of(len_ref)]
    last_start = jnp.int32(0)
    for loc in locs:
        last_start = jnp.where((loc >= 0) & (loc < TOK), loc, last_start)
    log_decay = -jnp.exp(alog_ref[...]) * softplus(dt_ref[...])
    rows = iota((TOK, heads), 0)
    decay = jnp.exp(jnp.sum(jnp.where(rows >= last_start, log_decay, 0.0), axis=0, keepdims=True))
    high = decay.astype(BF).astype(F32)
    mid = (decay - high).astype(BF).astype(F32)
    low = decay - high - mid
    tails = jnp.concatenate(
        [
            jnp.concatenate(
                [
                    tx_ref[s].astype(F32),
                    group_cols(lambda at: tbc_ref[s, :, pl.ds(at, STATE)], group, groups),
                ],
                axis=1,
            )
            for s in range(SLOTS_HERE)
        ],
        axis=0,
    )
    skip = xm_ref.shape[0] - LAGS
    x_last = xm_ref[...].astype(F32)[skip:] * wide_scale(xc_ref[...])[xc_ref.shape[0] - LAGS :]
    bc_last = group_cols(lambda at: bc_ref[:, pl.ds(at, STATE)], group, groups)[skip:]
    prev = jnp.concatenate([x_last, bc_last], axis=1)
    lanes = prev.shape[1] // STATE
    pieces = [tails[:, c * STATE : (c + 1) * STATE] for c in range(lanes)]
    pieces += [prev[:, c * STATE : (c + 1) * STATE] for c in range(lanes)]
    pieces.append(jnp.zeros((ROWS0 - DECAY_AT, STATE), F32))
    misc = jnp.concatenate(pieces, axis=0)
    body = misc[: ROWS0 - TAIL_AT - 16].astype(BF)
    foot = misc[ROWS0 - TAIL_AT - 16 :]
    at = iota(foot.shape, 0) + (ROWS0 - 16 - DECAY_AT)
    for k in range(devices):
        h = k * per_dev // WIDTH
        for s in range(SLOTS_HERE):
            out_ref[k, s * per_dev : (s + 1) * per_dev, :] = prefix_ref[s, k * per_dev : (k + 1) * per_dev, :]
        out_ref[k, TAIL_AT : ROWS0 - 16, :] = body
        tile = jnp.where(at == 0, high[:, h : h + 1], foot)
        tile = jnp.where(at == 1, mid[:, h : h + 1], tile)
        tile = jnp.where(at == 2, low[:, h : h + 1], tile)
        out_ref[k, ROWS0 - 16 :, :] = tile.astype(BF)


def block_kernel(
    len_ref,
    slot_ref,
    got_ref,
    xm_ref,
    xc_ref,
    bc_ref,
    wx_ref,
    wbc_ref,
    dt_ref,
    alog_ref,
    skip_ref,
    ends_ref,
    y_ref,
    c_ref,
    cw_ref,
    x_scr,
):
    ctx = lax.axis_index("ctx")
    heads = dt_ref.shape[1]
    chans = heads * WIDTH
    group = lax.axis_index("head") * heads // HEADS_GROUP
    groups = bc_ref.shape[1] // (2 * STATE)
    devices = got_ref.shape[0]
    all_chans = chans + 2 * STATE
    lanes = all_chans // STATE
    locs = [s - ctx * TOK for s in starts_of(len_ref)]

    x_scr[8:, :chans] = xm_ref[...].astype(F32) * wide_scale(xc_ref[...])
    x_scr[8:, chans:] = group_cols(lambda at: bc_ref[:, pl.ds(at, STATE)], group, groups)
    before = got_ref[(ctx + devices - 1) % devices].astype(F32)
    for c in range(lanes):
        x_scr[8 - LAGS : 8, c * STATE : (c + 1) * STATE] = before[PREV_AT + c * LAGS : PREV_AT + (c + 1) * LAGS]

    tails = []
    for p in range(PROMPTS):
        slot = slot_ref[p]
        from_owner = got_ref[slot // SLOTS_HERE].astype(F32)[TAIL_AT:PREV_AT]
        second = (jnp.zeros((LAGS, STATE), jnp.int32) + slot % SLOTS_HERE) == 1
        tails.append(
            jnp.concatenate(
                [
                    jnp.where(
                        second,
                        from_owner[c * 2 * LAGS + LAGS : (c + 1) * 2 * LAGS],
                        from_owner[c * 2 * LAGS : c * 2 * LAGS + LAGS],
                    )
                    for c in range(lanes)
                ],
                axis=1,
            )
        )
    tails.append(jnp.zeros((16 - PROMPTS * LAGS, all_chans), F32))
    tails = jnp.concatenate(tails, axis=0).astype(BF)

    token = iota((TOK, 16), 0)
    first = row_starts(locs, token)
    prompt = sum((token >= loc).astype(jnp.int32) for loc in locs) - 1
    taps = jnp.concatenate(
        [wx_ref[...], group_cols(lambda at: wbc_ref[:, pl.ds(at, STATE)], group, groups)], axis=1
    )
    conv = taps[LAGS : LAGS + 1] * x_scr[8:, :]
    for k in range(1, LAGS + 1):
        outside = token - k < first
        pick = outside & (iota((TOK, 16), 1) == prompt * LAGS + token - k - first + LAGS)
        tail_rows = jnp.dot(pick.astype(BF), tails, preferred_element_type=F32)
        value = jnp.where(outside[:, :1], tail_rows, x_scr[8 - k : 8 + TOK - k, :])
        conv = conv + taps[LAGS - k : LAGS - k + 1] * value
    act = silu(conv).astype(BF)
    x_act = act[:, :chans]
    b_act = act[:, chans : chans + STATE]
    c_act = act[:, chans + STATE :]
    c_ref[...] = c_act

    row, col = iota((TOK, TOK), 0), iota((TOK, TOK), 1)
    live = (col <= row) & (col >= row_starts(locs, row))
    delta = softplus(dt_ref[...])
    log_decay = -jnp.exp(alog_ref[...]) * delta
    within = jnp.dot(live.astype(F32), log_decay, precision=HIGH, preferred_element_type=F32)
    cw_ref[...] = within
    within_t = within.T
    delta_t = delta.T
    scores = lax.dot_general(c_act, b_act, (((1,), (1,)), ((), ())), preferred_element_type=F32)
    skip = jnp.dot(skip_ref[...], spread(WIDTH, heads), precision=HIGH, preferred_element_type=F32)
    left = iota((TOK, 2 * WIDTH), 1) < WIDTH
    for j in range(heads // 2):
        pair = []
        for h in (2 * j, 2 * j + 1):
            fade = jnp.exp(jnp.where(live, within[:, h : h + 1] - within_t[h : h + 1, :], FAR))
            pair.append((scores * fade * delta_t[h : h + 1, :]).astype(BF))
        at = slice(2 * j * WIDTH, 2 * (j + 1) * WIDTH)
        x_pair = x_act[:, at].astype(F32)
        both = jnp.concatenate([jnp.where(left, x_pair, 0.0), jnp.where(left, 0.0, x_pair)], axis=0)
        intra = jnp.dot(jnp.concatenate(pair, axis=1), both.astype(BF), preferred_element_type=F32)
        y_ref[:, at] = intra + skip[:, at] * x_pair

    token_h = iota((TOK, heads), 0)
    keep = token_h >= row_starts(locs, jnp.full((TOK, heads), TOK - 1, jnp.int32))
    to_end = delta * jnp.exp(jnp.where(keep, within[TOK - 1 :, :] - within, FAR))
    to_end = jnp.dot(to_end, spread(WIDTH, heads), precision=HIGH, preferred_element_type=F32)
    inputs = (x_act.astype(F32) * to_end).astype(BF)
    ends = lax.dot_general(inputs, b_act, (((0,), (0,)), ((), ())), preferred_element_type=F32)
    ends_ref[...] = ends.astype(BF)


def scan_kernel(len_ref, slot_ref, got_ref, ends_ref, out_ref):
    devices, rows = ends_ref.shape[0], ends_ref.shape[1]
    starts = starts_of(len_ref)
    blocks = [s // TOK for s in starts]
    prefixes = []
    for p in range(PROMPTS):
        slot = slot_ref[p]
        at = pl.multiple_of((slot % SLOTS_HERE) * rows, rows)
        prefixes.append(got_ref[slot // SLOTS_HERE, pl.ds(at, rows), :])
    wide = [piece.astype(F32) for piece in prefixes]
    state = jnp.zeros((rows, STATE), F32)
    for d in range(devices):
        out_ref[d, :rows, :] = state.astype(BF)
        out_ref[d, rows:, :] = jnp.zeros((out_ref.shape[1] - rows, STATE), BF)
        foot = got_ref[d, ROWS0 - 16 :, :].astype(F32)
        at = DECAY_AT - ROWS0 + 16
        decay = foot[at : at + 1] + foot[at + 1 : at + 2] + foot[at + 2 : at + 3]
        base = state
        for p in range(PROMPTS):
            base = jnp.where(blocks[p] == d, wide[p], base)
        state = decay * base + ends_ref[d].astype(F32)
    for p in range(PROMPTS):
        place = jnp.int32(1)
        for q in range(p):
            place = place + (blocks[q] == blocks[p]).astype(jnp.int32)
        out_ref[blocks[p], pl.ds(pl.multiple_of(place * rows, rows), rows), :] = prefixes[p]


def read_kernel(len_ref, got_ref, c_ref, cw_ref, y_ref, gate_ref, gated_ref, sq_ref):
    ctx = lax.axis_index("ctx")
    devices = got_ref.shape[0]
    heads = cw_ref.shape[1]
    chans = heads * WIDTH
    rows = chans // devices
    locs = [s - ctx * TOK for s in starts_of(len_ref)]
    token = iota((TOK, STATE), 0)
    place = sum(((loc >= 0) & (token >= loc)).astype(jnp.int32) for loc in locs)
    c_act = c_ref[...].astype(F32)
    reads = jnp.zeros((TOK, chans), F32)
    for j in range(got_ref.shape[1] // rows):
        state = got_ref[:, j * rows : (j + 1) * rows, :].reshape(chans, STATE)
        mine = jnp.where(place == j, c_act, 0.0).astype(BF)
        reads = reads + lax.dot_general(mine, state, (((1,), (1,)), ((), ())), preferred_element_type=F32)
    fade = jnp.dot(jnp.exp(cw_ref[...]), spread(WIDTH, heads), precision=HIGH, preferred_element_type=F32)
    gated = (y_ref[...] + fade * reads) * silu(gate_ref[...].astype(F32))
    gated_ref[...] = gated
    square = gated * gated
    part = square[:, :STATE]
    for c in range(1, chans // STATE):
        part = part + square[:, c * STATE : (c + 1) * STATE]
    sq_ref[...] = jnp.sum(part.T, axis=0, keepdims=True)


def norm_kernel(gated_ref, sq_ref, other_ref, gain_ref, out_ref):
    total = sq_ref[...] + other_ref[...]
    inverse = lax.rsqrt(total / (HEADS_GROUP * WIDTH) + EPS)
    inverse = jnp.broadcast_to(inverse, (TOK, TOK)).T
    for c in range(out_ref.shape[1] // TOK):
        at = slice(c * TOK, (c + 1) * TOK)
        out_ref[:, at] = (gated_ref[:, at] * inverse * gain_ref[:, at]).astype(BF)


def on_device(
    x_mant,
    x_codes,
    bc_raw,
    gate_z,
    conv_x,
    conv_bc,
    dt_raw,
    a_log,
    d_skip,
    norm_gain,
    prompt_lengths,
    cache_slot,
    prefix_state,
    tail_x,
    tail_bc,
):
    devices = lax.axis_size("ctx")
    head_devices = lax.axis_size("head")
    heads = a_log.shape[0]
    chans = heads * WIDTH
    rows = chans // devices
    a_row = a_log.reshape(1, heads)
    skip_row = d_skip.reshape(1, heads)
    gain_row = norm_gain.reshape(1, chans)

    def whole(array):
        return pl.BlockSpec(array.shape, lambda i: (0,) * array.ndim)

    last = TOK // 16 - 1
    send0 = call(
        pack_kernel,
        jax.ShapeDtypeStruct((devices, ROWS0, STATE), BF),
        grid=(1,),
        in_specs=[
            smem(),
            whole(dt_raw),
            whole(a_row),
            whole(prefix_state),
            whole(tail_x),
            whole(tail_bc),
            pl.BlockSpec((16, chans), lambda i: (last, 0)),
            pl.BlockSpec((16, x_codes.shape[1]), lambda i: (last, 0)),
            pl.BlockSpec((16, bc_raw.shape[1]), lambda i: (last, 0)),
        ],
        out_specs=pl.BlockSpec((devices, ROWS0, STATE), lambda i: (0, 0, 0)),
    )(prompt_lengths, dt_raw, a_row, prefix_state, tail_x, tail_bc, x_mant, x_codes, bc_raw)
    got0 = lax.all_to_all(send0, "ctx", 0, 0)

    ends, y_part, c_act, within = call(
        block_kernel,
        (
            jax.ShapeDtypeStruct((chans, STATE), BF),
            jax.ShapeDtypeStruct((TOK, chans), F32),
            jax.ShapeDtypeStruct((TOK, STATE), BF),
            jax.ShapeDtypeStruct((TOK, heads), F32),
        ),
        in_specs=[smem(), smem()] + [vmem()] * 9,
        out_specs=(vmem(),) * 4,
        scratch_shapes=[pltpu.VMEM((TOK + 8, chans + 2 * STATE), F32)],
    )(prompt_lengths, cache_slot, got0, x_mant, x_codes, bc_raw, conv_x, conv_bc, dt_raw, a_row, skip_row)
    got1 = lax.all_to_all(ends.reshape(devices, rows, STATE), "ctx", 0, 0)

    send2 = call(
        scan_kernel,
        jax.ShapeDtypeStruct((devices, PROMPTS * rows, STATE), BF),
        in_specs=[smem(), smem(), vmem(), vmem()],
        out_specs=vmem(),
    )(prompt_lengths, cache_slot, got0, got1)
    got2 = lax.all_to_all(send2, "ctx", 0, 0)

    gated, squares = call(
        read_kernel,
        (jax.ShapeDtypeStruct((TOK, chans), F32), jax.ShapeDtypeStruct((1, TOK), F32)),
        in_specs=[smem()] + [vmem()] * 5,
        out_specs=(vmem(), vmem()),
    )(prompt_lengths, got2, c_act, within, y_part, gate_z)
    other = lax.ppermute(squares, "head", [(i, i ^ 1) for i in range(head_devices)])
    return call(
        norm_kernel,
        jax.ShapeDtypeStruct((TOK, chans), BF),
        in_specs=[vmem()] * 4,
        out_specs=vmem(),
    )(gated, squares, other, gain_row)


def solution(mesh):
    in_specs = (
        P("ctx", "head"),
        P("ctx", "head"),
        P("ctx", None),
        P("ctx", "head"),
        P(None, "head"),
        P(),
        P("ctx", "head"),
        P("head"),
        P("head"),
        P("head"),
        P(),
        P(),
        P("ctx", "head", None),
        P("ctx", None, "head"),
        P("ctx", None, None),
    )
    out_specs = P("ctx", "head")
    return jax.shard_map(
        on_device, mesh=mesh, in_specs=in_specs, out_specs=out_specs, check_vma=False
    )
```

```python
import jax
import jax.numpy as jnp
from jax import lax
from jax.experimental import pallas as pl
from jax.experimental.pallas import tpu as pltpu
from jax.sharding import PartitionSpec as P

BF = jnp.bfloat16
F32 = jnp.float32
HIGH = lax.Precision.HIGHEST
INTERPRET = False

TOK = 128
WIDTH = 64
STATE = 128
MXB = 32
LAGS = 3
PROMPTS = 4
HEADS_GROUP = 32
SLOTS_HERE = 2
EPS = 1e-05
FAR = -1e30

PREFIX_AT = 32
XB_AT = 96
BB_AT = 104
XP_AT = 112
XT_AT = 124
BP_AT = 130
BT_AT = 142
CT_AT = 148
CP_AT = 154
ROWS1 = 160
DECAY_LANE = LAGS + PROMPTS * LAGS
WINDOWS = 40


def call(kernel, out_shape, **kw):
    return pl.pallas_call(
        kernel,
        out_shape=out_shape,
        interpret=INTERPRET,
        compiler_params=pltpu.CompilerParams(vmem_limit_bytes=48 * 1024 * 1024),
        **kw,
    )


def vmem():
    return pl.BlockSpec(memory_space=pltpu.VMEM)


def hbm():
    return pl.BlockSpec(memory_space=pltpu.HBM)


def smem():
    return pl.BlockSpec(memory_space=pltpu.SMEM)


def starts_of(len_ref):
    found = [jnp.int32(0)]
    for p in range(PROMPTS - 1):
        found.append(found[-1] + len_ref[p])
    return found


def iota(shape, axis):
    return lax.broadcasted_iota(jnp.int32, shape, axis)


def row_starts(locs, token):
    first = jnp.full(token.shape, locs[0], jnp.int32)
    for p in range(1, PROMPTS):
        first = jnp.where(token >= locs[p], locs[p], first)
    return first


def softplus(v):
    return jnp.maximum(v, 0.0) + jnp.log1p(jnp.exp(-jnp.abs(v)))


def silu(v):
    return v / (1.0 + jnp.exp(-v))


def spread(per, count):
    shape = (count, count * per)
    return (iota(shape, 1) // per == iota(shape, 0)).astype(F32)


def group_cols(load, group, groups):
    b_at = pl.multiple_of(group * STATE, STATE)
    c_at = pl.multiple_of((groups + group) * STATE, STATE)
    return load(b_at).astype(F32), load(c_at).astype(F32)


def nt_dot(a, b, **kw):
    return lax.dot_general(a, b, (((1,), (1,)), ((), ())), preferred_element_type=F32, **kw)


def live_matrix(locs):
    row, col = iota((TOK, TOK), 0), iota((TOK, TOK), 1)
    return (col <= row) & (col >= row_starts(locs, row))


def widen(per_head_t, per):
    return jnp.dot(
        per_head_t.T, spread(per, per_head_t.shape[0]), precision=HIGH, preferred_element_type=F32
    )


def block_kernel(*refs):
    (len_hbm, dt_hbm, alog_hbm, xc_hbm, xm_hbm, bc_hbm, tx_hbm, tbc_hbm, wx_hbm, wbc_hbm, prefix_hbm) = refs[:11]
    out_ref, act_ref, within_ref = refs[11:14]
    (len_ref, dt_ref, alog_ref, xc_ref, xm_ref, bc_ref, tx_ref, tbc_ref, wx_ref, wbc_ref) = refs[14:24]
    x_scr, sems = refs[24:]
    rows = PREFIX_AT
    copies = [
        pltpu.make_async_copy(src, dst, sems.at[n])
        for n, (src, dst) in enumerate(
            [
                (len_hbm, len_ref),
                (dt_hbm, dt_ref),
                (alog_hbm, alog_ref),
                (xc_hbm, xc_ref),
                (xm_hbm, xm_ref),
                (bc_hbm, bc_ref),
                (tx_hbm, tx_ref),
                (tbc_hbm, tbc_ref),
                (wx_hbm, wx_ref),
                (wbc_hbm, wbc_ref),
            ]
            + [
                (prefix_hbm.at[s], out_ref.at[:, pl.ds(PREFIX_AT + s * rows, rows), :])
                for s in range(SLOTS_HERE)
            ]
        )
    ]
    for copy in copies:
        copy.start()
    for copy in copies[:10]:
        copy.wait()

    ctx = lax.axis_index("ctx")
    heads = dt_ref.shape[0]
    chans = heads * WIDTH
    group = lax.axis_index("head") * heads // HEADS_GROUP
    groups = bc_ref.shape[1] // (2 * STATE)
    devices = out_ref.shape[0]
    starts = starts_of(len_ref)
    locs = [s - ctx * TOK for s in starts]

    scale = jnp.exp2(xc_ref[...].astype(F32)).T.astype(BF)
    wide = jnp.dot(scale, spread(MXB, xc_ref.shape[0]).astype(BF), preferred_element_type=F32)
    x = xm_ref[...].astype(F32) * wide
    b_raw, c_raw = group_cols(lambda at: bc_ref[:, pl.ds(at, STATE)], group, groups)
    x_scr[8:, :chans] = x
    x_scr[8:, chans:] = b_raw
    x_scr[:8, :] = jnp.zeros((8, chans + STATE), F32)

    live = live_matrix(locs)
    delta = softplus(dt_ref[...])
    log_decay = -jnp.exp(alog_ref[...].T) * delta
    within = nt_dot(log_decay, live.astype(F32), precision=HIGH)
    within_ref[...] = within
    token = iota((heads, TOK), 1)
    first = row_starts(locs, token)
    last_start = row_starts(locs, jnp.full((heads, TOK), TOK - 1, jnp.int32))
    to_end = delta * jnp.exp(jnp.where(token >= last_start, within[:, TOK - 1 :] - within, FAR))
    regular = (token >= LAGS) & (token - first >= LAGS)
    factor = widen(jnp.where(regular, to_end, 0.0), WIDTH)

    w_b, _ = group_cols(lambda at: wbc_ref[:, pl.ds(at, STATE)], group, groups)
    taps = jnp.concatenate([wx_ref[...], w_b], axis=1)
    conv = taps[LAGS : LAGS + 1] * x_scr[8:, :]
    for k in range(1, LAGS + 1):
        conv = conv + taps[LAGS - k : LAGS - k + 1] * x_scr[8 - k : 8 + TOK - k, :]
    act = silu(conv).astype(BF)
    act_ref[...] = act[:, :chans]
    inputs = (act[:, :chans].astype(F32) * factor).astype(BF)
    ends = lax.dot_general(
        inputs, act[:, chans:], (((0,), (0,)), ((), ())), preferred_element_type=F32
    ).astype(BF)

    entry = iota((16, TOK), 0)
    begin = jnp.full((16, TOK), -TOK, jnp.int32)
    for p in range(PROMPTS):
        for i in range(LAGS):
            at = jnp.where(len_ref[p] > i, locs[p] + i, -TOK)
            begin = jnp.where(entry == p * LAGS + i, at, begin)
    chosen = iota((16, TOK), 1) == begin
    raw = jnp.concatenate([x, b_raw], axis=1).astype(BF)
    at_start = jnp.dot(chosen.astype(BF), raw, preferred_element_type=F32)[: PROMPTS * LAGS]
    lane = iota((heads, TOK), 1)
    at_block = jnp.where((token < LAGS) & (token - first >= LAGS), to_end, 0.0)
    vals = nt_dot(to_end, chosen.astype(F32), precision=HIGH)[:, : PROMPTS * LAGS]
    vals = jnp.concatenate(
        [at_block[:, :LAGS], vals, jnp.exp(within[:, TOK - 1 :]), jnp.zeros((heads, TOK - 16), F32)], axis=1
    )
    high = vals.astype(BF).astype(F32)
    low = vals - high

    tails = jnp.concatenate([tx_ref[i].astype(F32) for i in range(LAGS)], axis=0)
    tails = jnp.concatenate(
        [tails[i * SLOTS_HERE + s : i * SLOTS_HERE + s + 1] for s in range(SLOTS_HERE) for i in range(LAGS)], axis=0
    )
    tails_b, tails_c = [], []
    for s in range(SLOTS_HERE):
        for i in range(LAGS):
            b_one, c_one = group_cols(lambda at: tbc_ref[i, :, pl.ds(at, STATE)], group, groups)
            tails_b.append(b_one[s : s + 1])
            tails_c.append(c_one[s : s + 1])
    gap = jnp.zeros((2, STATE), F32)
    b_tile = jnp.concatenate([b_raw[:LAGS], gap, b_raw[TOK - LAGS :]], axis=0)
    foot = jnp.concatenate(
        [at_start[:, chans:]] + tails_b + tails_c + [c_raw[TOK - LAGS :], jnp.zeros((ROWS1 - CP_AT - LAGS, STATE), F32)],
        axis=0,
    )
    for k in range(devices):
        out_ref[k, :rows, :] = ends[k * rows : (k + 1) * rows]
        lanes = slice(k * rows // STATE * STATE, (k * rows // STATE + 1) * STATE)
        h = k * rows // WIDTH
        x_tile = [x[:LAGS, lanes], high[h : h + 1], low[h : h + 1], x[TOK - LAGS :, lanes]]
        part = jnp.concatenate(
            x_tile + [b_tile, at_start[:, lanes], tails[:, lanes], foot], axis=0
        )
        out_ref[k, XB_AT:, :] = part.astype(BF)
    for copy in copies[10:]:
        copy.wait()


def scan_kernel(len_ref, slot_ref, got_ref, wx_ref, wbc_ref, out_ref, x_scr, b_scr, in_scr, mix_scr):
    devices = got_ref.shape[0]
    rows = PREFIX_AT
    ctx = lax.axis_index("ctx")
    chans = wx_ref.shape[1]
    group = lax.axis_index("head") * (chans // WIDTH) // HEADS_GROUP
    groups = wbc_ref.shape[1] // (2 * STATE)
    at = ctx * rows % STATE
    starts = starts_of(len_ref)
    blocks = [s // TOK for s in starts]

    x_scr[...] = got_ref[:, XB_AT : XB_AT + 8, :].astype(F32).reshape(devices * 8, STATE)
    b_scr[...] = got_ref[:, BB_AT : BB_AT + 8, :].astype(F32).reshape(devices * 8, STATE)
    factors = x_scr[pl.ds(LAGS, devices, stride=8), :] + x_scr[pl.ds(LAGS + 1, devices, stride=8), :]
    prompt_factors = jnp.sum(factors, axis=0, keepdims=True)

    def windows(scr, start_at, tail_at):
        before, now = [], []
        for p in range(PROMPTS):
            slot = slot_ref[p]
            own = got_ref[blocks[p], XB_AT:, :].astype(F32)
            after = got_ref[jnp.minimum(blocks[p] + 1, devices - 1), XB_AT:, :].astype(F32)
            after = jnp.where(blocks[p] + 1 < devices, after, 0.0)
            place = start_at - XB_AT + p * LAGS
            now.append((own + after)[place : place + LAGS])
            owner = got_ref[slot // SLOTS_HERE, XB_AT:, :].astype(F32)
            place = tail_at - XB_AT
            before.append(
                jnp.where(
                    slot % SLOTS_HERE == 1, owner[place + LAGS : place + 2 * LAGS], owner[place : place + LAGS]
                )
            )
        pad = jnp.zeros((WINDOWS - devices - PROMPTS, STATE), F32)
        found = []
        for i in range(LAGS):
            last = scr[pl.ds(8 - LAGS + i, devices, stride=8), :]
            last = jnp.concatenate([last[devices - 1 :], last[: devices - 1]], axis=0)
            found.append(jnp.concatenate([last] + [b[i : i + 1] for b in before] + [pad], axis=0))
        for i in range(LAGS):
            fresh = scr[pl.ds(i, devices, stride=8), :]
            found.append(jnp.concatenate([fresh] + [n[i : i + 1] for n in now] + [pad], axis=0))
        return found

    def activation(rows6, taps, i):
        conv = taps[LAGS : LAGS + 1] * rows6[LAGS + i]
        for k in range(1, LAGS + 1):
            conv = conv + taps[LAGS - k : LAGS - k + 1] * rows6[LAGS + i - k]
        return silu(conv).astype(BF).astype(F32)

    x_taps = wx_ref[:, pl.ds(pl.multiple_of(ctx * rows // STATE * STATE, STATE), STATE)]
    b_taps, _ = group_cols(lambda at: wbc_ref[:, pl.ds(at, STATE)], group, groups)
    x_rows = windows(x_scr, XP_AT, XT_AT)
    b_rows = windows(b_scr, BP_AT, BT_AT)
    x_act = [activation(x_rows, x_taps, i) for i in range(LAGS)]
    b_act = [activation(b_rows, b_taps, i) for i in range(LAGS)]
    scaled = []
    for i in range(LAGS):
        column = [factors[:, i : i + 1]]
        for p in range(PROMPTS):
            lane = LAGS + p * LAGS + i
            column.append(prompt_factors[:, lane : lane + 1])
        column.append(jnp.zeros((WINDOWS - devices - PROMPTS, 1), F32))
        scaled.append(x_act[i] * jnp.concatenate(column, axis=0))
    spare = jnp.zeros((STATE - LAGS * WINDOWS, STATE), F32)
    in_scr[...] = jnp.concatenate(scaled + [spare], axis=0).T
    mine = in_scr[pl.ds(pl.multiple_of(at, rows), rows), :]
    lane = iota((rows, STATE), 1)
    target = lane % WINDOWS
    for p in range(PROMPTS):
        for i in range(LAGS):
            target = jnp.where(lane == i * WINDOWS + devices + p, (starts[p] + i) // TOK, target)
    for d in range(devices):
        mix_scr[d * rows : (d + 1) * rows, :] = jnp.where(target == d, mine, 0.0).astype(BF)
    b_all = jnp.concatenate(b_act + [spare], axis=0).astype(BF)
    extra = jnp.dot(mix_scr[...], b_all, preferred_element_type=F32)

    turn = at // rows
    from_prompts = jnp.where(
        turn == 0, x_act[0][devices:], jnp.where(turn == 1, x_act[1][devices:], x_act[2][devices:])
    )
    pad = jnp.zeros((8 - LAGS, STATE), F32)

    prefixes = []
    for p in range(PROMPTS):
        slot = slot_ref[p]
        place = pl.multiple_of(PREFIX_AT + (slot % SLOTS_HERE) * rows, rows)
        prefixes.append(got_ref[slot // SLOTS_HERE, pl.ds(place, rows), :])
    wide = [piece.astype(F32) for piece in prefixes]
    state = jnp.zeros((rows, STATE), F32)
    states = PROMPTS * rows
    for d in range(devices):
        out_ref[d, :rows, :] = state.astype(BF)
        out_ref[d, rows:states, :] = jnp.zeros((states - rows, STATE), BF)
        from_block = jnp.concatenate([x_act[i][d : d + 1] for i in range(LAGS)] + [pad], axis=0)
        out_ref[d, states:, :] = jnp.where(turn == LAGS, from_block, from_prompts).astype(BF)
        base = state
        for p in range(PROMPTS):
            base = jnp.where(blocks[p] == d, wide[p], base)
        decay = factors[d : d + 1, DECAY_LANE : DECAY_LANE + 1]
        state = decay * base + (got_ref[d, :rows, :].astype(F32) + extra[d * rows : (d + 1) * rows])
    for p in range(PROMPTS):
        place = jnp.int32(1)
        for q in range(p):
            place = place + (blocks[q] == blocks[p]).astype(jnp.int32)
        out_ref[blocks[p], pl.ds(pl.multiple_of(place * rows, rows), rows), :] = prefixes[p]


def read_kernel(
    len_ref,
    slot_ref,
    sent_ref,
    got_ref,
    act_ref,
    bc_ref,
    wbc_ref,
    within_ref,
    dt_ref,
    skip_ref,
    gate_ref,
    gated_ref,
    sq_ref,
    bc_scr,
):
    ctx = lax.axis_index("ctx")
    devices = got_ref.shape[0]
    heads = dt_ref.shape[0]
    chans = heads * WIDTH
    rows = chans // devices
    group = lax.axis_index("head") * heads // HEADS_GROUP
    groups = bc_ref.shape[1] // (2 * STATE)
    locs = [s - ctx * TOK for s in starts_of(len_ref)]

    token = iota((TOK, 16), 0)
    entry = iota((TOK, 16), 1)
    first = row_starts(locs, token)
    prompt = sum((token >= loc).astype(jnp.int32) for loc in locs) - 1

    bc_scr[8:, :] = jnp.concatenate(group_cols(lambda at: bc_ref[:, pl.ds(at, STATE)], group, groups), axis=1)
    before = sent_ref[(ctx + devices - 1) % devices, XB_AT:, :].astype(F32)
    bc_scr[8 - LAGS : 8, :STATE] = before[BB_AT - XB_AT + 8 - LAGS : BB_AT - XB_AT + 8]
    bc_scr[8 - LAGS : 8, STATE:] = before[CP_AT - XB_AT : CP_AT - XB_AT + LAGS]
    tails = []
    for p in range(PROMPTS):
        owner = sent_ref[slot_ref[p] // SLOTS_HERE, XB_AT:, :].astype(F32)
        pair = []
        for place in (BT_AT - XB_AT, CT_AT - XB_AT):
            pair.append(
                jnp.where(
                    slot_ref[p] % SLOTS_HERE == 1,
                    owner[place + LAGS : place + 2 * LAGS],
                    owner[place : place + LAGS],
                )
            )
        tails.append(jnp.concatenate(pair, axis=1))
    tails.append(jnp.zeros((16 - PROMPTS * LAGS, 2 * STATE), F32))
    tails = jnp.concatenate(tails, axis=0).astype(BF)
    taps = jnp.concatenate(group_cols(lambda at: wbc_ref[:, pl.ds(at, STATE)], group, groups), axis=1)
    conv = taps[LAGS : LAGS + 1] * bc_scr[8:, :]
    for k in range(1, LAGS + 1):
        outside = token - k < first
        pick = outside & (entry == prompt * LAGS + token - k - first + LAGS)
        tail_rows = jnp.dot(pick.astype(BF), tails, preferred_element_type=F32)
        value = jnp.where(outside[:, :1], tail_rows, bc_scr[8 - k : 8 + TOK - k, :])
        conv = conv + taps[LAGS - k : LAGS - k + 1] * value
    bc_act = silu(conv).astype(BF)
    b_act, c_act = bc_act[:, :STATE], bc_act[:, STATE:]

    near = token - first < LAGS
    by_prompt = (prompt == entry % PROMPTS) & (token - first == entry // PROMPTS) & near
    by_block = (token == entry - LAGS * PROMPTS) & (token < LAGS) & jnp.logical_not(near)
    pick = by_prompt | by_block
    other = (near | (token < LAGS))[:, :1]
    per = STATE // rows
    states = PROMPTS * rows
    spec = []
    for c in range(chans // STATE):
        spec.append(
            jnp.concatenate(
                [got_ref[c * per + j, states:, :].astype(F32)[:PROMPTS] for j in range(per)], axis=0
            )
        )
    spec = jnp.concatenate(spec, axis=1).astype(BF)
    patch = jnp.dot(pick.astype(BF), spec, preferred_element_type=F32)
    x_wide = jnp.where(other, patch, act_ref[...].astype(F32))

    live = live_matrix(locs)
    delta = softplus(dt_ref[...])
    within = within_ref[...]
    within_c = within.T
    scores = nt_dot(c_act, b_act)
    place = iota((TOK, STATE), 0)
    place = sum(((loc >= 0) & (place >= loc)).astype(jnp.int32) for loc in locs)
    c_wide = c_act.astype(F32)
    reads = jnp.zeros((TOK, chans), F32)
    for j in range(PROMPTS):
        state = got_ref[:, j * rows : (j + 1) * rows, :].reshape(chans, STATE)
        reads = reads + nt_dot(jnp.where(place == j, c_wide, 0.0).astype(BF), state)
    y = widen(jnp.exp(within), WIDTH) * reads
    skip = jnp.dot(skip_ref[...], spread(WIDTH, heads), precision=HIGH, preferred_element_type=F32)
    left = iota((TOK, 2 * WIDTH), 1) < WIDTH
    part = jnp.zeros((TOK, TOK), F32)
    for j in range(heads // 2):
        pair = []
        for h in (2 * j, 2 * j + 1):
            fade = jnp.exp(jnp.where(live, within_c[:, h : h + 1] - within[h : h + 1, :], FAR))
            pair.append((scores * fade * delta[h : h + 1, :]).astype(BF))
        at = slice(2 * j * WIDTH, 2 * (j + 1) * WIDTH)
        x_pair = x_wide[:, at]
        both = jnp.concatenate([jnp.where(left, x_pair, 0.0), jnp.where(left, 0.0, x_pair)], axis=0)
        intra = jnp.dot(jnp.concatenate(pair, axis=1), both.astype(BF), preferred_element_type=F32)
        total = y[:, at] + (intra + skip[:, at] * x_pair)
        gated = total * silu(gate_ref[:, at].astype(F32))
        gated_ref[:, at] = gated
        part = part + gated * gated
    sq_ref[...] = jnp.sum(part.T, axis=0, keepdims=True)


def norm_kernel(gated_ref, sq_ref, other_ref, gain_ref, out_ref):
    total = sq_ref[...] + other_ref[...]
    inverse = lax.rsqrt(total / (HEADS_GROUP * WIDTH) + EPS)
    inverse = jnp.broadcast_to(inverse, (TOK, TOK)).T
    for c in range(out_ref.shape[1] // TOK):
        at = slice(c * TOK, (c + 1) * TOK)
        out_ref[:, at] = (gated_ref[:, at] * inverse * gain_ref[:, at]).astype(BF)


def on_device(
    x_mant,
    x_codes,
    bc_raw,
    gate_z,
    conv_x,
    conv_bc,
    dt_raw,
    a_log,
    d_skip,
    norm_gain,
    prompt_lengths,
    cache_slot,
    prefix_state,
    tail_x,
    tail_bc,
):
    devices = lax.axis_size("ctx")
    head_devices = lax.axis_size("head")
    heads = a_log.shape[0]
    chans = heads * WIDTH
    rows = chans // devices
    dt_t = dt_raw.T
    sources = [
        prompt_lengths,
        dt_t,
        a_log.reshape(1, heads),
        x_codes.T,
        x_mant,
        bc_raw,
        jnp.transpose(tail_x, (1, 0, 2)),
        jnp.transpose(tail_bc, (1, 0, 2)),
        conv_x,
        conv_bc,
    ]
    prefixes = prefix_state.reshape(SLOTS_HERE, devices, rows, STATE)
    send1, act, within = call(
        block_kernel,
        (
            jax.ShapeDtypeStruct((devices, ROWS1, STATE), BF),
            jax.ShapeDtypeStruct((TOK, chans), BF),
            jax.ShapeDtypeStruct((heads, TOK), F32),
        ),
        in_specs=[hbm()] * 11,
        out_specs=(vmem(),) * 3,
        scratch_shapes=[pltpu.SMEM((PROMPTS,), jnp.int32)]
        + [pltpu.VMEM(source.shape, source.dtype) for source in sources[1:]]
        + [pltpu.VMEM((TOK + 8, chans + STATE), F32), pltpu.SemaphoreType.DMA((12,))],
    )(*sources, prefixes)
    got1 = lax.all_to_all(send1, "ctx", 0, 0)

    send2 = call(
        scan_kernel,
        jax.ShapeDtypeStruct((devices, PROMPTS * rows + 8, STATE), BF),
        in_specs=[smem(), smem()] + [vmem()] * 3,
        out_specs=vmem(),
        scratch_shapes=[
            pltpu.VMEM((devices * 8, STATE), F32),
            pltpu.VMEM((devices * 8, STATE), F32),
            pltpu.VMEM((STATE, STATE), F32),
            pltpu.VMEM((chans, STATE), BF),
        ],
    )(prompt_lengths, cache_slot, got1, conv_x, conv_bc)
    got2 = lax.all_to_all(send2, "ctx", 0, 0)

    gated, squares = call(
        read_kernel,
        (jax.ShapeDtypeStruct((TOK, chans), F32), jax.ShapeDtypeStruct((1, TOK), F32)),
        in_specs=[smem(), smem()] + [vmem()] * 9,
        out_specs=(vmem(), vmem()),
        scratch_shapes=[pltpu.VMEM((TOK + 8, 2 * STATE), F32)],
    )(
        prompt_lengths,
        cache_slot,
        got1,
        got2,
        act,
        bc_raw,
        conv_bc,
        within,
        dt_t,
        d_skip.reshape(1, heads),
        gate_z,
    )
    other = lax.ppermute(squares, "head", [(i, i ^ 1) for i in range(head_devices)])
    return call(
        norm_kernel,
        jax.ShapeDtypeStruct((TOK, chans), BF),
        in_specs=[vmem()] * 4,
        out_specs=vmem(),
    )(gated, squares, other, norm_gain.reshape(1, chans))


def solution(mesh):
    in_specs = (
        P("ctx", "head"),
        P("ctx", "head"),
        P("ctx", None),
        P("ctx", "head"),
        P(None, "head"),
        P(),
        P("ctx", "head"),
        P("head"),
        P("head"),
        P("head"),
        P(),
        P(),
        P("ctx", "head", None),
        P("ctx", None, "head"),
        P("ctx", None, None),
    )
    out_specs = P("ctx", "head")
    return jax.shard_map(
        on_device, mesh=mesh, in_specs=in_specs, out_specs=out_specs, check_vma=False
    )
```

```python
import functools

import jax
import jax.numpy as jnp
from jax import lax
from jax.experimental import pallas as pl
from jax.experimental.pallas import tpu as pltpu
from jax.sharding import PartitionSpec as P

BF = jnp.bfloat16
F32 = jnp.float32
HIGH = lax.Precision.HIGHEST
INTERPRET = False

TOK = 128
WIDTH = 64
STATE = 128
MXB = 32
LAGS = 3
PROMPTS = 4
HEADS_GROUP = 32
SLOTS_HERE = 2
EPS = 1e-05
FAR = -1e30


class Plan:
    def __init__(self, slots, prompts):
        self.slots, self.prompts = slots, prompts
        at = 32
        self.prefix, at = at, at + 32 * slots
        self.xb, at = at, at + 8
        self.bb, at = at, at + 8
        self.xp, at = at, at + LAGS * prompts
        self.xt, at = at, at + LAGS * slots
        self.bp, at = at, at + LAGS * prompts
        self.bt, at = at, at + LAGS * slots
        self.ct, at = at, at + LAGS * slots
        self.cp, at = at, at + LAGS
        self.used = at
        self.rows = (at + 7) // 8 * 8


SMALL = Plan(1, 2)
FULL = Plan(SLOTS_HERE, PROMPTS)
DECAY_LANE = LAGS + PROMPTS * LAGS
WINDOWS = 40


def call(kernel, out_shape, **kw):
    return pl.pallas_call(
        kernel,
        out_shape=out_shape,
        interpret=INTERPRET,
        compiler_params=pltpu.CompilerParams(vmem_limit_bytes=48 * 1024 * 1024),
        **kw,
    )


def vmem():
    return pl.BlockSpec(memory_space=pltpu.VMEM)


def hbm():
    return pl.BlockSpec(memory_space=pltpu.HBM)


def pinned(array):
    return array if INTERPRET else pltpu.with_memory_space_constraint(array, pltpu.HBM)


def smem():
    return pl.BlockSpec(memory_space=pltpu.SMEM)


def starts_of(len_ref):
    found = [jnp.int32(0)]
    for p in range(PROMPTS - 1):
        found.append(found[-1] + len_ref[p])
    return found


def iota(shape, axis):
    return lax.broadcasted_iota(jnp.int32, shape, axis)


def row_starts(locs, token):
    first = jnp.full(token.shape, locs[0], jnp.int32)
    for p in range(1, PROMPTS):
        first = jnp.where(token >= locs[p], locs[p], first)
    return first


def softplus(v):
    return jnp.maximum(v, 0.0) + jnp.log1p(jnp.exp(-jnp.abs(v)))


def silu(v):
    return v / (1.0 + jnp.exp(-v))


def spread(per, count):
    shape = (count, count * per)
    return (iota(shape, 1) // per == iota(shape, 0)).astype(F32)


def group_cols(load, group, groups):
    b_at = pl.multiple_of(group * STATE, STATE)
    c_at = pl.multiple_of((groups + group) * STATE, STATE)
    return load(b_at).astype(F32), load(c_at).astype(F32)


def nt_dot(a, b, **kw):
    return lax.dot_general(a, b, (((1,), (1,)), ((), ())), preferred_element_type=F32, **kw)


def live_matrix(locs):
    row, col = iota((TOK, TOK), 0), iota((TOK, TOK), 1)
    return (col <= row) & (col >= row_starts(locs, row))


def widen(per_head_t, per):
    return jnp.dot(
        per_head_t.T, spread(per, per_head_t.shape[0]), precision=HIGH, preferred_element_type=F32
    )


def small_enough(starts, slot_ref):
    fits = jnp.int32(1)
    for p in range(PROMPTS - 2):
        crowded = (starts[p + 1] - 1) // TOK == starts[p + 2] // TOK
        fits = jnp.where(crowded, 0, fits)
    for p in range(PROMPTS):
        for q in range(p):
            one, two = slot_ref[p], slot_ref[q]
            shared = (one // SLOTS_HERE == two // SLOTS_HERE) & (one != two)
            fits = jnp.where(shared, 0, fits)
    return fits


def block_kernel(plan, *refs):
    (
        len_hbm,
        slot_hbm,
        dt_hbm,
        alog_hbm,
        xc_hbm,
        xm_hbm,
        bc_hbm,
        tx_hbm,
        tbc_hbm,
        wx_hbm,
        wbc_hbm,
        prefix_hbm,
    ) = refs[:12]
    out_ref, act_ref, within_ref, fits_ref = refs[12:16]
    (len_ref, slot_ref, dt_ref, alog_ref, xc_ref, xm_ref, bc_ref, tx_ref, tbc_ref, wx_ref, wbc_ref) = refs[16:27]
    x_scr, sems = refs[27:]
    rows = plan.prefix
    small = plan.slots == 1
    ctx = lax.axis_index("ctx")
    copies = [
        pltpu.make_async_copy(src, dst, sems.at[n])
        for n, (src, dst) in enumerate(
            [
                (len_hbm, len_ref),
                (slot_hbm, slot_ref),
                (dt_hbm, dt_ref),
                (alog_hbm, alog_ref),
                (xc_hbm, xc_ref),
                (xm_hbm, xm_ref),
                (bc_hbm, bc_ref),
                (wx_hbm, wx_ref),
                (wbc_hbm, wbc_ref),
                (tx_hbm, tx_ref),
                (tbc_hbm, tbc_ref),
            ]
        )
    ]
    for copy in copies:
        copy.start()
    copies[0].wait()
    copies[1].wait()
    used = jnp.int32(0)
    for p in range(PROMPTS):
        used = jnp.where(slot_ref[p] // SLOTS_HERE == ctx, slot_ref[p] % SLOTS_HERE, used)
    states = [
        pltpu.make_async_copy(
            prefix_hbm.at[used if small else s],
            out_ref.at[:, pl.ds(plan.prefix + s * rows, rows), :],
            sems.at[len(copies) + s],
        )
        for s in range(plan.slots)
    ]
    for copy in states:
        copy.start()
    for copy in copies[2:]:
        copy.wait()

    heads = dt_ref.shape[0]
    chans = heads * WIDTH
    group = lax.axis_index("head") * heads // HEADS_GROUP
    groups = bc_ref.shape[1] // (2 * STATE)
    devices = out_ref.shape[0]
    starts = starts_of(len_ref)
    fits_ref[0] = small_enough(starts, slot_ref)
    locs = [s - ctx * TOK for s in starts]

    scale = jnp.exp2(xc_ref[...].astype(F32)).T.astype(BF)
    wide = jnp.dot(scale, spread(MXB, xc_ref.shape[0]).astype(BF), preferred_element_type=F32)
    x = xm_ref[...].astype(F32) * wide
    b_raw, c_raw = group_cols(lambda at: bc_ref[:, pl.ds(at, STATE)], group, groups)
    x_scr[8:, :chans] = x
    x_scr[8:, chans:] = b_raw
    x_scr[:8, :] = jnp.zeros((8, chans + STATE), F32)

    live = live_matrix(locs)
    delta = softplus(dt_ref[...])
    log_decay = -jnp.exp(alog_ref[...].T) * delta
    within = nt_dot(log_decay, live.astype(F32), precision=HIGH)
    within_ref[...] = within
    token = iota((heads, TOK), 1)
    first = row_starts(locs, token)
    last_start = row_starts(locs, jnp.full((heads, TOK), TOK - 1, jnp.int32))
    to_end = delta * jnp.exp(jnp.where(token >= last_start, within[:, TOK - 1 :] - within, FAR))
    regular = (token >= LAGS) & (token - first >= LAGS)
    factor = widen(jnp.where(regular, to_end, 0.0), WIDTH)

    w_b, _ = group_cols(lambda at: wbc_ref[:, pl.ds(at, STATE)], group, groups)
    taps = jnp.concatenate([wx_ref[...], w_b], axis=1)
    conv = taps[LAGS : LAGS + 1] * x_scr[8:, :]
    for k in range(1, LAGS + 1):
        conv = conv + taps[LAGS - k : LAGS - k + 1] * x_scr[8 - k : 8 + TOK - k, :]
    act = silu(conv).astype(BF)
    act_ref[...] = act[:, :chans]
    inputs = (act[:, :chans].astype(F32) * factor).astype(BF)
    ends = lax.dot_general(
        inputs, act[:, chans:], (((0,), (0,)), ((), ())), preferred_element_type=F32
    ).astype(BF)

    def chosen_rows(modulus):
        entry = iota((16, TOK), 0)
        begin = jnp.full((16, TOK), -TOK, jnp.int32)
        for p in range(PROMPTS):
            for i in range(LAGS):
                at = locs[p] + i
                inside = (len_ref[p] > i) & (at >= 0) & (at < TOK)
                begin = jnp.where((entry == p % modulus * LAGS + i) & inside, at, begin)
        return iota((16, TOK), 1) == begin

    raw = jnp.concatenate([x, b_raw], axis=1).astype(BF)
    at_start = jnp.dot(chosen_rows(plan.prompts).astype(BF), raw, preferred_element_type=F32)
    at_start = at_start[: plan.prompts * LAGS]
    at_block = jnp.where((token < LAGS) & (token - first >= LAGS), to_end, 0.0)
    vals = nt_dot(to_end, chosen_rows(PROMPTS).astype(F32), precision=HIGH)[:, : PROMPTS * LAGS]
    vals = jnp.concatenate(
        [at_block[:, :LAGS], vals, jnp.exp(within[:, TOK - 1 :]), jnp.zeros((heads, TOK - 16), F32)], axis=1
    )
    high = vals.astype(BF).astype(F32)
    low = vals - high

    tails_x, tails_b, tails_c = [], [], []
    for s in range(plan.slots):
        for i in range(LAGS):
            b_two, c_two = group_cols(lambda at: tbc_ref[i, :, pl.ds(at, STATE)], group, groups)
            for found, two in ((tails_x, tx_ref[i].astype(F32)), (tails_b, b_two), (tails_c, c_two)):
                found.append(jnp.where(used == 1, two[1:], two[:1]) if small else two[s : s + 1])
    tails = jnp.concatenate(tails_x, axis=0)
    gap = jnp.zeros((2, STATE), F32)
    b_tile = jnp.concatenate([b_raw[:LAGS], gap, b_raw[TOK - LAGS :]], axis=0)
    foot = jnp.concatenate(
        [at_start[:, chans:]] + tails_b + tails_c + [c_raw[TOK - LAGS :]],
        axis=0,
    )
    if plan.rows > plan.used:
        foot = jnp.concatenate([foot, jnp.zeros((plan.rows - plan.used, STATE), F32)], axis=0)
    for k in range(devices):
        out_ref[k, :rows, :] = ends[k * rows : (k + 1) * rows]
        lanes = slice(k * rows // STATE * STATE, (k * rows // STATE + 1) * STATE)
        h = k * rows // WIDTH
        x_tile = [x[:LAGS, lanes], high[h : h + 1], low[h : h + 1], x[TOK - LAGS :, lanes]]
        part = jnp.concatenate(
            x_tile + [b_tile, at_start[:, lanes], tails[:, lanes], foot], axis=0
        )
        out_ref[k, plan.xb :, :] = part.astype(BF)
    for copy in states:
        copy.wait()


def tail_of(plan, got_ref, slot, tail_at):
    owner = got_ref[slot // SLOTS_HERE, plan.xb :, :].astype(F32)
    place = tail_at - plan.xb
    tail = owner[place : place + LAGS]
    if plan.slots > 1:
        tail = jnp.where(slot % SLOTS_HERE == 1, owner[place + LAGS : place + 2 * LAGS], tail)
    return tail


def scan_kernel(plan, len_ref, slot_ref, got_ref, wx_ref, wbc_ref, out_ref, x_scr, b_scr, in_scr, mix_scr):
    devices = got_ref.shape[0]
    rows = plan.prefix
    ctx = lax.axis_index("ctx")
    chans = wx_ref.shape[1]
    group = lax.axis_index("head") * (chans // WIDTH) // HEADS_GROUP
    groups = wbc_ref.shape[1] // (2 * STATE)
    at = ctx * rows % STATE
    starts = starts_of(len_ref)
    blocks = [s // TOK for s in starts]

    x_scr[...] = got_ref[:, plan.xb : plan.xb + 8, :].astype(F32).reshape(devices * 8, STATE)
    b_scr[...] = got_ref[:, plan.bb : plan.bb + 8, :].astype(F32).reshape(devices * 8, STATE)
    factors = x_scr[pl.ds(LAGS, devices, stride=8), :] + x_scr[pl.ds(LAGS + 1, devices, stride=8), :]
    prompt_factors = jnp.sum(factors, axis=0, keepdims=True)

    def windows(scr, start_at, tail_at):
        before, now = [], []
        for p in range(PROMPTS):
            own = got_ref[blocks[p], plan.xb :, :].astype(F32)
            after = got_ref[jnp.minimum(blocks[p] + 1, devices - 1), plan.xb :, :].astype(F32)
            place = start_at - plan.xb + p % plan.prompts * LAGS
            now.append(
                [
                    jnp.where(
                        (starts[p] + i) // TOK == blocks[p],
                        own[place + i : place + i + 1],
                        after[place + i : place + i + 1],
                    )
                    for i in range(LAGS)
                ]
            )
            before.append(tail_of(plan, got_ref, slot_ref[p], tail_at))
        pad = jnp.zeros((WINDOWS - devices - PROMPTS, STATE), F32)
        found = []
        for i in range(LAGS):
            last = scr[pl.ds(8 - LAGS + i, devices, stride=8), :]
            last = jnp.concatenate([last[devices - 1 :], last[: devices - 1]], axis=0)
            found.append(jnp.concatenate([last] + [b[i : i + 1] for b in before] + [pad], axis=0))
        for i in range(LAGS):
            fresh = scr[pl.ds(i, devices, stride=8), :]
            found.append(jnp.concatenate([fresh] + [n[i] for n in now] + [pad], axis=0))
        return found

    def activation(rows6, taps, i):
        conv = taps[LAGS : LAGS + 1] * rows6[LAGS + i]
        for k in range(1, LAGS + 1):
            conv = conv + taps[LAGS - k : LAGS - k + 1] * rows6[LAGS + i - k]
        return silu(conv).astype(BF).astype(F32)

    x_taps = wx_ref[:, pl.ds(pl.multiple_of(ctx * rows // STATE * STATE, STATE), STATE)]
    b_taps, _ = group_cols(lambda at: wbc_ref[:, pl.ds(at, STATE)], group, groups)
    x_rows = windows(x_scr, plan.xp, plan.xt)
    b_rows = windows(b_scr, plan.bp, plan.bt)
    x_act = [activation(x_rows, x_taps, i) for i in range(LAGS)]
    b_act = [activation(b_rows, b_taps, i) for i in range(LAGS)]
    scaled = []
    for i in range(LAGS):
        column = [factors[:, i : i + 1]]
        for p in range(PROMPTS):
            lane = LAGS + p * LAGS + i
            column.append(prompt_factors[:, lane : lane + 1])
        column.append(jnp.zeros((WINDOWS - devices - PROMPTS, 1), F32))
        scaled.append(x_act[i] * jnp.concatenate(column, axis=0))
    spare = jnp.zeros((STATE - LAGS * WINDOWS, STATE), F32)
    in_scr[...] = jnp.concatenate(scaled + [spare], axis=0).T
    mine = in_scr[pl.ds(pl.multiple_of(at, rows), rows), :]
    lane = iota((rows, STATE), 1)
    target = lane % WINDOWS
    for p in range(PROMPTS):
        for i in range(LAGS):
            target = jnp.where(lane == i * WINDOWS + devices + p, (starts[p] + i) // TOK, target)
    for d in range(devices):
        mix_scr[d * rows : (d + 1) * rows, :] = jnp.where(target == d, mine, 0.0).astype(BF)
    b_all = jnp.concatenate(b_act + [spare], axis=0).astype(BF)
    extra = jnp.dot(mix_scr[...], b_all, preferred_element_type=F32)

    turn = at // rows
    from_prompts = jnp.where(
        turn == 0, x_act[0][devices:], jnp.where(turn == 1, x_act[1][devices:], x_act[2][devices:])
    )
    pad = jnp.zeros((8 - LAGS, STATE), F32)

    prefixes = []
    for p in range(PROMPTS):
        slot = slot_ref[p]
        place = plan.prefix
        if plan.slots > 1:
            place = pl.multiple_of(place + (slot % SLOTS_HERE) * rows, rows)
        prefixes.append(got_ref[slot // SLOTS_HERE, pl.ds(place, rows), :])
    wide = [piece.astype(F32) for piece in prefixes]
    state = jnp.zeros((rows, STATE), F32)
    states = plan.prompts * rows
    for d in range(devices):
        out_ref[d, :rows, :] = state.astype(BF)
        out_ref[d, rows:states, :] = jnp.zeros((states - rows, STATE), BF)
        from_block = jnp.concatenate([x_act[i][d : d + 1] for i in range(LAGS)] + [pad], axis=0)
        out_ref[d, states:, :] = jnp.where(turn == LAGS, from_block, from_prompts).astype(BF)
        base = state
        for p in range(PROMPTS):
            base = jnp.where(blocks[p] == d, wide[p], base)
        decay = factors[d : d + 1, DECAY_LANE : DECAY_LANE + 1]
        state = decay * base + (got_ref[d, :rows, :].astype(F32) + extra[d * rows : (d + 1) * rows])
    for p in range(PROMPTS):
        place = jnp.int32(0)
        for q in range(p + 1):
            place = place + (starts[q] > blocks[p] * TOK).astype(jnp.int32)
        place = jnp.minimum(place, plan.prompts - 1)
        out_ref[blocks[p], pl.ds(pl.multiple_of(place * rows, rows), rows), :] = prefixes[p]


def read_kernel(
    plan,
    len_ref,
    slot_ref,
    sent_ref,
    got_ref,
    act_ref,
    bc_ref,
    wbc_ref,
    within_ref,
    dt_ref,
    skip_ref,
    gate_ref,
    gated_ref,
    sq_ref,
    bc_scr,
):
    ctx = lax.axis_index("ctx")
    devices = got_ref.shape[0]
    heads = dt_ref.shape[0]
    chans = heads * WIDTH
    rows = chans // devices
    group = lax.axis_index("head") * heads // HEADS_GROUP
    groups = bc_ref.shape[1] // (2 * STATE)
    locs = [s - ctx * TOK for s in starts_of(len_ref)]

    token = iota((TOK, 16), 0)
    entry = iota((TOK, 16), 1)
    first = row_starts(locs, token)
    prompt = sum((token >= loc).astype(jnp.int32) for loc in locs) - 1

    bc_scr[8:, :] = jnp.concatenate(group_cols(lambda at: bc_ref[:, pl.ds(at, STATE)], group, groups), axis=1)
    before = sent_ref[(ctx + devices - 1) % devices, plan.bb :, :].astype(F32)
    bc_scr[8 - LAGS : 8, :STATE] = before[8 - LAGS : 8]
    bc_scr[8 - LAGS : 8, STATE:] = before[plan.cp - plan.bb : plan.cp - plan.bb + LAGS]
    tails = []
    for p in range(PROMPTS):
        pair = [tail_of(plan, sent_ref, slot_ref[p], at) for at in (plan.bt, plan.ct)]
        tails.append(jnp.concatenate(pair, axis=1))
    tails.append(jnp.zeros((16 - PROMPTS * LAGS, 2 * STATE), F32))
    tails = jnp.concatenate(tails, axis=0).astype(BF)
    taps = jnp.concatenate(group_cols(lambda at: wbc_ref[:, pl.ds(at, STATE)], group, groups), axis=1)
    conv = taps[LAGS : LAGS + 1] * bc_scr[8:, :]
    for k in range(1, LAGS + 1):
        outside = token - k < first
        pick = outside & (entry == prompt * LAGS + token - k - first + LAGS)
        tail_rows = jnp.dot(pick.astype(BF), tails, preferred_element_type=F32)
        value = jnp.where(outside[:, :1], tail_rows, bc_scr[8 - k : 8 + TOK - k, :])
        conv = conv + taps[LAGS - k : LAGS - k + 1] * value
    bc_act = silu(conv).astype(BF)
    b_act, c_act = bc_act[:, :STATE], bc_act[:, STATE:]

    near = token - first < LAGS
    by_prompt = (prompt == entry % PROMPTS) & (token - first == entry // PROMPTS) & near
    by_block = (token == entry - LAGS * PROMPTS) & (token < LAGS) & jnp.logical_not(near)
    pick = by_prompt | by_block
    other = (near | (token < LAGS))[:, :1]
    per = STATE // rows
    states = plan.prompts * rows
    spec = []
    for c in range(chans // STATE):
        spec.append(
            jnp.concatenate(
                [got_ref[c * per + j, states:, :].astype(F32)[:PROMPTS] for j in range(per)], axis=0
            )
        )
    spec = jnp.concatenate(spec, axis=1).astype(BF)
    patch = jnp.dot(pick.astype(BF), spec, preferred_element_type=F32)
    x_wide = jnp.where(other, patch, act_ref[...].astype(F32))

    live = live_matrix(locs)
    delta = softplus(dt_ref[...])
    within = within_ref[...]
    within_c = within.T
    scores = nt_dot(c_act, b_act)
    place = iota((TOK, STATE), 0)
    place = sum(((loc > 0) & (place >= loc)).astype(jnp.int32) for loc in locs)
    c_wide = c_act.astype(F32)
    reads = jnp.zeros((TOK, chans), F32)
    for j in range(plan.prompts):
        state = got_ref[:, j * rows : (j + 1) * rows, :].reshape(chans, STATE)
        reads = reads + nt_dot(jnp.where(place == j, c_wide, 0.0).astype(BF), state)
    y = widen(jnp.exp(within), WIDTH) * reads
    skip = jnp.dot(skip_ref[...], spread(WIDTH, heads), precision=HIGH, preferred_element_type=F32)
    left = iota((TOK, 2 * WIDTH), 1) < WIDTH
    part = jnp.zeros((TOK, TOK), F32)
    for j in range(heads // 2):
        pair = []
        for h in (2 * j, 2 * j + 1):
            fade = jnp.exp(jnp.where(live, within_c[:, h : h + 1] - within[h : h + 1, :], FAR))
            pair.append((scores * fade * delta[h : h + 1, :]).astype(BF))
        at = slice(2 * j * WIDTH, 2 * (j + 1) * WIDTH)
        x_pair = x_wide[:, at]
        both = jnp.concatenate([jnp.where(left, x_pair, 0.0), jnp.where(left, 0.0, x_pair)], axis=0)
        intra = jnp.dot(jnp.concatenate(pair, axis=1), both.astype(BF), preferred_element_type=F32)
        total = y[:, at] + (intra + skip[:, at] * x_pair)
        gated = total * silu(gate_ref[:, at].astype(F32))
        gated_ref[:, at] = gated
        part = part + gated * gated
    sq_ref[...] = jnp.sum(part.T, axis=0, keepdims=True)


def norm_kernel(gated_ref, sq_ref, gain_ref, out_ref):
    inverse = lax.rsqrt(sq_ref[...] / (HEADS_GROUP * WIDTH) + EPS)
    inverse = jnp.broadcast_to(inverse, (TOK, TOK)).T
    for c in range(out_ref.shape[1] // TOK):
        at = slice(c * TOK, (c + 1) * TOK)
        out_ref[:, at] = (gated_ref[:, at] * inverse * gain_ref[:, at]).astype(BF)


def on_device(
    x_mant,
    x_codes,
    bc_raw,
    gate_z,
    conv_x,
    conv_bc,
    dt_raw,
    a_log,
    d_skip,
    norm_gain,
    prompt_lengths,
    cache_slot,
    prefix_state,
    tail_x,
    tail_bc,
):
    devices = lax.axis_size("ctx")
    head_devices = lax.axis_size("head")
    heads = a_log.shape[0]
    chans = heads * WIDTH
    rows = chans // devices
    dt_t = dt_raw.T
    a_row = a_log.reshape(1, heads)
    skip_row = d_skip.reshape(1, heads)
    tail_x = jnp.transpose(tail_x, (1, 0, 2))
    tail_bc = jnp.transpose(tail_bc, (1, 0, 2))
    prefixes = prefix_state.reshape(SLOTS_HERE, devices, rows, STATE)

    def first_part(plan):
        sources = [
            prompt_lengths,
            cache_slot,
            dt_t,
            a_row,
            x_codes.T,
            x_mant,
            bc_raw,
            tail_x,
            tail_bc,
            conv_x,
            conv_bc,
        ]
        return call(
            functools.partial(block_kernel, plan),
            (
                jax.ShapeDtypeStruct((devices, plan.rows, STATE), BF),
                jax.ShapeDtypeStruct((TOK, chans), BF),
                jax.ShapeDtypeStruct((heads, TOK), F32),
                jax.ShapeDtypeStruct((1,), jnp.int32),
            ),
            in_specs=[hbm()] * 12,
            out_specs=(vmem(), vmem(), vmem(), smem()),
            scratch_shapes=[pltpu.SMEM((PROMPTS,), jnp.int32)] * 2
            + [pltpu.VMEM(source.shape, source.dtype) for source in sources[2:]]
            + [pltpu.VMEM((TOK + 8, chans + STATE), F32), pltpu.SemaphoreType.DMA((11 + plan.slots,))],
        )(*[pinned(source) for source in sources + [prefixes]])

    def second_part(plan, send1, act, within):
        got1 = lax.all_to_all(send1, "ctx", 0, 0)
        send2 = call(
            functools.partial(scan_kernel, plan),
            jax.ShapeDtypeStruct((devices, plan.prompts * rows + 8, STATE), BF),
            in_specs=[smem(), smem()] + [vmem()] * 3,
            out_specs=vmem(),
            scratch_shapes=[
                pltpu.VMEM((devices * 8, STATE), F32),
                pltpu.VMEM((devices * 8, STATE), F32),
                pltpu.VMEM((STATE, STATE), F32),
                pltpu.VMEM((chans, STATE), BF),
            ],
        )(prompt_lengths, cache_slot, got1, conv_x, conv_bc)
        got2 = lax.all_to_all(send2, "ctx", 0, 0)
        return call(
            functools.partial(read_kernel, plan),
            (jax.ShapeDtypeStruct((TOK, chans), F32), jax.ShapeDtypeStruct((1, TOK), F32)),
            in_specs=[smem(), smem()] + [vmem()] * 9,
            out_specs=(vmem(), vmem()),
            scratch_shapes=[pltpu.VMEM((TOK + 8, 2 * STATE), F32)],
        )(
            prompt_lengths,
            cache_slot,
            got1,
            got2,
            act,
            bc_raw,
            conv_bc,
            within,
            dt_t,
            skip_row,
            gate_z,
        )

    send1, act, within, fits = first_part(SMALL)
    gated, squares = lax.cond(
        fits[0] == 1,
        lambda: second_part(SMALL, send1, act, within),
        lambda: second_part(FULL, *first_part(FULL)[:3]),
    )
    pairs = [[i, i + 1] for i in range(0, head_devices, 2)]
    total = lax.psum(squares, "head", axis_index_groups=pairs)
    return call(
        norm_kernel,
        jax.ShapeDtypeStruct((TOK, chans), BF),
        in_specs=[vmem()] * 3,
        out_specs=vmem(),
    )(gated, total, norm_gain.reshape(1, chans))


def solution(mesh):
    in_specs = (
        P("ctx", "head"),
        P("ctx", "head"),
        P("ctx", None),
        P("ctx", "head"),
        P(None, "head"),
        P(),
        P("ctx", "head"),
        P("head"),
        P("head"),
        P("head"),
        P(),
        P(),
        P("ctx", "head", None),
        P("ctx", None, "head"),
        P("ctx", None, None),
    )
    out_specs = P("ctx", "head")
    return jax.shard_map(
        on_device, mesh=mesh, in_specs=in_specs, out_specs=out_specs, check_vma=False
    )
```

```python
import functools

import jax
import jax.numpy as jnp
from jax import lax
from jax.experimental import pallas as pl
from jax.experimental.pallas import tpu as pltpu
from jax.sharding import PartitionSpec as P

BF = jnp.bfloat16
F32 = jnp.float32
INTERPRET = False

TOK = 128
WIDTH = 64
STATE = 128
MXB = 32
LAGS = 3
PROMPTS = 4
HEADS_GROUP = 32
SLOTS_HERE = 2
EPS = 1e-05
FAR = -1e30
NORM_PARTS = 4


class Plan:
    def __init__(self, slots, prompts):
        self.slots, self.prompts = slots, prompts
        self.begun = 1 if prompts == 2 else PROMPTS
        at = 32
        self.prefix, at = at, at + 32 * slots
        self.xb, at = at, at + 8
        self.bb, at = at, at + 8
        self.xp, at = at, at + LAGS * self.begun
        self.xt, at = at, at + LAGS * slots
        self.bp, at = at, at + LAGS * self.begun
        self.bt, at = at, at + LAGS * slots
        self.ct, at = at, at + LAGS * slots
        self.cp, at = at, at + 1
        self.used = at
        self.rows = (at + 7) // 8 * 8


PLANS = (Plan(1, 2), Plan(SLOTS_HERE, 2), Plan(1, 3), Plan(SLOTS_HERE, PROMPTS))
DECAY_LANE = LAGS + PROMPTS * LAGS
WINDOWS = 40


def call(kernel, out_shape, **kw):
    return pl.pallas_call(
        kernel,
        out_shape=out_shape,
        interpret=INTERPRET,
        compiler_params=pltpu.CompilerParams(vmem_limit_bytes=48 * 1024 * 1024),
        **kw,
    )


def vmem():
    return pl.BlockSpec(memory_space=pltpu.VMEM)


def hbm():
    return pl.BlockSpec(memory_space=pltpu.HBM)


def pinned(array):
    return array if INTERPRET else pltpu.with_memory_space_constraint(array, pltpu.HBM)


def smem():
    return pl.BlockSpec(memory_space=pltpu.SMEM)


def starts_of(len_ref):
    found = [jnp.int32(0)]
    for p in range(PROMPTS - 1):
        found.append(found[-1] + len_ref[p])
    return found


def iota(shape, axis):
    return lax.broadcasted_iota(jnp.int32, shape, axis)


def row_starts(locs, token):
    first = jnp.full(token.shape, locs[0], jnp.int32)
    for p in range(1, PROMPTS):
        first = jnp.where(token >= locs[p], locs[p], first)
    return first


def softplus(v):
    return jnp.maximum(v, 0.0) + jnp.log1p(jnp.exp(-jnp.abs(v)))


def silu(v):
    half = 0.5 * v
    return half + half * jnp.tanh(half)


def terms(v, axis):
    high = v.astype(BF).astype(F32)
    mid = (v - high).astype(BF).astype(F32)
    return jnp.concatenate([high, mid, v - high - mid], axis=axis)


def spread(per, count):
    shape = (count, count * per)
    return (iota(shape, 1) // per == iota(shape, 0)).astype(BF)


def nt_dot(a, b, **kw):
    return lax.dot_general(a, b, (((1,), (1,)), ((), ())), preferred_element_type=F32, **kw)


def live_matrix(locs):
    row, col = iota((TOK, TOK), 0), iota((TOK, TOK), 1)
    return (col <= row) & (col >= row_starts(locs, row))


def spread_terms(heads):
    shape = (3 * heads, heads * WIDTH)
    return (iota(shape, 1) // WIDTH == iota(shape, 0) % heads).astype(BF)


def widen(per_head_t):
    columns = terms(per_head_t, 0).T.astype(BF)
    return jnp.dot(columns, spread_terms(per_head_t.shape[0]), preferred_element_type=F32)


def exact_nt(v, zero_one):
    rows = v.shape[0]
    parts = nt_dot(terms(v, 0).astype(BF), zero_one.astype(BF))
    return parts[:rows] + parts[rows : 2 * rows] + parts[2 * rows :]


def plan_number(starts, slot_ref):
    crowd = jnp.int32(2)
    for p in range(PROMPTS - 2):
        crowd = jnp.where((starts[p + 1] - 1) // TOK == starts[p + 2] // TOK, 3, crowd)
    crowd = jnp.where((starts[1] - 1) // TOK == starts[3] // TOK, 4, crowd)
    shared = jnp.int32(0)
    for p in range(PROMPTS):
        for q in range(p):
            one, two = slot_ref[p], slot_ref[q]
            both = (one // SLOTS_HERE == two // SLOTS_HERE) & (one != two)
            shared = jnp.where(both, 1, shared)
    return jnp.where(crowd == 2, shared, jnp.where((crowd == 3) & (shared == 0), 2, 3))


def block_kernel(plan, *refs):
    (
        len_hbm,
        slot_hbm,
        dt_hbm,
        alog_hbm,
        xc_hbm,
        xm_hbm,
        bc_hbm,
        tx_hbm,
        tbc_hbm,
        wx_hbm,
        wbc_hbm,
        prefix_hbm,
    ) = refs[:12]
    out_ref, act_ref, within_ref, delta_ref, bc_ref, taps_ref, number_ref = refs[12:19]
    (len_ref, slot_ref, dt_ref, alog_ref, xc_ref, xm_ref, tx_ref, tbc_ref, wx_ref) = refs[19:28]
    x_scr, sems = refs[28:]
    rows = plan.prefix
    small = plan.slots == 1
    ctx = lax.axis_index("ctx")
    heads = dt_ref.shape[0]
    chans = heads * WIDTH
    group = lax.axis_index("head") * heads // HEADS_GROUP
    groups = bc_hbm.shape[1] // (2 * STATE)
    b_cols = pl.ds(pl.multiple_of(group * STATE, STATE), STATE)
    x_cols = pl.ds(pl.multiple_of(ctx * rows // STATE * STATE, STATE), STATE)
    c_cols = pl.ds(pl.multiple_of((groups + group) * STATE, STATE), STATE)
    copies = [
        pltpu.make_async_copy(src, dst, sems.at[n])
        for n, (src, dst) in enumerate(
            [
                (len_hbm, len_ref),
                (slot_hbm, slot_ref),
                (dt_hbm, dt_ref),
                (alog_hbm, alog_ref),
                (xc_hbm, xc_ref),
                (xm_hbm, xm_ref),
                (bc_hbm.at[:, b_cols], bc_ref.at[0]),
                (bc_hbm.at[:, c_cols], bc_ref.at[1]),
                (wx_hbm, wx_ref),
                (wbc_hbm.at[:, b_cols], taps_ref.at[1]),
                (wx_hbm.at[:, x_cols], taps_ref.at[0]),
                (wbc_hbm.at[:, c_cols], taps_ref.at[2]),
                (tx_hbm, tx_ref),
                (tbc_hbm.at[:, :, b_cols], tbc_ref.at[0]),
                (tbc_hbm.at[:, :, c_cols], tbc_ref.at[1]),
            ]
        )
    ]
    for copy in copies:
        copy.start()
    copies[0].wait()
    copies[1].wait()
    used = jnp.int32(0)
    for p in range(PROMPTS):
        used = jnp.where(slot_ref[p] // SLOTS_HERE == ctx, slot_ref[p] % SLOTS_HERE, used)
    states = [
        pltpu.make_async_copy(
            prefix_hbm.at[used if small else s],
            out_ref.at[:, pl.ds(plan.prefix + s * rows, rows), :],
            sems.at[len(copies) + s],
        )
        for s in range(plan.slots)
    ]
    for copy in states:
        copy.start()
    for copy in copies[2:]:
        copy.wait()

    devices = out_ref.shape[0]
    starts = starts_of(len_ref)
    number_ref[0] = plan_number(starts, slot_ref)
    locs = [s - ctx * TOK for s in starts]

    scale = jnp.exp2(xc_ref[...].astype(F32)).T.astype(BF)
    wide = jnp.dot(scale, spread(MXB, xc_ref.shape[0]), preferred_element_type=F32)
    x = xm_ref[...].astype(F32) * wide
    b_raw, c_raw = bc_ref[0].astype(F32), bc_ref[1].astype(F32)
    x_scr[8:, :chans] = x
    x_scr[8:, chans:] = b_raw
    x_scr[:8, :] = jnp.zeros((8, chans + STATE), F32)

    live = live_matrix(locs)
    delta = softplus(dt_ref[...])
    delta_ref[...] = delta
    log_decay = -jnp.exp(alog_ref[...].T) * delta
    within = exact_nt(log_decay, live)
    within_ref[...] = within
    token = iota((heads, TOK), 1)
    first = row_starts(locs, token)
    last_start = row_starts(locs, jnp.full((heads, TOK), TOK - 1, jnp.int32))
    to_end = delta * jnp.exp(jnp.where(token >= last_start, within[:, TOK - 1 :] - within, FAR))
    regular = (token >= LAGS) & (token - first >= LAGS)
    factor = widen(jnp.where(regular, to_end, 0.0))

    taps = jnp.concatenate([wx_ref[...], taps_ref[1]], axis=1)
    conv = taps[LAGS : LAGS + 1] * x_scr[8:, :]
    for k in range(1, LAGS + 1):
        conv = conv + taps[LAGS - k : LAGS - k + 1] * x_scr[8 - k : 8 + TOK - k, :]
    act = silu(conv).astype(BF)
    act_ref[...] = act[:, :chans]
    inputs = (act[:, :chans].astype(F32) * factor).astype(BF)
    ends = lax.dot_general(
        inputs, act[:, chans:], (((0,), (0,)), ((), ())), preferred_element_type=F32
    ).astype(BF)

    def chosen_rows(modulus, lowest):
        entry = iota((16, TOK), 0)
        begin = jnp.full((16, TOK), -TOK, jnp.int32)
        for p in range(PROMPTS):
            for i in range(LAGS):
                at = locs[p] + i
                inside = (len_ref[p] > i) & (at >= lowest) & (at < TOK)
                begin = jnp.where((entry == p % modulus * LAGS + i) & inside, at, begin)
        return iota((16, TOK), 1) == begin

    raw = jnp.concatenate([x, b_raw], axis=1).astype(BF)
    at_start = jnp.dot(chosen_rows(plan.begun, LAGS).astype(BF), raw, preferred_element_type=F32)
    at_start = at_start[: plan.begun * LAGS]
    at_block = jnp.where((token < LAGS) & (token - first >= LAGS), to_end, 0.0)
    vals = exact_nt(to_end, chosen_rows(PROMPTS, 0))[:, : PROMPTS * LAGS]
    vals = jnp.concatenate(
        [at_block[:, :LAGS], vals, jnp.exp(within[:, TOK - 1 :]), jnp.zeros((heads, TOK - 16), F32)], axis=1
    )
    high = vals.astype(BF).astype(F32)
    low = vals - high

    tails_x, tails_b, tails_c = [], [], []
    for s in range(plan.slots):
        for i in range(LAGS):
            for found, two in ((tails_x, tx_ref[i]), (tails_b, tbc_ref[0, i]), (tails_c, tbc_ref[1, i])):
                two = two.astype(F32)
                found.append(jnp.where(used == 1, two[1:], two[:1]) if small else two[s : s + 1])
    tails = jnp.concatenate(tails_x, axis=0)
    gap = jnp.zeros((2, STATE), F32)
    c_last = c_raw[TOK - LAGS :]
    b_tile = jnp.concatenate([b_raw[:LAGS], c_last[:2], b_raw[TOK - LAGS :]], axis=0)
    foot = jnp.concatenate(
        [at_start[:, chans:]] + tails_b + tails_c + [c_last[2:]],
        axis=0,
    )
    if plan.rows > plan.used:
        foot = jnp.concatenate([foot, jnp.zeros((plan.rows - plan.used, STATE), F32)], axis=0)
    tile_row = iota((8, STATE), 0)
    for c in range(chans // STATE):
        lanes = slice(c * STATE, (c + 1) * STATE)
        x_tile = jnp.concatenate([x[:LAGS, lanes], gap, x[TOK - LAGS :, lanes]], axis=0)
        part = jnp.concatenate([b_tile, at_start[:, lanes], tails[:, lanes], foot], axis=0).astype(BF)
        for k in range(c * STATE // rows, (c + 1) * STATE // rows):
            h = k * rows // WIDTH
            out_ref[k, :rows, :] = ends[k * rows : (k + 1) * rows]
            tile = jnp.where(tile_row == LAGS, high[h : h + 1], x_tile)
            tile = jnp.where(tile_row == LAGS + 1, low[h : h + 1], tile)
            out_ref[k, plan.xb : plan.bb, :] = tile.astype(BF)
            out_ref[k, plan.bb :, :] = part
    for copy in states:
        copy.wait()


def tail_of(plan, got_ref, slot, tail_at):
    owner = got_ref[slot // SLOTS_HERE, plan.xb :, :].astype(F32)
    place = tail_at - plan.xb
    tail = owner[place : place + LAGS]
    if plan.slots > 1:
        tail = jnp.where(slot % SLOTS_HERE == 1, owner[place + LAGS : place + 2 * LAGS], tail)
    return tail


def scan_kernel(plan, len_ref, slot_ref, got_ref, taps_ref, out_ref, x_scr, b_scr, in_scr, mix_scr):
    devices = got_ref.shape[0]
    rows = plan.prefix
    ctx = lax.axis_index("ctx")
    at = ctx * rows % STATE
    starts = starts_of(len_ref)
    blocks = [s // TOK for s in starts]

    x_scr[...] = got_ref[:, plan.xb : plan.xb + 8, :].astype(F32).reshape(devices * 8, STATE)
    b_scr[...] = got_ref[:, plan.bb : plan.bb + 8, :].astype(F32).reshape(devices * 8, STATE)
    factors = x_scr[pl.ds(LAGS, devices, stride=8), :] + x_scr[pl.ds(LAGS + 1, devices, stride=8), :]
    prompt_factors = jnp.sum(factors, axis=0, keepdims=True)

    def windows(scr, start_at, tail_at):
        before, now = [], []
        for p in range(PROMPTS):
            own = got_ref[blocks[p], plan.xb :, :].astype(F32)
            place = start_at - plan.xb + p % plan.begun * LAGS
            found = []
            for i in range(LAGS):
                row = (starts[p] + i) % TOK
                block = jnp.minimum((starts[p] + i) // TOK, devices - 1)
                early = scr[pl.ds(8 * block + jnp.minimum(row, LAGS - 1), 1), :]
                found.append(jnp.where(row < LAGS, early, own[place + i : place + i + 1]))
            now.append(found)
            before.append(tail_of(plan, got_ref, slot_ref[p], tail_at))
        pad = jnp.zeros((WINDOWS - devices - PROMPTS, STATE), F32)
        found = []
        for i in range(LAGS):
            last = scr[pl.ds(8 - LAGS + i, devices, stride=8), :]
            last = jnp.concatenate([last[devices - 1 :], last[: devices - 1]], axis=0)
            found.append(jnp.concatenate([last] + [b[i : i + 1] for b in before] + [pad], axis=0))
        for i in range(LAGS):
            fresh = scr[pl.ds(i, devices, stride=8), :]
            found.append(jnp.concatenate([fresh] + [n[i] for n in now] + [pad], axis=0))
        return found

    def activation(rows6, taps, i):
        conv = taps[LAGS : LAGS + 1] * rows6[LAGS + i]
        for k in range(1, LAGS + 1):
            conv = conv + taps[LAGS - k : LAGS - k + 1] * rows6[LAGS + i - k]
        return silu(conv).astype(BF).astype(F32)

    x_rows = windows(x_scr, plan.xp, plan.xt)
    b_rows = windows(b_scr, plan.bp, plan.bt)
    x_act = [activation(x_rows, taps_ref[0], i) for i in range(LAGS)]
    b_act = [activation(b_rows, taps_ref[1], i) for i in range(LAGS)]
    scaled = []
    for i in range(LAGS):
        column = [factors[:, i : i + 1]]
        for p in range(PROMPTS):
            lane = LAGS + p * LAGS + i
            column.append(prompt_factors[:, lane : lane + 1])
        column.append(jnp.zeros((WINDOWS - devices - PROMPTS, 1), F32))
        scaled.append(x_act[i] * jnp.concatenate(column, axis=0))
    spare = jnp.zeros((STATE - LAGS * WINDOWS, STATE), F32)
    in_scr[...] = jnp.concatenate(scaled + [spare], axis=0).T
    mine = in_scr[pl.ds(pl.multiple_of(at, rows), rows), :]
    lane = iota((rows, STATE), 1)
    target = lane % WINDOWS
    for p in range(PROMPTS):
        for i in range(LAGS):
            target = jnp.where(lane == i * WINDOWS + devices + p, (starts[p] + i) // TOK, target)
    for d in range(devices):
        mix_scr[d * rows : (d + 1) * rows, :] = jnp.where(target == d, mine, 0.0).astype(BF)
    b_all = jnp.concatenate(b_act + [spare], axis=0).astype(BF)
    extra = jnp.dot(mix_scr[...], b_all, preferred_element_type=F32)

    turn = at // rows
    from_prompts = jnp.where(
        turn == 0, x_act[0][devices:], jnp.where(turn == 1, x_act[1][devices:], x_act[2][devices:])
    )
    pad = jnp.zeros((8 - LAGS, STATE), F32)

    prefixes = []
    for p in range(PROMPTS):
        slot = slot_ref[p]
        place = plan.prefix
        if plan.slots > 1:
            place = pl.multiple_of(place + (slot % SLOTS_HERE) * rows, rows)
        prefixes.append(got_ref[slot // SLOTS_HERE, pl.ds(place, rows), :])
    wide = [piece.astype(F32) for piece in prefixes]
    state = jnp.zeros((rows, STATE), F32)
    states = plan.prompts * rows
    for d in range(devices):
        out_ref[d, :rows, :] = state.astype(BF)
        out_ref[d, rows:states, :] = jnp.zeros((states - rows, STATE), BF)
        from_block = jnp.concatenate([x_act[i][d : d + 1] for i in range(LAGS)] + [pad], axis=0)
        out_ref[d, states:, :] = jnp.where(turn == LAGS, from_block, from_prompts).astype(BF)
        base = state
        for p in range(PROMPTS):
            base = jnp.where(blocks[p] == d, wide[p], base)
        decay = factors[d : d + 1, DECAY_LANE : DECAY_LANE + 1]
        state = decay * base + (got_ref[d, :rows, :].astype(F32) + extra[d * rows : (d + 1) * rows])
    for p in range(PROMPTS):
        place = jnp.int32(0)
        for q in range(p + 1):
            place = place + (starts[q] > blocks[p] * TOK).astype(jnp.int32)
        place = jnp.minimum(place, plan.prompts - 1)
        out_ref[blocks[p], pl.ds(pl.multiple_of(place * rows, rows), rows), :] = prefixes[p]


def read_kernel(
    plan,
    len_ref,
    slot_ref,
    sent_ref,
    got_ref,
    act_ref,
    bc_ref,
    taps_ref,
    within_ref,
    delta_ref,
    skip_ref,
    gate_ref,
    gated_ref,
    sq_ref,
    bc_scr,
):
    ctx = lax.axis_index("ctx")
    devices = got_ref.shape[0]
    heads = delta_ref.shape[0]
    chans = heads * WIDTH
    rows = chans // devices
    locs = [s - ctx * TOK for s in starts_of(len_ref)]

    token = iota((TOK, 16), 0)
    entry = iota((TOK, 16), 1)
    first = row_starts(locs, token)
    prompt = sum((token >= loc).astype(jnp.int32) for loc in locs) - 1

    bc_scr[8:, :] = jnp.concatenate([bc_ref[0], bc_ref[1]], axis=1).astype(F32)
    before = sent_ref[(ctx + devices - 1) % devices, plan.bb :, :].astype(F32)
    bc_scr[8 - LAGS : 8, :STATE] = before[8 - LAGS : 8]
    c_last = plan.cp - plan.bb
    bc_scr[8 - LAGS : 8, STATE:] = jnp.concatenate([before[LAGS : LAGS + 2], before[c_last : c_last + 1]], axis=0)
    tails = []
    for p in range(PROMPTS):
        pair = [tail_of(plan, sent_ref, slot_ref[p], at) for at in (plan.bt, plan.ct)]
        tails.append(jnp.concatenate(pair, axis=1))
    tails.append(jnp.zeros((16 - PROMPTS * LAGS, 2 * STATE), F32))
    tails = jnp.concatenate(tails, axis=0).astype(BF)
    taps = jnp.concatenate([taps_ref[1], taps_ref[2]], axis=1)
    conv = taps[LAGS : LAGS + 1] * bc_scr[8:, :]
    for k in range(1, LAGS + 1):
        outside = token - k < first
        pick = outside & (entry == prompt * LAGS + token - k - first + LAGS)
        tail_rows = jnp.dot(pick.astype(BF), tails, preferred_element_type=F32)
        value = jnp.where(outside[:, :1], tail_rows, bc_scr[8 - k : 8 + TOK - k, :])
        conv = conv + taps[LAGS - k : LAGS - k + 1] * value
    bc_act = silu(conv).astype(BF)
    b_act, c_act = bc_act[:, :STATE], bc_act[:, STATE:]

    near = token - first < LAGS
    by_prompt = (prompt == entry % PROMPTS) & (token - first == entry // PROMPTS) & near
    by_block = (token == entry - LAGS * PROMPTS) & (token < LAGS) & jnp.logical_not(near)
    pick = by_prompt | by_block
    other = (near | (token < LAGS))[:, :1]
    per = STATE // rows
    states = plan.prompts * rows
    spec = []
    for c in range(chans // STATE):
        spec.append(
            jnp.concatenate(
                [got_ref[c * per + j, states:, :].astype(F32)[:PROMPTS] for j in range(per)], axis=0
            )
        )
    spec = jnp.concatenate(spec, axis=1).astype(BF)
    patch = jnp.dot(pick.astype(BF), spec, preferred_element_type=F32)
    x_wide = jnp.where(other, patch, act_ref[...].astype(F32))

    live = live_matrix(locs)
    delta = delta_ref[...]
    within = within_ref[...]
    within_c = within.T
    scores = nt_dot(c_act, b_act)
    place = iota((TOK, STATE), 0)
    place = sum(((loc > 0) & (place >= loc)).astype(jnp.int32) for loc in locs)
    c_wide = c_act.astype(F32)
    reads = jnp.zeros((TOK, chans), F32)
    for j in range(plan.prompts):
        state = got_ref[:, j * rows : (j + 1) * rows, :].reshape(chans, STATE)
        reads = reads + nt_dot(jnp.where(place == j, c_wide, 0.0).astype(BF), state)
    y = widen(jnp.exp(within)) * reads
    skip = jnp.dot(terms(skip_ref[...], 1).astype(BF), spread_terms(heads), preferred_element_type=F32)
    left = iota((TOK, 2 * WIDTH), 1) < WIDTH
    part = jnp.zeros((TOK, TOK), F32)
    for j in range(heads // 2):
        pair = []
        for h in (2 * j, 2 * j + 1):
            fade = jnp.exp(jnp.where(live, within_c[:, h : h + 1] - within[h : h + 1, :], FAR))
            pair.append((scores * fade * delta[h : h + 1, :]).astype(BF))
        at = slice(2 * j * WIDTH, 2 * (j + 1) * WIDTH)
        x_pair = x_wide[:, at]
        both = jnp.concatenate([jnp.where(left, x_pair, 0.0), jnp.where(left, 0.0, x_pair)], axis=0)
        intra = jnp.dot(jnp.concatenate(pair, axis=1), both.astype(BF), preferred_element_type=F32)
        total = y[:, at] + (intra + skip[:, at] * x_pair)
        gated = total * silu(gate_ref[:, at].astype(F32))
        gated_ref[:, at] = gated
        part = part + gated * gated
    sq_ref[...] = jnp.sum(part.T, axis=0, keepdims=True)


def norm_kernel(gated_ref, sq_ref, gain_ref, out_hbm, out_scr, sems):
    inverse = lax.rsqrt(sq_ref[...] / (HEADS_GROUP * WIDTH) + EPS)
    inverse = jnp.broadcast_to(inverse, (TOK, TOK)).T
    rows = TOK // NORM_PARTS
    copies = []
    for part in range(NORM_PARTS):
        at = slice(part * rows, (part + 1) * rows)
        for c in range(out_scr.shape[1] // TOK):
            cols = slice(c * TOK, (c + 1) * TOK)
            out_scr[at, cols] = (gated_ref[at, cols] * inverse[at] * gain_ref[:, cols]).astype(BF)
        copies.append(pltpu.make_async_copy(out_scr.at[at], out_hbm.at[at], sems.at[part]))
        copies[-1].start()
    for copy in copies:
        copy.wait()


def on_device(
    x_mant,
    x_codes,
    bc_raw,
    gate_z,
    conv_x,
    conv_bc,
    dt_raw,
    a_log,
    d_skip,
    norm_gain,
    prompt_lengths,
    cache_slot,
    prefix_state,
    tail_x,
    tail_bc,
):
    devices = lax.axis_size("ctx")
    head_devices = lax.axis_size("head")
    heads = a_log.shape[0]
    chans = heads * WIDTH
    rows = chans // devices
    dt_t = dt_raw.T
    a_row = a_log.reshape(1, heads)
    skip_row = d_skip.reshape(1, heads)
    tail_x = jnp.transpose(tail_x, (1, 0, 2))
    tail_bc = jnp.transpose(tail_bc, (1, 0, 2))
    prefixes = prefix_state.reshape(SLOTS_HERE, devices, rows, STATE)

    def first_part(plan):
        sources = [
            prompt_lengths,
            cache_slot,
            dt_t,
            a_row,
            x_codes.T,
            x_mant,
            bc_raw,
            tail_x,
            tail_bc,
            conv_x,
            conv_bc,
        ]
        return call(
            functools.partial(block_kernel, plan),
            (
                jax.ShapeDtypeStruct((devices, plan.rows, STATE), BF),
                jax.ShapeDtypeStruct((TOK, chans), BF),
                jax.ShapeDtypeStruct((heads, TOK), F32),
                jax.ShapeDtypeStruct((heads, TOK), F32),
                jax.ShapeDtypeStruct((2, TOK, STATE), BF),
                jax.ShapeDtypeStruct((3, conv_x.shape[0], STATE), F32),
                jax.ShapeDtypeStruct((1,), jnp.int32),
            ),
            in_specs=[hbm()] * 12,
            out_specs=(vmem(),) * 6 + (smem(),),
            scratch_shapes=[pltpu.SMEM((PROMPTS,), jnp.int32)] * 2
            + [pltpu.VMEM(source.shape, source.dtype) for source in sources[2:6]]
            + [
                pltpu.VMEM(tail_x.shape, BF),
                pltpu.VMEM((2,) + tail_x.shape[:2] + (STATE,), BF),
                pltpu.VMEM(conv_x.shape, F32),
                pltpu.VMEM((TOK + 8, chans + STATE), F32),
                pltpu.SemaphoreType.DMA((15 + plan.slots,)),
            ],
        )(*[pinned(source) for source in sources + [prefixes]])

    def second_part(plan, send1, act, within, delta, bc_here, taps):
        got1 = lax.all_to_all(send1, "ctx", 0, 0)
        send2 = call(
            functools.partial(scan_kernel, plan),
            jax.ShapeDtypeStruct((devices, plan.prompts * rows + 8, STATE), BF),
            in_specs=[smem(), smem()] + [vmem()] * 2,
            out_specs=vmem(),
            scratch_shapes=[
                pltpu.VMEM((devices * 8, STATE), F32),
                pltpu.VMEM((devices * 8, STATE), F32),
                pltpu.VMEM((STATE, STATE), F32),
                pltpu.VMEM((chans, STATE), BF),
            ],
        )(prompt_lengths, cache_slot, got1, taps)
        got2 = lax.all_to_all(send2, "ctx", 0, 0)
        return call(
            functools.partial(read_kernel, plan),
            (jax.ShapeDtypeStruct((TOK, chans), F32), jax.ShapeDtypeStruct((1, TOK), F32)),
            in_specs=[smem(), smem()] + [vmem()] * 9,
            out_specs=(vmem(), vmem()),
            scratch_shapes=[pltpu.VMEM((TOK + 8, 2 * STATE), F32)],
        )(
            prompt_lengths,
            cache_slot,
            got1,
            got2,
            act,
            bc_here,
            taps,
            within,
            delta,
            skip_row,
            gate_z,
        )

    *first, number = first_part(PLANS[0])
    gated, squares = lax.switch(
        number[0],
        [lambda: second_part(PLANS[0], *first)]
        + [lambda plan=plan: second_part(plan, *first_part(plan)[:-1]) for plan in PLANS[1:]],
    )
    pairs = [[i, i + 1] for i in range(0, head_devices, 2)]
    total = lax.psum(squares, "head", axis_index_groups=pairs)
    return call(
        norm_kernel,
        jax.ShapeDtypeStruct((TOK, chans), BF),
        in_specs=[vmem()] * 3,
        out_specs=hbm(),
        scratch_shapes=[pltpu.VMEM((TOK, chans), BF), pltpu.SemaphoreType.DMA((NORM_PARTS,))],
    )(gated, total, norm_gain.reshape(1, chans))


def solution(mesh):
    in_specs = (
        P("ctx", "head"),
        P("ctx", "head"),
        P("ctx", None),
        P("ctx", "head"),
        P(None, "head"),
        P(),
        P("ctx", "head"),
        P("head"),
        P("head"),
        P("head"),
        P(),
        P(),
        P("ctx", "head", None),
        P("ctx", None, "head"),
        P("ctx", None, None),
    )
    out_specs = P("ctx", "head")
    return jax.shard_map(
        on_device, mesh=mesh, in_specs=in_specs, out_specs=out_specs, check_vma=False
    )
```

```python
import functools

import jax
import jax.numpy as jnp
from jax import lax
from jax.experimental import pallas as pl
from jax.experimental.pallas import tpu as pltpu
from jax.sharding import PartitionSpec as P

BF = jnp.bfloat16
F32 = jnp.float32
INTERPRET = False

TOK = 128
WIDTH = 64
STATE = 128
MXB = 32
LAGS = 3
PROMPTS = 4
HEADS_GROUP = 32
SLOTS_HERE = 2
EPS = 1e-05
FAR = -1e30
NORM_PARTS = 4


class Plan:
    def __init__(self, slots, prompts):
        self.slots, self.prompts = slots, prompts
        self.begun = prompts - 1
        at = 32
        self.prefix, at = at, at + 32 * slots
        self.xb, at = at, at + 8
        self.bb, at = at, at + 8
        self.xp, at = at, at + LAGS * self.begun
        self.xt, at = at, at + LAGS * slots
        self.bp, at = at, at + LAGS * self.begun
        self.bt, at = at, at + LAGS * slots
        self.ct, at = at, at + LAGS * slots
        self.cp, at = at, at + 1
        self.used = at
        self.rows = (at + 7) // 8 * 8


PLANS = (Plan(1, 2), Plan(SLOTS_HERE, 2), Plan(1, 3), Plan(SLOTS_HERE, PROMPTS))
DECAY_LANE = LAGS + PROMPTS * LAGS
WINDOWS = 40


def call(kernel, out_shape, **kw):
    return pl.pallas_call(
        kernel,
        out_shape=out_shape,
        interpret=INTERPRET,
        compiler_params=pltpu.CompilerParams(vmem_limit_bytes=48 * 1024 * 1024),
        **kw,
    )


def vmem():
    return pl.BlockSpec(memory_space=pltpu.VMEM)


def hbm():
    return pl.BlockSpec(memory_space=pltpu.HBM)


def pinned(array):
    return array if INTERPRET else pltpu.with_memory_space_constraint(array, pltpu.HBM)


def smem():
    return pl.BlockSpec(memory_space=pltpu.SMEM)


def starts_of(len_ref):
    found = [jnp.int32(0)]
    for p in range(PROMPTS - 1):
        found.append(found[-1] + len_ref[p])
    return found


def iota(shape, axis):
    return lax.broadcasted_iota(jnp.int32, shape, axis)


def row_starts(locs, token):
    first = jnp.full(token.shape, locs[0], jnp.int32)
    for p in range(1, PROMPTS):
        first = jnp.where(token >= locs[p], locs[p], first)
    return first


def softplus(v):
    return jnp.maximum(v, 0.0) + jnp.log1p(jnp.exp(-jnp.abs(v)))


def silu(v):
    half = 0.5 * v
    return half + half * jnp.tanh(half)


def terms(v, axis):
    high = v.astype(BF).astype(F32)
    mid = (v - high).astype(BF).astype(F32)
    return jnp.concatenate([high, mid, v - high - mid], axis=axis)


def spread(per, count):
    shape = (count, count * per)
    return (iota(shape, 1) // per == iota(shape, 0)).astype(BF)


def nt_dot(a, b, **kw):
    return lax.dot_general(a, b, (((1,), (1,)), ((), ())), preferred_element_type=F32, **kw)


def live_matrix(locs):
    row, col = iota((TOK, TOK), 0), iota((TOK, TOK), 1)
    return (col <= row) & (col >= row_starts(locs, row))


def spread_terms(heads):
    shape = (3 * heads, heads * WIDTH)
    return (iota(shape, 1) // WIDTH == iota(shape, 0) % heads).astype(BF)


def widen(per_head_t):
    columns = terms(per_head_t, 0).T.astype(BF)
    return jnp.dot(columns, spread_terms(per_head_t.shape[0]), preferred_element_type=F32)


def exact_nt(v, zero_one):
    rows = v.shape[0]
    parts = nt_dot(terms(v, 0).astype(BF), zero_one.astype(BF))
    return parts[:rows] + parts[rows : 2 * rows] + parts[2 * rows :]


def plan_number(starts, slot_ref):
    crowd = jnp.int32(2)
    for p in range(PROMPTS - 2):
        crowd = jnp.where((starts[p + 1] - 1) // TOK == starts[p + 2] // TOK, 3, crowd)
    crowd = jnp.where((starts[1] - 1) // TOK == starts[3] // TOK, 4, crowd)
    shared = jnp.int32(0)
    for p in range(PROMPTS):
        for q in range(p):
            one, two = slot_ref[p], slot_ref[q]
            both = (one // SLOTS_HERE == two // SLOTS_HERE) & (one != two)
            shared = jnp.where(both, 1, shared)
    return jnp.where(crowd == 2, shared, jnp.where((crowd == 3) & (shared == 0), 2, 3))


def block_kernel(*refs):
    (
        len_hbm,
        slot_hbm,
        dt_hbm,
        alog_hbm,
        xc_hbm,
        xm_hbm,
        bc_hbm,
        tx_hbm,
        tbc_hbm,
        wx_hbm,
        wbc_hbm,
        prefix_hbm,
    ) = refs[:12]
    out_refs, refs = refs[12 : 12 + len(PLANS)], refs[12 + len(PLANS) :]
    act_ref, within_ref, delta_ref, bc_ref, taps_ref, number_ref = refs[:6]
    (len_ref, slot_ref, dt_ref, alog_ref, xc_ref, xm_ref, tx_ref, tbc_ref, wx_ref) = refs[6:15]
    x_scr, vals_scr, sems = refs[15:]
    rows = PLANS[0].prefix
    ctx = lax.axis_index("ctx")
    heads = dt_ref.shape[0]
    chans = heads * WIDTH
    devices = out_refs[0].shape[0]
    group = lax.axis_index("head") * heads // HEADS_GROUP
    groups = bc_hbm.shape[1] // (2 * STATE)
    b_cols = pl.ds(pl.multiple_of(group * STATE, STATE), STATE)
    c_cols = pl.ds(pl.multiple_of((groups + group) * STATE, STATE), STATE)
    x_cols = pl.ds(pl.multiple_of(ctx * rows // STATE * STATE, STATE), STATE)
    copies = [
        pltpu.make_async_copy(src, dst, sems.at[n])
        for n, (src, dst) in enumerate(
            [
                (len_hbm, len_ref),
                (slot_hbm, slot_ref),
                (dt_hbm, dt_ref),
                (alog_hbm, alog_ref),
                (xc_hbm, xc_ref),
                (xm_hbm, xm_ref),
                (bc_hbm.at[:, b_cols], bc_ref.at[0]),
                (bc_hbm.at[:, c_cols], bc_ref.at[1]),
                (wx_hbm, wx_ref),
                (wbc_hbm.at[:, b_cols], taps_ref.at[1]),
                (wx_hbm.at[:, x_cols], taps_ref.at[0]),
                (wbc_hbm.at[:, c_cols], taps_ref.at[2]),
                (tx_hbm, tx_ref),
                (tbc_hbm.at[:, :, b_cols], tbc_ref.at[0]),
                (tbc_hbm.at[:, :, c_cols], tbc_ref.at[1]),
            ]
        )
    ]
    for copy in copies:
        copy.start()
    copies[0].wait()
    copies[1].wait()
    used = jnp.int32(0)
    for p in range(PROMPTS):
        used = jnp.where(slot_ref[p] // SLOTS_HERE == ctx, slot_ref[p] % SLOTS_HERE, used)
    starts = starts_of(len_ref)
    locs = [s - ctx * TOK for s in starts]
    number = plan_number(starts, slot_ref)
    number_ref[0] = number

    def state_copies(plan, out_ref):
        return [
            pltpu.make_async_copy(
                prefix_hbm.at[used if plan.slots == 1 else s],
                out_ref.at[:, pl.ds(plan.prefix + s * rows, rows), :],
                sems.at[len(copies) + s],
            )
            for s in range(plan.slots)
        ]

    states = state_copies(PLANS[0], out_refs[0])
    for copy in states:
        copy.start()
    for copy in copies[2:]:
        copy.wait()
    scale = jnp.exp2(xc_ref[...].astype(F32)).T.astype(BF)
    wide = jnp.dot(scale, spread(MXB, xc_ref.shape[0]), preferred_element_type=F32)
    x = xm_ref[...].astype(F32) * wide
    b_raw = bc_ref[0].astype(F32)
    x_scr[8:, :chans] = x
    x_scr[8:, chans:] = b_raw
    x_scr[:8, :] = jnp.zeros((8, chans + STATE), F32)

    live = live_matrix(locs)
    delta = softplus(dt_ref[...])
    delta_ref[...] = delta
    log_decay = -jnp.exp(alog_ref[...].T) * delta
    within = exact_nt(log_decay, live)
    within_ref[...] = within
    token = iota((heads, TOK), 1)
    first = row_starts(locs, token)
    last_start = row_starts(locs, jnp.full((heads, TOK), TOK - 1, jnp.int32))
    to_end = delta * jnp.exp(jnp.where(token >= last_start, within[:, TOK - 1 :] - within, FAR))
    regular = (token >= LAGS) & (token - first >= LAGS)
    factor = widen(jnp.where(regular, to_end, 0.0))

    def chosen_rows(modulus, lowest):
        entry = iota((16, TOK), 0)
        begin = jnp.full((16, TOK), -TOK, jnp.int32)
        for p in range(PROMPTS):
            for i in range(LAGS):
                at = locs[p] + i
                inside = (len_ref[p] > i) & (at >= lowest) & (at < TOK)
                begin = jnp.where((entry == p % modulus * LAGS + i) & inside, at, begin)
        return iota((16, TOK), 1) == begin

    at_block = jnp.where((token < LAGS) & (token - first >= LAGS), to_end, 0.0)
    vals = exact_nt(to_end, chosen_rows(PROMPTS, 0))[:, : PROMPTS * LAGS]
    vals = jnp.concatenate(
        [at_block[:, :LAGS], vals, jnp.exp(within[:, TOK - 1 :]), jnp.zeros((heads, TOK - 16), F32)], axis=1
    )
    high = vals.astype(BF).astype(F32)
    low = vals - high
    vals_scr[0] = high
    vals_scr[1] = low

    taps = jnp.concatenate([wx_ref[...], taps_ref[1]], axis=1)
    conv = taps[LAGS : LAGS + 1] * x_scr[8:, :]
    for k in range(1, LAGS + 1):
        conv = conv + taps[LAGS - k : LAGS - k + 1] * x_scr[8 - k : 8 + TOK - k, :]
    act = silu(conv).astype(BF)
    act_ref[...] = act[:, :chans]
    inputs = (act[:, :chans].astype(F32) * factor).astype(BF)
    ends = lax.dot_general(
        inputs, act[:, chans:], (((0,), (0,)), ((), ())), preferred_element_type=F32
    ).astype(BF)
    for k in range(devices):
        out_refs[0][k, :rows, :] = ends[k * rows : (k + 1) * rows]

    def finish(plan, out_ref, x, b_raw, high, low):
        raw = jnp.concatenate([x, b_raw], axis=1).astype(BF)
        at_start = jnp.dot(chosen_rows(plan.begun, LAGS).astype(BF), raw, preferred_element_type=F32)
        at_start = at_start[: plan.begun * LAGS]
        tails_x, tails_b, tails_c = [], [], []
        for s in range(plan.slots):
            for i in range(LAGS):
                for found, two in ((tails_x, tx_ref[i]), (tails_b, tbc_ref[0, i]), (tails_c, tbc_ref[1, i])):
                    two = two.astype(F32)
                    found.append(jnp.where(used == 1, two[1:], two[:1]) if plan.slots == 1 else two[s : s + 1])
        tails = jnp.concatenate(tails_x, axis=0)
        c_last = bc_ref[1].astype(F32)[TOK - LAGS :]
        b_tile = jnp.concatenate([b_raw[:LAGS], c_last[:2], b_raw[TOK - LAGS :]], axis=0)
        foot = [at_start[:, chans:]] + tails_b + tails_c + [c_last[2:]]
        if plan.rows > plan.used:
            foot.append(jnp.zeros((plan.rows - plan.used, STATE), F32))
        foot = jnp.concatenate(foot, axis=0)
        gap = jnp.zeros((2, STATE), F32)
        tile_row = iota((8, STATE), 0)
        for c in range(chans // STATE):
            lanes = slice(c * STATE, (c + 1) * STATE)
            x_tile = jnp.concatenate([x[:LAGS, lanes], gap, x[TOK - LAGS :, lanes]], axis=0)
            part = jnp.concatenate([b_tile, at_start[:, lanes], tails[:, lanes], foot], axis=0).astype(BF)
            for k in range(c * STATE // rows, (c + 1) * STATE // rows):
                h = k * rows // WIDTH
                tile = jnp.where(tile_row == LAGS, high[h : h + 1], x_tile)
                tile = jnp.where(tile_row == LAGS + 1, low[h : h + 1], tile)
                out_ref[k, plan.xb : plan.bb, :] = tile.astype(BF)
                out_ref[k, plan.bb :, :] = part

    finish(PLANS[0], out_refs[0], x, b_raw, high, low)
    for copy in states:
        copy.wait()

    @pl.when(number > 0)
    def _():
        for n, plan in list(enumerate(PLANS))[1:]:

            @pl.when(number == n)
            def _():
                own = state_copies(plan, out_refs[n])
                for copy in own:
                    copy.start()
                out_refs[n][:, :rows, :] = out_refs[0][:, :rows, :]
                finish(plan, out_refs[n], x_scr[8:, :chans], x_scr[8:, chans:], vals_scr[0], vals_scr[1])
                for copy in own:
                    copy.wait()


def tail_of(plan, got_ref, slot, tail_at):
    owner = got_ref[slot // SLOTS_HERE, plan.xb :, :].astype(F32)
    place = tail_at - plan.xb
    tail = owner[place : place + LAGS]
    if plan.slots > 1:
        tail = jnp.where(slot % SLOTS_HERE == 1, owner[place + LAGS : place + 2 * LAGS], tail)
    return tail


def scan_kernel(plan, len_ref, slot_ref, got_ref, taps_ref, out_ref, x_scr, b_scr, in_scr, mix_scr):
    devices = got_ref.shape[0]
    rows = plan.prefix
    ctx = lax.axis_index("ctx")
    at = ctx * rows % STATE
    starts = starts_of(len_ref)
    blocks = [s // TOK for s in starts]

    x_scr[...] = got_ref[:, plan.xb : plan.xb + 8, :].astype(F32).reshape(devices * 8, STATE)
    b_scr[...] = got_ref[:, plan.bb : plan.bb + 8, :].astype(F32).reshape(devices * 8, STATE)
    factors = x_scr[pl.ds(LAGS, devices, stride=8), :] + x_scr[pl.ds(LAGS + 1, devices, stride=8), :]
    prompt_factors = jnp.sum(factors, axis=0, keepdims=True)

    def windows(scr, start_at, tail_at):
        before, now = [], []
        for p in range(PROMPTS):
            own = got_ref[blocks[p], plan.xb :, :].astype(F32)
            place = start_at - plan.xb + p % plan.begun * LAGS
            found = []
            for i in range(LAGS):
                row = (starts[p] + i) % TOK
                block = jnp.minimum((starts[p] + i) // TOK, devices - 1)
                early = scr[pl.ds(8 * block + jnp.minimum(row, LAGS - 1), 1), :]
                found.append(jnp.where(row < LAGS, early, own[place + i : place + i + 1]))
            now.append(found)
            before.append(tail_of(plan, got_ref, slot_ref[p], tail_at))
        pad = jnp.zeros((WINDOWS - devices - PROMPTS, STATE), F32)
        found = []
        for i in range(LAGS):
            last = scr[pl.ds(8 - LAGS + i, devices, stride=8), :]
            last = jnp.concatenate([last[devices - 1 :], last[: devices - 1]], axis=0)
            found.append(jnp.concatenate([last] + [b[i : i + 1] for b in before] + [pad], axis=0))
        for i in range(LAGS):
            fresh = scr[pl.ds(i, devices, stride=8), :]
            found.append(jnp.concatenate([fresh] + [n[i] for n in now] + [pad], axis=0))
        return found

    def activation(rows6, taps, i):
        conv = taps[LAGS : LAGS + 1] * rows6[LAGS + i]
        for k in range(1, LAGS + 1):
            conv = conv + taps[LAGS - k : LAGS - k + 1] * rows6[LAGS + i - k]
        return silu(conv).astype(BF).astype(F32)

    x_rows = windows(x_scr, plan.xp, plan.xt)
    b_rows = windows(b_scr, plan.bp, plan.bt)
    x_act = [activation(x_rows, taps_ref[0], i) for i in range(LAGS)]
    b_act = [activation(b_rows, taps_ref[1], i) for i in range(LAGS)]
    scaled = []
    for i in range(LAGS):
        column = [factors[:, i : i + 1]]
        for p in range(PROMPTS):
            lane = LAGS + p * LAGS + i
            column.append(prompt_factors[:, lane : lane + 1])
        column.append(jnp.zeros((WINDOWS - devices - PROMPTS, 1), F32))
        scaled.append(x_act[i] * jnp.concatenate(column, axis=0))
    spare = jnp.zeros((STATE - LAGS * WINDOWS, STATE), F32)
    in_scr[...] = jnp.concatenate(scaled + [spare], axis=0).T
    mine = in_scr[pl.ds(pl.multiple_of(at, rows), rows), :]
    lane = iota((rows, STATE), 1)
    target = lane % WINDOWS
    for p in range(PROMPTS):
        for i in range(LAGS):
            target = jnp.where(lane == i * WINDOWS + devices + p, (starts[p] + i) // TOK, target)
    for d in range(devices):
        mix_scr[d * rows : (d + 1) * rows, :] = jnp.where(target == d, mine, 0.0).astype(BF)
    b_all = jnp.concatenate(b_act + [spare], axis=0).astype(BF)
    extra = jnp.dot(mix_scr[...], b_all, preferred_element_type=F32)

    turn = at // rows
    from_prompts = jnp.where(
        turn == 0, x_act[0][devices:], jnp.where(turn == 1, x_act[1][devices:], x_act[2][devices:])
    )
    pad = jnp.zeros((8 - LAGS, STATE), F32)

    prefixes = []
    for p in range(PROMPTS):
        slot = slot_ref[p]
        place = plan.prefix
        if plan.slots > 1:
            place = pl.multiple_of(place + (slot % SLOTS_HERE) * rows, rows)
        prefixes.append(got_ref[slot // SLOTS_HERE, pl.ds(place, rows), :])
    wide = [piece.astype(F32) for piece in prefixes]
    state = jnp.zeros((rows, STATE), F32)
    states = plan.prompts * rows
    for d in range(devices):
        out_ref[d, :rows, :] = state.astype(BF)
        out_ref[d, rows:states, :] = jnp.zeros((states - rows, STATE), BF)
        from_block = jnp.concatenate([x_act[i][d : d + 1] for i in range(LAGS)] + [pad], axis=0)
        out_ref[d, states:, :] = jnp.where(turn == LAGS, from_block, from_prompts).astype(BF)
        base = state
        for p in range(PROMPTS):
            base = jnp.where(blocks[p] == d, wide[p], base)
        decay = factors[d : d + 1, DECAY_LANE : DECAY_LANE + 1]
        state = decay * base + (got_ref[d, :rows, :].astype(F32) + extra[d * rows : (d + 1) * rows])
    for p in range(PROMPTS):
        place = jnp.int32(0)
        for q in range(p + 1):
            place = place + (starts[q] > blocks[p] * TOK).astype(jnp.int32)
        place = jnp.minimum(place, plan.prompts - 1)
        out_ref[blocks[p], pl.ds(pl.multiple_of(place * rows, rows), rows), :] = prefixes[p]


def read_kernel(
    plan,
    len_ref,
    slot_ref,
    sent_ref,
    got_ref,
    act_ref,
    bc_ref,
    taps_ref,
    within_ref,
    delta_ref,
    skip_ref,
    gate_ref,
    gated_ref,
    sq_ref,
    bc_scr,
):
    ctx = lax.axis_index("ctx")
    devices = got_ref.shape[0]
    heads = delta_ref.shape[0]
    chans = heads * WIDTH
    rows = chans // devices
    locs = [s - ctx * TOK for s in starts_of(len_ref)]

    token = iota((TOK, 16), 0)
    entry = iota((TOK, 16), 1)
    first = row_starts(locs, token)
    prompt = sum((token >= loc).astype(jnp.int32) for loc in locs) - 1

    bc_scr[8:, :] = jnp.concatenate([bc_ref[0], bc_ref[1]], axis=1).astype(F32)
    before = sent_ref[(ctx + devices - 1) % devices, plan.bb :, :].astype(F32)
    bc_scr[8 - LAGS : 8, :STATE] = before[8 - LAGS : 8]
    c_last = plan.cp - plan.bb
    bc_scr[8 - LAGS : 8, STATE:] = jnp.concatenate([before[LAGS : LAGS + 2], before[c_last : c_last + 1]], axis=0)
    tails = []
    for p in range(PROMPTS):
        pair = [tail_of(plan, sent_ref, slot_ref[p], at) for at in (plan.bt, plan.ct)]
        tails.append(jnp.concatenate(pair, axis=1))
    tails.append(jnp.zeros((16 - PROMPTS * LAGS, 2 * STATE), F32))
    tails = jnp.concatenate(tails, axis=0).astype(BF)
    taps = jnp.concatenate([taps_ref[1], taps_ref[2]], axis=1)
    conv = taps[LAGS : LAGS + 1] * bc_scr[8:, :]
    for k in range(1, LAGS + 1):
        outside = token - k < first
        pick = outside & (entry == prompt * LAGS + token - k - first + LAGS)
        tail_rows = jnp.dot(pick.astype(BF), tails, preferred_element_type=F32)
        value = jnp.where(outside[:, :1], tail_rows, bc_scr[8 - k : 8 + TOK - k, :])
        conv = conv + taps[LAGS - k : LAGS - k + 1] * value
    bc_act = silu(conv).astype(BF)
    b_act, c_act = bc_act[:, :STATE], bc_act[:, STATE:]

    near = token - first < LAGS
    by_prompt = (prompt == entry % PROMPTS) & (token - first == entry // PROMPTS) & near
    by_block = (token == entry - LAGS * PROMPTS) & (token < LAGS) & jnp.logical_not(near)
    pick = by_prompt | by_block
    other = (near | (token < LAGS))[:, :1]
    per = STATE // rows
    states = plan.prompts * rows
    spec = []
    for c in range(chans // STATE):
        spec.append(
            jnp.concatenate(
                [got_ref[c * per + j, states:, :].astype(F32)[:PROMPTS] for j in range(per)], axis=0
            )
        )
    spec = jnp.concatenate(spec, axis=1).astype(BF)
    patch = jnp.dot(pick.astype(BF), spec, preferred_element_type=F32)
    x_wide = jnp.where(other, patch, act_ref[...].astype(F32))

    live = live_matrix(locs)
    delta = delta_ref[...]
    within = within_ref[...]
    within_c = within.T
    scores = nt_dot(c_act, b_act)
    place = iota((TOK, STATE), 0)
    place = sum(((loc > 0) & (place >= loc)).astype(jnp.int32) for loc in locs)
    c_wide = c_act.astype(F32)
    reads = jnp.zeros((TOK, chans), F32)
    for j in range(plan.prompts):
        state = got_ref[:, j * rows : (j + 1) * rows, :].reshape(chans, STATE)
        reads = reads + nt_dot(jnp.where(place == j, c_wide, 0.0).astype(BF), state)
    y = widen(jnp.exp(within)) * reads
    skip = jnp.dot(terms(skip_ref[...], 1).astype(BF), spread_terms(heads), preferred_element_type=F32)
    left = iota((TOK, 2 * WIDTH), 1) < WIDTH
    part = jnp.zeros((TOK, TOK), F32)
    for j in range(heads // 2):
        pair = []
        for h in (2 * j, 2 * j + 1):
            fade = jnp.exp(jnp.where(live, within_c[:, h : h + 1] - within[h : h + 1, :], FAR))
            pair.append((scores * fade * delta[h : h + 1, :]).astype(BF))
        at = slice(2 * j * WIDTH, 2 * (j + 1) * WIDTH)
        x_pair = x_wide[:, at]
        both = jnp.concatenate([jnp.where(left, x_pair, 0.0), jnp.where(left, 0.0, x_pair)], axis=0)
        intra = jnp.dot(jnp.concatenate(pair, axis=1), both.astype(BF), preferred_element_type=F32)
        total = y[:, at] + (intra + skip[:, at] * x_pair)
        gated = total * silu(gate_ref[:, at].astype(F32))
        gated_ref[:, at] = gated
        part = part + gated * gated
    sq_ref[...] = jnp.sum(part.T, axis=0, keepdims=True)


def norm_kernel(gated_ref, sq_ref, gain_ref, out_hbm, out_scr, sems):
    inverse = lax.rsqrt(sq_ref[...] / (HEADS_GROUP * WIDTH) + EPS)
    inverse = jnp.broadcast_to(inverse, (TOK, TOK)).T
    rows = TOK // NORM_PARTS
    copies = []
    for part in range(NORM_PARTS):
        at = slice(part * rows, (part + 1) * rows)
        for c in range(out_scr.shape[1] // TOK):
            cols = slice(c * TOK, (c + 1) * TOK)
            out_scr[at, cols] = (gated_ref[at, cols] * inverse[at] * gain_ref[:, cols]).astype(BF)
        copies.append(pltpu.make_async_copy(out_scr.at[at], out_hbm.at[at], sems.at[part]))
        copies[-1].start()
    for copy in copies:
        copy.wait()


def on_device(
    x_mant,
    x_codes,
    bc_raw,
    gate_z,
    conv_x,
    conv_bc,
    dt_raw,
    a_log,
    d_skip,
    norm_gain,
    prompt_lengths,
    cache_slot,
    prefix_state,
    tail_x,
    tail_bc,
):
    devices = lax.axis_size("ctx")
    head_devices = lax.axis_size("head")
    heads = a_log.shape[0]
    chans = heads * WIDTH
    rows = chans // devices
    dt_t = dt_raw.T
    a_row = a_log.reshape(1, heads)
    skip_row = d_skip.reshape(1, heads)
    tail_x = jnp.transpose(tail_x, (1, 0, 2))
    tail_bc = jnp.transpose(tail_bc, (1, 0, 2))
    prefixes = prefix_state.reshape(SLOTS_HERE, devices, rows, STATE)

    sources = [
        prompt_lengths,
        cache_slot,
        dt_t,
        a_row,
        x_codes.T,
        x_mant,
        bc_raw,
        tail_x,
        tail_bc,
        conv_x,
        conv_bc,
    ]
    found = call(
        block_kernel,
        tuple(jax.ShapeDtypeStruct((devices, plan.rows, STATE), BF) for plan in PLANS)
        + (
            jax.ShapeDtypeStruct((TOK, chans), BF),
            jax.ShapeDtypeStruct((heads, TOK), F32),
            jax.ShapeDtypeStruct((heads, TOK), F32),
            jax.ShapeDtypeStruct((2, TOK, STATE), BF),
            jax.ShapeDtypeStruct((3, conv_x.shape[0], STATE), F32),
            jax.ShapeDtypeStruct((1,), jnp.int32),
        ),
        in_specs=[hbm()] * 12,
        out_specs=(vmem(),) * (5 + len(PLANS)) + (smem(),),
        scratch_shapes=[pltpu.SMEM((PROMPTS,), jnp.int32)] * 2
        + [pltpu.VMEM(source.shape, source.dtype) for source in sources[2:6]]
        + [
            pltpu.VMEM(tail_x.shape, BF),
            pltpu.VMEM((2,) + tail_x.shape[:2] + (STATE,), BF),
            pltpu.VMEM(conv_x.shape, F32),
            pltpu.VMEM((TOK + 8, chans + STATE), F32),
            pltpu.VMEM((2, heads, STATE), F32),
            pltpu.SemaphoreType.DMA((15 + SLOTS_HERE,)),
        ],
    )(*[pinned(source) for source in sources + [prefixes]])
    messages, rest, number = found[: len(PLANS)], found[len(PLANS) : -1], found[-1]

    def second_part(plan, send1, act, within, delta, bc_here, taps):
        got1 = lax.all_to_all(send1, "ctx", 0, 0)
        send2 = call(
            functools.partial(scan_kernel, plan),
            jax.ShapeDtypeStruct((devices, plan.prompts * rows + 8, STATE), BF),
            in_specs=[smem(), smem()] + [vmem()] * 2,
            out_specs=vmem(),
            scratch_shapes=[
                pltpu.VMEM((devices * 8, STATE), F32),
                pltpu.VMEM((devices * 8, STATE), F32),
                pltpu.VMEM((STATE, STATE), F32),
                pltpu.VMEM((chans, STATE), BF),
            ],
        )(prompt_lengths, cache_slot, got1, taps)
        got2 = lax.all_to_all(send2, "ctx", 0, 0)
        return call(
            functools.partial(read_kernel, plan),
            (jax.ShapeDtypeStruct((TOK, chans), F32), jax.ShapeDtypeStruct((1, TOK), F32)),
            in_specs=[smem(), smem()] + [vmem()] * 9,
            out_specs=(vmem(), vmem()),
            scratch_shapes=[pltpu.VMEM((TOK + 8, 2 * STATE), F32)],
        )(
            prompt_lengths,
            cache_slot,
            got1,
            got2,
            act,
            bc_here,
            taps,
            within,
            delta,
            skip_row,
            gate_z,
        )

    gated, squares = lax.switch(
        number[0],
        [
            lambda plan=plan, message=message: second_part(plan, message, *rest)
            for plan, message in zip(PLANS, messages)
        ],
    )
    pairs = [[i, i + 1] for i in range(0, head_devices, 2)]
    total = lax.psum(squares, "head", axis_index_groups=pairs)
    return call(
        norm_kernel,
        jax.ShapeDtypeStruct((TOK, chans), BF),
        in_specs=[vmem()] * 3,
        out_specs=hbm(),
        scratch_shapes=[pltpu.VMEM((TOK, chans), BF), pltpu.SemaphoreType.DMA((NORM_PARTS,))],
    )(gated, total, norm_gain.reshape(1, chans))


def solution(mesh):
    in_specs = (
        P("ctx", "head"),
        P("ctx", "head"),
        P("ctx", None),
        P("ctx", "head"),
        P(None, "head"),
        P(),
        P("ctx", "head"),
        P("head"),
        P("head"),
        P("head"),
        P(),
        P(),
        P("ctx", "head", None),
        P("ctx", None, "head"),
        P("ctx", None, None),
    )
    out_specs = P("ctx", "head")
    return jax.shard_map(
        on_device, mesh=mesh, in_specs=in_specs, out_specs=out_specs, check_vma=False
    )
```

```python
import functools

import jax
import jax.numpy as jnp
from jax import lax
from jax.experimental import pallas as pl
from jax.experimental.pallas import tpu as pltpu
from jax.sharding import PartitionSpec as P

BF = jnp.bfloat16
F32 = jnp.float32
INTERPRET = False

TOK = 128
WIDTH = 64
STATE = 128
MXB = 32
LAGS = 3
PROMPTS = 4
HEADS_GROUP = 32
SLOTS_HERE = 2
EPS = 1e-05
FAR = -1e30
NORM_PARTS = 4


class Plan:
    def __init__(self, slots, prompts):
        self.slots, self.prompts = slots, prompts
        self.begun = prompts - 1
        at = 32
        self.prefix, at = at, at + 32 * slots
        self.xb, at = at, at + 8
        self.bb, at = at, at + 8
        self.xp, at = at, at + LAGS * self.begun
        self.xt, at = at, at + LAGS * slots
        self.bp, at = at, at + LAGS * self.begun
        self.bt, at = at, at + LAGS * slots
        self.ct, at = at, at + LAGS * slots
        self.cp, at = at, at + 1
        self.used = at
        self.rows = (at + 7) // 8 * 8


PLANS = (Plan(1, 2), Plan(SLOTS_HERE, 2), Plan(1, 3), Plan(SLOTS_HERE, PROMPTS))
DECAY_LANE = LAGS + PROMPTS * LAGS
WINDOWS = 40


def call(kernel, out_shape, **kw):
    return pl.pallas_call(
        kernel,
        out_shape=out_shape,
        interpret=INTERPRET,
        compiler_params=pltpu.CompilerParams(vmem_limit_bytes=48 * 1024 * 1024),
        **kw,
    )


def vmem():
    return pl.BlockSpec(memory_space=pltpu.VMEM)


def hbm():
    return pl.BlockSpec(memory_space=pltpu.HBM)


def pinned(array):
    return array if INTERPRET else pltpu.with_memory_space_constraint(array, pltpu.HBM)


def smem():
    return pl.BlockSpec(memory_space=pltpu.SMEM)


def starts_of(len_ref):
    found = [jnp.int32(0)]
    for p in range(PROMPTS - 1):
        found.append(found[-1] + len_ref[p])
    return found


def iota(shape, axis):
    return lax.broadcasted_iota(jnp.int32, shape, axis)


def row_starts(locs, token):
    first = jnp.full(token.shape, locs[0], jnp.int32)
    for p in range(1, PROMPTS):
        first = jnp.where(token >= locs[p], locs[p], first)
    return first


def softplus(v):
    return jnp.maximum(v, 0.0) + jnp.log1p(jnp.exp(-jnp.abs(v)))


def silu(v):
    half = 0.5 * v
    return half + half * jnp.tanh(half)


def terms(v, axis):
    high = v.astype(BF).astype(F32)
    mid = (v - high).astype(BF).astype(F32)
    return jnp.concatenate([high, mid, v - high - mid], axis=axis)


def spread(per, count):
    shape = (count, count * per)
    return (iota(shape, 1) // per == iota(shape, 0)).astype(BF)


def nt_dot(a, b, **kw):
    return lax.dot_general(a, b, (((1,), (1,)), ((), ())), preferred_element_type=F32, **kw)


def live_matrix(locs):
    row, col = iota((TOK, TOK), 0), iota((TOK, TOK), 1)
    return (col <= row) & (col >= row_starts(locs, row))


def spread_terms(heads):
    shape = (3 * heads, heads * WIDTH)
    return (iota(shape, 1) // WIDTH == iota(shape, 0) % heads).astype(BF)


def widen(per_head_t):
    columns = terms(per_head_t, 0).T.astype(BF)
    return jnp.dot(columns, spread_terms(per_head_t.shape[0]), preferred_element_type=F32)


def exact_nt(v, zero_one):
    rows = v.shape[0]
    parts = nt_dot(terms(v, 0).astype(BF), zero_one.astype(BF))
    return parts[:rows] + parts[rows : 2 * rows] + parts[2 * rows :]


def plan_number(starts, slot_ref):
    crowd = jnp.int32(2)
    for p in range(PROMPTS - 2):
        crowd = jnp.where((starts[p + 1] - 1) // TOK == starts[p + 2] // TOK, 3, crowd)
    crowd = jnp.where((starts[1] - 1) // TOK == starts[3] // TOK, 4, crowd)
    shared = jnp.int32(0)
    for p in range(PROMPTS):
        for q in range(p):
            one, two = slot_ref[p], slot_ref[q]
            both = (one // SLOTS_HERE == two // SLOTS_HERE) & (one != two)
            shared = jnp.where(both, 1, shared)
    return jnp.where(crowd == 2, shared, jnp.where((crowd == 3) & (shared == 0), 2, 3))


def block_kernel(*refs):
    (
        len_hbm,
        slot_hbm,
        dt_hbm,
        alog_hbm,
        xc_hbm,
        xm_hbm,
        bc_hbm,
        tx_hbm,
        tbc_hbm,
        wx_hbm,
        wbc_hbm,
        prefix_hbm,
    ) = refs[:12]
    out_refs, refs = refs[12 : 12 + len(PLANS)], refs[12 + len(PLANS) :]
    act_ref, within_ref, delta_ref, bc_ref, taps_ref, number_hbm = refs[:6]
    (len_ref, slot_ref, dt_ref, alog_ref, xc_ref, xm_ref, tx_ref, tbc_ref, wx_ref) = refs[6:15]
    prefix_ref, x_scr, vals_scr, number_ref, sems = refs[15:]
    rows = PLANS[0].prefix
    ctx = lax.axis_index("ctx")
    heads = dt_ref.shape[0]
    chans = heads * WIDTH
    devices = out_refs[0].shape[0]
    group = lax.axis_index("head") * heads // HEADS_GROUP
    groups = bc_hbm.shape[1] // (2 * STATE)
    b_cols = pl.ds(pl.multiple_of(group * STATE, STATE), STATE)
    c_cols = pl.ds(pl.multiple_of((groups + group) * STATE, STATE), STATE)
    x_cols = pl.ds(pl.multiple_of(ctx * rows // STATE * STATE, STATE), STATE)
    copies = [
        pltpu.make_async_copy(src, dst, sems.at[n])
        for n, (src, dst) in enumerate(
            [
                (len_hbm, len_ref),
                (slot_hbm, slot_ref),
                (dt_hbm, dt_ref),
                (alog_hbm, alog_ref),
                (xc_hbm, xc_ref),
                (xm_hbm, xm_ref),
                (bc_hbm.at[:, b_cols], bc_ref.at[0]),
                (bc_hbm.at[:, c_cols], bc_ref.at[1]),
                (wx_hbm, wx_ref),
                (wbc_hbm.at[:, b_cols], taps_ref.at[1]),
                (wx_hbm.at[:, x_cols], taps_ref.at[0]),
                (wbc_hbm.at[:, c_cols], taps_ref.at[2]),
                (tx_hbm, tx_ref),
                (tbc_hbm.at[:, :, b_cols], tbc_ref.at[0]),
                (tbc_hbm.at[:, :, c_cols], tbc_ref.at[1]),
                (prefix_hbm, prefix_ref),
            ]
        )
    ]
    for copy in copies:
        copy.start()
    copies[0].wait()
    copies[1].wait()
    used = jnp.int32(0)
    for p in range(PROMPTS):
        used = jnp.where(slot_ref[p] // SLOTS_HERE == ctx, slot_ref[p] % SLOTS_HERE, used)
    starts = starts_of(len_ref)
    locs = [s - ctx * TOK for s in starts]
    number = plan_number(starts, slot_ref)
    number_ref[0] = number
    tell = pltpu.make_async_copy(number_ref, number_hbm, sems.at[len(copies)])
    tell.start()

    for copy in copies[2:-1]:
        copy.wait()
    scale = jnp.exp2(xc_ref[...].astype(F32)).T.astype(BF)
    wide = jnp.dot(scale, spread(MXB, xc_ref.shape[0]), preferred_element_type=F32)
    x = xm_ref[...].astype(F32) * wide
    b_raw = bc_ref[0].astype(F32)
    x_scr[8:, :chans] = x
    x_scr[8:, chans:] = b_raw
    x_scr[:8, :] = jnp.zeros((8, chans + STATE), F32)

    live = live_matrix(locs)
    delta = softplus(dt_ref[...])
    delta_ref[...] = delta
    log_decay = -jnp.exp(alog_ref[...].T) * delta
    within = exact_nt(log_decay, live)
    within_ref[...] = within
    token = iota((heads, TOK), 1)
    first = row_starts(locs, token)
    last_start = row_starts(locs, jnp.full((heads, TOK), TOK - 1, jnp.int32))
    to_end = delta * jnp.exp(jnp.where(token >= last_start, within[:, TOK - 1 :] - within, FAR))
    regular = (token >= LAGS) & (token - first >= LAGS)
    factor = widen(jnp.where(regular, to_end, 0.0))

    def chosen_rows(modulus, lowest):
        entry = iota((16, TOK), 0)
        begin = jnp.full((16, TOK), -TOK, jnp.int32)
        for p in range(PROMPTS):
            for i in range(LAGS):
                at = locs[p] + i
                inside = (len_ref[p] > i) & (at >= lowest) & (at < TOK)
                begin = jnp.where((entry == p % modulus * LAGS + i) & inside, at, begin)
        return iota((16, TOK), 1) == begin

    at_block = jnp.where((token < LAGS) & (token - first >= LAGS), to_end, 0.0)
    vals = exact_nt(to_end, chosen_rows(PROMPTS, 0))[:, : PROMPTS * LAGS]
    vals = jnp.concatenate(
        [at_block[:, :LAGS], vals, jnp.exp(within[:, TOK - 1 :]), jnp.zeros((heads, TOK - 16), F32)], axis=1
    )
    high = vals.astype(BF).astype(F32)
    low = vals - high
    vals_scr[0] = high
    vals_scr[1] = low

    taps = jnp.concatenate([wx_ref[...], taps_ref[1]], axis=1)
    conv = taps[LAGS : LAGS + 1] * x_scr[8:, :]
    for k in range(1, LAGS + 1):
        conv = conv + taps[LAGS - k : LAGS - k + 1] * x_scr[8 - k : 8 + TOK - k, :]
    act = silu(conv).astype(BF)
    act_ref[...] = act[:, :chans]
    inputs = (act[:, :chans].astype(F32) * factor).astype(BF)
    ends = lax.dot_general(
        inputs, act[:, chans:], (((0,), (0,)), ((), ())), preferred_element_type=F32
    ).astype(BF)
    for k in range(devices):
        out_refs[0][k, :rows, :] = ends[k * rows : (k + 1) * rows]

    def finish(plan, out_ref, x, b_raw, high, low):
        raw = jnp.concatenate([x, b_raw], axis=1).astype(BF)
        at_start = jnp.dot(chosen_rows(plan.begun, LAGS).astype(BF), raw, preferred_element_type=F32)
        at_start = at_start[: plan.begun * LAGS]
        tails_x, tails_b, tails_c = [], [], []
        for s in range(plan.slots):
            for i in range(LAGS):
                for found, two in ((tails_x, tx_ref[i]), (tails_b, tbc_ref[0, i]), (tails_c, tbc_ref[1, i])):
                    two = two.astype(F32)
                    found.append(jnp.where(used == 1, two[1:], two[:1]) if plan.slots == 1 else two[s : s + 1])
        tails = jnp.concatenate(tails_x, axis=0)
        c_last = bc_ref[1].astype(F32)[TOK - LAGS :]
        b_tile = jnp.concatenate([b_raw[:LAGS], c_last[:2], b_raw[TOK - LAGS :]], axis=0)
        foot = [at_start[:, chans:]] + tails_b + tails_c + [c_last[2:]]
        if plan.rows > plan.used:
            foot.append(jnp.zeros((plan.rows - plan.used, STATE), F32))
        foot = jnp.concatenate(foot, axis=0)
        gap = jnp.zeros((2, STATE), F32)
        tile_row = iota((8, STATE), 0)
        for c in range(chans // STATE):
            lanes = slice(c * STATE, (c + 1) * STATE)
            x_tile = jnp.concatenate([x[:LAGS, lanes], gap, x[TOK - LAGS :, lanes]], axis=0)
            part = jnp.concatenate([b_tile, at_start[:, lanes], tails[:, lanes], foot], axis=0).astype(BF)
            for k in range(c * STATE // rows, (c + 1) * STATE // rows):
                h = k * rows // WIDTH
                tile = jnp.where(tile_row == LAGS, high[h : h + 1], x_tile)
                tile = jnp.where(tile_row == LAGS + 1, low[h : h + 1], tile)
                out_ref[k, plan.xb : plan.bb, :] = tile.astype(BF)
                out_ref[k, plan.bb :, :] = part

    finish(PLANS[0], out_refs[0], x, b_raw, high, low)
    copies[-1].wait()
    out_refs[0][:, rows : 2 * rows, :] = prefix_ref[used]

    tell.wait()

    @pl.when(number > 0)
    def _():
        for n, plan in list(enumerate(PLANS))[1:]:

            @pl.when(number == n)
            def _():
                out_refs[n][:, :rows, :] = out_refs[0][:, :rows, :]
                for s in range(plan.slots):
                    at = plan.prefix + s * rows
                    out_refs[n][:, at : at + rows, :] = prefix_ref[used if plan.slots == 1 else s]
                finish(plan, out_refs[n], x_scr[8:, :chans], x_scr[8:, chans:], vals_scr[0], vals_scr[1])


def tail_of(plan, got_ref, slot, tail_at):
    owner = got_ref[slot // SLOTS_HERE, plan.xb :, :].astype(F32)
    place = tail_at - plan.xb
    tail = owner[place : place + LAGS]
    if plan.slots > 1:
        tail = jnp.where(slot % SLOTS_HERE == 1, owner[place + LAGS : place + 2 * LAGS], tail)
    return tail


def scan_kernel(plan, len_ref, slot_ref, got_ref, taps_ref, out_ref, x_scr, b_scr, in_scr, mix_scr):
    devices = got_ref.shape[0]
    rows = plan.prefix
    ctx = lax.axis_index("ctx")
    at = ctx * rows % STATE
    starts = starts_of(len_ref)
    blocks = [s // TOK for s in starts]

    x_scr[...] = got_ref[:, plan.xb : plan.xb + 8, :].astype(F32).reshape(devices * 8, STATE)
    b_scr[...] = got_ref[:, plan.bb : plan.bb + 8, :].astype(F32).reshape(devices * 8, STATE)
    factors = x_scr[pl.ds(LAGS, devices, stride=8), :] + x_scr[pl.ds(LAGS + 1, devices, stride=8), :]
    prompt_factors = jnp.sum(factors, axis=0, keepdims=True)

    def windows(scr, start_at, tail_at):
        before, now = [], []
        for p in range(PROMPTS):
            own = got_ref[blocks[p], plan.xb :, :].astype(F32)
            place = start_at - plan.xb + p % plan.begun * LAGS
            found = []
            for i in range(LAGS):
                row = (starts[p] + i) % TOK
                block = jnp.minimum((starts[p] + i) // TOK, devices - 1)
                early = scr[pl.ds(8 * block + jnp.minimum(row, LAGS - 1), 1), :]
                found.append(jnp.where(row < LAGS, early, own[place + i : place + i + 1]))
            now.append(found)
            before.append(tail_of(plan, got_ref, slot_ref[p], tail_at))
        pad = jnp.zeros((WINDOWS - devices - PROMPTS, STATE), F32)
        found = []
        for i in range(LAGS):
            last = scr[pl.ds(8 - LAGS + i, devices, stride=8), :]
            last = jnp.concatenate([last[devices - 1 :], last[: devices - 1]], axis=0)
            found.append(jnp.concatenate([last] + [b[i : i + 1] for b in before] + [pad], axis=0))
        for i in range(LAGS):
            fresh = scr[pl.ds(i, devices, stride=8), :]
            found.append(jnp.concatenate([fresh] + [n[i] for n in now] + [pad], axis=0))
        return found

    def activation(rows6, taps, i):
        conv = taps[LAGS : LAGS + 1] * rows6[LAGS + i]
        for k in range(1, LAGS + 1):
            conv = conv + taps[LAGS - k : LAGS - k + 1] * rows6[LAGS + i - k]
        return silu(conv).astype(BF).astype(F32)

    x_rows = windows(x_scr, plan.xp, plan.xt)
    b_rows = windows(b_scr, plan.bp, plan.bt)
    x_act = [activation(x_rows, taps_ref[0], i) for i in range(LAGS)]
    b_act = [activation(b_rows, taps_ref[1], i) for i in range(LAGS)]
    scaled = []
    for i in range(LAGS):
        column = [factors[:, i : i + 1]]
        for p in range(PROMPTS):
            lane = LAGS + p * LAGS + i
            column.append(prompt_factors[:, lane : lane + 1])
        column.append(jnp.zeros((WINDOWS - devices - PROMPTS, 1), F32))
        scaled.append(x_act[i] * jnp.concatenate(column, axis=0))
    spare = jnp.zeros((STATE - LAGS * WINDOWS, STATE), F32)
    in_scr[...] = jnp.concatenate(scaled + [spare], axis=0).T
    mine = in_scr[pl.ds(pl.multiple_of(at, rows), rows), :]
    lane = iota((rows, STATE), 1)
    target = lane % WINDOWS
    for p in range(PROMPTS):
        for i in range(LAGS):
            target = jnp.where(lane == i * WINDOWS + devices + p, (starts[p] + i) // TOK, target)
    for d in range(devices):
        mix_scr[d * rows : (d + 1) * rows, :] = jnp.where(target == d, mine, 0.0).astype(BF)
    b_all = jnp.concatenate(b_act + [spare], axis=0).astype(BF)
    extra = jnp.dot(mix_scr[...], b_all, preferred_element_type=F32)

    turn = at // rows
    from_prompts = jnp.where(
        turn == 0, x_act[0][devices:], jnp.where(turn == 1, x_act[1][devices:], x_act[2][devices:])
    )
    pad = jnp.zeros((8 - LAGS, STATE), F32)

    prefixes = []
    for p in range(PROMPTS):
        slot = slot_ref[p]
        place = plan.prefix
        if plan.slots > 1:
            place = pl.multiple_of(place + (slot % SLOTS_HERE) * rows, rows)
        prefixes.append(got_ref[slot // SLOTS_HERE, pl.ds(place, rows), :])
    wide = [piece.astype(F32) for piece in prefixes]
    state = jnp.zeros((rows, STATE), F32)
    states = plan.prompts * rows
    for d in range(devices):
        out_ref[d, :rows, :] = state.astype(BF)
        out_ref[d, rows:states, :] = jnp.zeros((states - rows, STATE), BF)
        from_block = jnp.concatenate([x_act[i][d : d + 1] for i in range(LAGS)] + [pad], axis=0)
        out_ref[d, states:, :] = jnp.where(turn == LAGS, from_block, from_prompts).astype(BF)
        base = state
        for p in range(PROMPTS):
            base = jnp.where(blocks[p] == d, wide[p], base)
        decay = factors[d : d + 1, DECAY_LANE : DECAY_LANE + 1]
        state = decay * base + (got_ref[d, :rows, :].astype(F32) + extra[d * rows : (d + 1) * rows])
    for p in range(PROMPTS):
        place = jnp.int32(0)
        for q in range(p + 1):
            place = place + (starts[q] > blocks[p] * TOK).astype(jnp.int32)
        place = jnp.minimum(place, plan.prompts - 1)
        out_ref[blocks[p], pl.ds(pl.multiple_of(place * rows, rows), rows), :] = prefixes[p]


def read_kernel(
    plan,
    len_ref,
    slot_ref,
    sent_ref,
    got_ref,
    act_ref,
    bc_ref,
    taps_ref,
    within_ref,
    delta_ref,
    skip_ref,
    gate_ref,
    gated_ref,
    sq_ref,
    bc_scr,
):
    ctx = lax.axis_index("ctx")
    devices = got_ref.shape[0]
    heads = delta_ref.shape[0]
    chans = heads * WIDTH
    rows = chans // devices
    locs = [s - ctx * TOK for s in starts_of(len_ref)]

    token = iota((TOK, 16), 0)
    entry = iota((TOK, 16), 1)
    first = row_starts(locs, token)
    prompt = sum((token >= loc).astype(jnp.int32) for loc in locs) - 1

    bc_scr[8:, :] = jnp.concatenate([bc_ref[0], bc_ref[1]], axis=1).astype(F32)
    before = sent_ref[(ctx + devices - 1) % devices, plan.bb :, :].astype(F32)
    bc_scr[8 - LAGS : 8, :STATE] = before[8 - LAGS : 8]
    c_last = plan.cp - plan.bb
    bc_scr[8 - LAGS : 8, STATE:] = jnp.concatenate([before[LAGS : LAGS + 2], before[c_last : c_last + 1]], axis=0)
    tails = []
    for p in range(PROMPTS):
        pair = [tail_of(plan, sent_ref, slot_ref[p], at) for at in (plan.bt, plan.ct)]
        tails.append(jnp.concatenate(pair, axis=1))
    tails.append(jnp.zeros((16 - PROMPTS * LAGS, 2 * STATE), F32))
    tails = jnp.concatenate(tails, axis=0).astype(BF)
    taps = jnp.concatenate([taps_ref[1], taps_ref[2]], axis=1)
    conv = taps[LAGS : LAGS + 1] * bc_scr[8:, :]
    for k in range(1, LAGS + 1):
        outside = token - k < first
        pick = outside & (entry == prompt * LAGS + token - k - first + LAGS)
        tail_rows = jnp.dot(pick.astype(BF), tails, preferred_element_type=F32)
        value = jnp.where(outside[:, :1], tail_rows, bc_scr[8 - k : 8 + TOK - k, :])
        conv = conv + taps[LAGS - k : LAGS - k + 1] * value
    bc_act = silu(conv).astype(BF)
    b_act, c_act = bc_act[:, :STATE], bc_act[:, STATE:]

    near = token - first < LAGS
    by_prompt = (prompt == entry % PROMPTS) & (token - first == entry // PROMPTS) & near
    by_block = (token == entry - LAGS * PROMPTS) & (token < LAGS) & jnp.logical_not(near)
    pick = by_prompt | by_block
    other = (near | (token < LAGS))[:, :1]
    per = STATE // rows
    states = plan.prompts * rows
    spec = []
    for c in range(chans // STATE):
        spec.append(
            jnp.concatenate(
                [got_ref[c * per + j, states:, :].astype(F32)[:PROMPTS] for j in range(per)], axis=0
            )
        )
    spec = jnp.concatenate(spec, axis=1).astype(BF)
    patch = jnp.dot(pick.astype(BF), spec, preferred_element_type=F32)
    x_wide = jnp.where(other, patch, act_ref[...].astype(F32))

    live = live_matrix(locs)
    delta = delta_ref[...]
    within = within_ref[...]
    within_c = within.T
    scores = nt_dot(c_act, b_act)
    place = iota((TOK, STATE), 0)
    place = sum(((loc > 0) & (place >= loc)).astype(jnp.int32) for loc in locs)
    c_wide = c_act.astype(F32)
    reads = jnp.zeros((TOK, chans), F32)
    for j in range(plan.prompts):
        state = got_ref[:, j * rows : (j + 1) * rows, :].reshape(chans, STATE)
        reads = reads + nt_dot(jnp.where(place == j, c_wide, 0.0).astype(BF), state)
    y = widen(jnp.exp(within)) * reads
    skip = jnp.dot(terms(skip_ref[...], 1).astype(BF), spread_terms(heads), preferred_element_type=F32)
    left = iota((TOK, 2 * WIDTH), 1) < WIDTH
    part = jnp.zeros((TOK, TOK), F32)
    for j in range(heads // 2):
        pair = []
        for h in (2 * j, 2 * j + 1):
            fade = jnp.exp(jnp.where(live, within_c[:, h : h + 1] - within[h : h + 1, :], FAR))
            pair.append((scores * fade * delta[h : h + 1, :]).astype(BF))
        at = slice(2 * j * WIDTH, 2 * (j + 1) * WIDTH)
        x_pair = x_wide[:, at]
        both = jnp.concatenate([jnp.where(left, x_pair, 0.0), jnp.where(left, 0.0, x_pair)], axis=0)
        intra = jnp.dot(jnp.concatenate(pair, axis=1), both.astype(BF), preferred_element_type=F32)
        total = y[:, at] + (intra + skip[:, at] * x_pair)
        gated = total * silu(gate_ref[:, at].astype(F32))
        gated_ref[:, at] = gated
        part = part + gated * gated
    sq_ref[...] = jnp.sum(part.T, axis=0, keepdims=True)


def norm_kernel(gated_ref, sq_ref, gain_ref, out_hbm, out_scr, sems):
    inverse = lax.rsqrt((sq_ref[0] + sq_ref[1]) / (HEADS_GROUP * WIDTH) + EPS)
    inverse = jnp.broadcast_to(inverse, (TOK, TOK)).T
    rows = TOK // NORM_PARTS
    copies = []
    for part in range(NORM_PARTS):
        at = slice(part * rows, (part + 1) * rows)
        for c in range(out_scr.shape[1] // TOK):
            cols = slice(c * TOK, (c + 1) * TOK)
            out_scr[at, cols] = (gated_ref[at, cols] * inverse[at] * gain_ref[:, cols]).astype(BF)
        copies.append(pltpu.make_async_copy(out_scr.at[at], out_hbm.at[at], sems.at[part]))
        copies[-1].start()
    for copy in copies:
        copy.wait()


def on_device(
    x_mant,
    x_codes,
    bc_raw,
    gate_z,
    conv_x,
    conv_bc,
    dt_raw,
    a_log,
    d_skip,
    norm_gain,
    prompt_lengths,
    cache_slot,
    prefix_state,
    tail_x,
    tail_bc,
):
    devices = lax.axis_size("ctx")
    head_devices = lax.axis_size("head")
    heads = a_log.shape[0]
    chans = heads * WIDTH
    rows = chans // devices
    dt_t = dt_raw.T
    a_row = a_log.reshape(1, heads)
    skip_row = d_skip.reshape(1, heads)
    tail_x = jnp.transpose(tail_x, (1, 0, 2))
    tail_bc = jnp.transpose(tail_bc, (1, 0, 2))
    prefixes = prefix_state.reshape(SLOTS_HERE, devices, rows, STATE)

    sources = [
        prompt_lengths,
        cache_slot,
        dt_t,
        a_row,
        x_codes.T,
        x_mant,
        bc_raw,
        tail_x,
        tail_bc,
        conv_x,
        conv_bc,
    ]
    found = call(
        block_kernel,
        tuple(jax.ShapeDtypeStruct((devices, plan.rows, STATE), BF) for plan in PLANS)
        + (
            jax.ShapeDtypeStruct((TOK, chans), BF),
            jax.ShapeDtypeStruct((heads, TOK), F32),
            jax.ShapeDtypeStruct((heads, TOK), F32),
            jax.ShapeDtypeStruct((2, TOK, STATE), BF),
            jax.ShapeDtypeStruct((3, conv_x.shape[0], STATE), F32),
            jax.ShapeDtypeStruct((1,), jnp.int32),
        ),
        in_specs=[hbm()] * 12,
        out_specs=(vmem(),) * (5 + len(PLANS)) + (hbm(),),
        scratch_shapes=[pltpu.SMEM((PROMPTS,), jnp.int32)] * 2
        + [pltpu.VMEM(source.shape, source.dtype) for source in sources[2:6]]
        + [
            pltpu.VMEM(tail_x.shape, BF),
            pltpu.VMEM((2,) + tail_x.shape[:2] + (STATE,), BF),
            pltpu.VMEM(conv_x.shape, F32),
            pltpu.VMEM(prefixes.shape, BF),
            pltpu.VMEM((TOK + 8, chans + STATE), F32),
            pltpu.VMEM((2, heads, STATE), F32),
            pltpu.SMEM((1,), jnp.int32),
            pltpu.SemaphoreType.DMA((17,)),
        ],
    )(*[pinned(source) for source in sources + [prefixes]])
    messages, rest, number = found[: len(PLANS)], found[len(PLANS) : -1], found[-1]

    def second_part(plan, send1, act, within, delta, bc_here, taps):
        got1 = lax.all_to_all(send1, "ctx", 0, 0)
        send2 = call(
            functools.partial(scan_kernel, plan),
            jax.ShapeDtypeStruct((devices, plan.prompts * rows + 8, STATE), BF),
            in_specs=[smem(), smem()] + [vmem()] * 2,
            out_specs=vmem(),
            scratch_shapes=[
                pltpu.VMEM((devices * 8, STATE), F32),
                pltpu.VMEM((devices * 8, STATE), F32),
                pltpu.VMEM((STATE, STATE), F32),
                pltpu.VMEM((chans, STATE), BF),
            ],
        )(prompt_lengths, cache_slot, got1, taps)
        got2 = lax.all_to_all(send2, "ctx", 0, 0)
        return call(
            functools.partial(read_kernel, plan),
            (jax.ShapeDtypeStruct((TOK, chans), F32), jax.ShapeDtypeStruct((1, TOK), F32)),
            in_specs=[smem(), smem()] + [vmem()] * 9,
            out_specs=(vmem(), vmem()),
            scratch_shapes=[pltpu.VMEM((TOK + 8, 2 * STATE), F32)],
        )(
            prompt_lengths,
            cache_slot,
            got1,
            got2,
            act,
            bc_here,
            taps,
            within,
            delta,
            skip_row,
            gate_z,
        )

    gated, squares = lax.switch(
        number[0],
        [
            lambda plan=plan, message=message: second_part(plan, message, *rest)
            for plan, message in zip(PLANS, messages)
        ],
    )
    pairs = [[i, i + 1] for i in range(0, head_devices, 2)]
    both = lax.all_gather(squares, "head", axis_index_groups=pairs)
    return call(
        norm_kernel,
        jax.ShapeDtypeStruct((TOK, chans), BF),
        in_specs=[vmem()] * 3,
        out_specs=hbm(),
        scratch_shapes=[pltpu.VMEM((TOK, chans), BF), pltpu.SemaphoreType.DMA((NORM_PARTS,))],
    )(gated, both, norm_gain.reshape(1, chans))


def solution(mesh):
    in_specs = (
        P("ctx", "head"),
        P("ctx", "head"),
        P("ctx", None),
        P("ctx", "head"),
        P(None, "head"),
        P(),
        P("ctx", "head"),
        P("head"),
        P("head"),
        P("head"),
        P(),
        P(),
        P("ctx", "head", None),
        P("ctx", None, "head"),
        P("ctx", None, None),
    )
    out_specs = P("ctx", "head")
    return jax.shard_map(
        on_device, mesh=mesh, in_specs=in_specs, out_specs=out_specs, check_vma=False
    )
```

```python
import functools

import jax
import jax.numpy as jnp
from jax import lax
from jax.experimental import pallas as pl
from jax.experimental.pallas import tpu as pltpu
from jax.sharding import PartitionSpec as P

BF = jnp.bfloat16
F32 = jnp.float32
INTERPRET = False

TOK = 128
WIDTH = 64
STATE = 128
MXB = 32
LAGS = 3
PROMPTS = 4
HEADS_GROUP = 32
SLOTS_HERE = 2
EPS = 1e-05
FAR = -1e30
NORM_PARTS = 4


class Plan:
    def __init__(self, slots, prompts):
        self.slots, self.prompts = slots, prompts
        self.begun = prompts - 1
        at = 32
        self.prefix, at = at, at + 32 * slots
        self.xb, at = at, at + 8
        self.bb, at = at, at + 8
        self.xp, at = at, at + LAGS * self.begun
        self.xt, at = at, at + LAGS * slots
        self.bp, at = at, at + LAGS * self.begun
        self.bt, at = at, at + LAGS * slots
        self.ct, at = at, at + LAGS * slots
        self.packed = slots > 1
        if not self.packed:
            self.cp, at = at, at + 1
        self.used = at
        self.rows = (at + 7) // 8 * 8


PLANS = (Plan(1, 2), Plan(SLOTS_HERE, 2), Plan(1, 3), Plan(SLOTS_HERE, PROMPTS))
DECAY_LANE = LAGS + PROMPTS * LAGS
FACTORS = 16
WINDOWS = 40


def call(kernel, out_shape, **kw):
    return pl.pallas_call(
        kernel,
        out_shape=out_shape,
        interpret=INTERPRET,
        compiler_params=pltpu.CompilerParams(vmem_limit_bytes=48 * 1024 * 1024),
        **kw,
    )


def vmem():
    return pl.BlockSpec(memory_space=pltpu.VMEM)


def hbm():
    return pl.BlockSpec(memory_space=pltpu.HBM)


def pinned(array):
    return array if INTERPRET else pltpu.with_memory_space_constraint(array, pltpu.HBM)


def smem():
    return pl.BlockSpec(memory_space=pltpu.SMEM)


def starts_of(len_ref):
    found = [jnp.int32(0)]
    for p in range(PROMPTS - 1):
        found.append(found[-1] + len_ref[p])
    return found


def iota(shape, axis):
    return lax.broadcasted_iota(jnp.int32, shape, axis)


def row_starts(locs, token):
    first = jnp.full(token.shape, locs[0], jnp.int32)
    for p in range(1, PROMPTS):
        first = jnp.where(token >= locs[p], locs[p], first)
    return first


def softplus(v):
    return jnp.maximum(v, 0.0) + jnp.log1p(jnp.exp(-jnp.abs(v)))


def silu(v):
    half = 0.5 * v
    return half + half * jnp.tanh(half)


def terms(v, axis):
    high = v.astype(BF).astype(F32)
    mid = (v - high).astype(BF).astype(F32)
    return jnp.concatenate([high, mid, v - high - mid], axis=axis)


def spread(per, count):
    shape = (count, count * per)
    return (iota(shape, 1) // per == iota(shape, 0)).astype(BF)


def nt_dot(a, b, **kw):
    return lax.dot_general(a, b, (((1,), (1,)), ((), ())), preferred_element_type=F32, **kw)


def live_matrix(locs):
    row, col = iota((TOK, TOK), 0), iota((TOK, TOK), 1)
    return (col <= row) & (col >= row_starts(locs, row))


def spread_terms(heads):
    shape = (3 * heads, heads * WIDTH)
    return (iota(shape, 1) // WIDTH == iota(shape, 0) % heads).astype(BF)


def widen(per_head_t):
    columns = terms(per_head_t, 0).T.astype(BF)
    return jnp.dot(columns, spread_terms(per_head_t.shape[0]), preferred_element_type=F32)


def exact_nt(v, zero_one):
    rows = v.shape[0]
    parts = nt_dot(terms(v, 0).astype(BF), zero_one.astype(BF))
    return parts[:rows] + parts[rows : 2 * rows] + parts[2 * rows :]


def plan_number(starts, slot_ref):
    crowd = jnp.int32(2)
    for p in range(PROMPTS - 2):
        crowd = jnp.where((starts[p + 1] - 1) // TOK == starts[p + 2] // TOK, 3, crowd)
    crowd = jnp.where((starts[1] - 1) // TOK == starts[3] // TOK, 4, crowd)
    shared = jnp.int32(0)
    for p in range(PROMPTS):
        for q in range(p):
            one, two = slot_ref[p], slot_ref[q]
            both = (one // SLOTS_HERE == two // SLOTS_HERE) & (one != two)
            shared = jnp.where(both, 1, shared)
    return jnp.where(crowd == 2, shared, jnp.where((crowd == 3) & (shared == 0), 2, 3))


def block_kernel(*refs):
    (
        len_hbm,
        slot_hbm,
        dt_hbm,
        alog_hbm,
        xc_hbm,
        xm_hbm,
        bc_hbm,
        tx_hbm,
        tbc_hbm,
        wx_hbm,
        wbc_hbm,
        prefix_hbm,
    ) = refs[:12]
    out_refs, refs = refs[12 : 12 + len(PLANS)], refs[12 + len(PLANS) :]
    act_ref, within_ref, delta_ref, bc_ref, taps_ref, number_hbm = refs[:6]
    (len_ref, slot_ref, dt_ref, alog_ref, xc_ref, xm_ref, tx_ref, tbc_ref, wx_ref) = refs[6:15]
    prefix_ref, x_scr, vals_scr, number_ref, sems = refs[15:]
    rows = PLANS[0].prefix
    ctx = lax.axis_index("ctx")
    heads = dt_ref.shape[0]
    chans = heads * WIDTH
    devices = out_refs[0].shape[0]
    group = lax.axis_index("head") * heads // HEADS_GROUP
    groups = bc_hbm.shape[1] // (2 * STATE)
    b_cols = pl.ds(pl.multiple_of(group * STATE, STATE), STATE)
    c_cols = pl.ds(pl.multiple_of((groups + group) * STATE, STATE), STATE)
    x_cols = pl.ds(pl.multiple_of(ctx * rows // STATE * STATE, STATE), STATE)
    copies = [
        pltpu.make_async_copy(src, dst, sems.at[n])
        for n, (src, dst) in enumerate(
            [
                (len_hbm, len_ref),
                (slot_hbm, slot_ref),
                (dt_hbm, dt_ref),
                (alog_hbm, alog_ref),
                (xc_hbm, xc_ref),
                (xm_hbm, xm_ref),
                (bc_hbm.at[:, b_cols], bc_ref.at[0]),
                (bc_hbm.at[:, c_cols], bc_ref.at[1]),
                (wx_hbm, wx_ref),
                (wbc_hbm.at[:, b_cols], taps_ref.at[1]),
                (wx_hbm.at[:, x_cols], taps_ref.at[0]),
                (wbc_hbm.at[:, c_cols], taps_ref.at[2]),
                (tx_hbm, tx_ref),
                (tbc_hbm.at[:, :, b_cols], tbc_ref.at[0]),
                (tbc_hbm.at[:, :, c_cols], tbc_ref.at[1]),
                (prefix_hbm, prefix_ref),
            ]
        )
    ]
    for copy in copies:
        copy.start()
    copies[0].wait()
    copies[1].wait()
    used = jnp.int32(0)
    for p in range(PROMPTS):
        used = jnp.where(slot_ref[p] // SLOTS_HERE == ctx, slot_ref[p] % SLOTS_HERE, used)
    starts = starts_of(len_ref)
    locs = [s - ctx * TOK for s in starts]
    number = plan_number(starts, slot_ref)
    number_ref[0] = number
    tell = pltpu.make_async_copy(number_ref, number_hbm, sems.at[len(copies)])
    tell.start()

    for copy in copies[2:-1]:
        copy.wait()
    scale = jnp.exp2(xc_ref[...].astype(F32)).T.astype(BF)
    wide = jnp.dot(scale, spread(MXB, xc_ref.shape[0]), preferred_element_type=F32)
    x = xm_ref[...].astype(F32) * wide
    b_raw = bc_ref[0].astype(F32)
    x_scr[8:, :chans] = x
    x_scr[8:, chans:] = b_raw
    x_scr[:8, :] = jnp.zeros((8, chans + STATE), F32)

    live = live_matrix(locs)
    delta = softplus(dt_ref[...])
    delta_ref[...] = delta
    log_decay = -jnp.exp(alog_ref[...].T) * delta
    within = exact_nt(log_decay, live)
    within_ref[...] = within
    token = iota((heads, TOK), 1)
    first = row_starts(locs, token)
    last_start = row_starts(locs, jnp.full((heads, TOK), TOK - 1, jnp.int32))
    to_end = delta * jnp.exp(jnp.where(token >= last_start, within[:, TOK - 1 :] - within, FAR))
    regular = (token >= LAGS) & (token - first >= LAGS)
    factor = widen(jnp.where(regular, to_end, 0.0))

    def chosen_rows(modulus, lowest):
        entry = iota((16, TOK), 0)
        begin = jnp.full((16, TOK), -TOK, jnp.int32)
        for p in range(PROMPTS):
            for i in range(LAGS):
                at = locs[p] + i
                inside = (len_ref[p] > i) & (at >= lowest) & (at < TOK)
                begin = jnp.where((entry == p % modulus * LAGS + i) & inside, at, begin)
        return iota((16, TOK), 1) == begin

    at_block = jnp.where((token < LAGS) & (token - first >= LAGS), to_end, 0.0)
    vals = exact_nt(to_end, chosen_rows(PROMPTS, 0))[:, : PROMPTS * LAGS]
    vals = jnp.concatenate(
        [at_block[:, :LAGS], vals, jnp.exp(within[:, TOK - 1 :]), jnp.zeros((heads, TOK - 16), F32)], axis=1
    )
    high = vals.astype(BF).astype(F32)
    low = vals - high
    vals_scr[0] = high
    vals_scr[1] = low

    taps = jnp.concatenate([wx_ref[...], taps_ref[1]], axis=1)
    conv = taps[LAGS : LAGS + 1] * x_scr[8:, :]
    for k in range(1, LAGS + 1):
        conv = conv + taps[LAGS - k : LAGS - k + 1] * x_scr[8 - k : 8 + TOK - k, :]
    act = silu(conv).astype(BF)
    act_ref[...] = act[:, :chans]
    inputs = (act[:, :chans].astype(F32) * factor).astype(BF)
    ends = lax.dot_general(
        inputs, act[:, chans:], (((0,), (0,)), ((), ())), preferred_element_type=F32
    ).astype(BF)
    for k in range(devices):
        out_refs[0][k, :rows, :] = ends[k * rows : (k + 1) * rows]

    def finish(plan, out_ref, x, b_raw, high, low):
        raw = jnp.concatenate([x, b_raw], axis=1).astype(BF)
        at_start = jnp.dot(chosen_rows(plan.begun, LAGS).astype(BF), raw, preferred_element_type=F32)
        at_start = at_start[: plan.begun * LAGS]
        tails_x, tails_b, tails_c = [], [], []
        for s in range(plan.slots):
            for i in range(LAGS):
                for found, two in ((tails_x, tx_ref[i]), (tails_b, tbc_ref[0, i]), (tails_c, tbc_ref[1, i])):
                    two = two.astype(F32)
                    found.append(jnp.where(used == 1, two[1:], two[:1]) if plan.slots == 1 else two[s : s + 1])
        tails = jnp.concatenate(tails_x, axis=0)
        c_last = bc_ref[1].astype(F32)[TOK - LAGS :]
        b_tile = jnp.concatenate([b_raw[:LAGS], c_last[:2], b_raw[TOK - LAGS :]], axis=0)
        foot = [at_start[:, chans:]] + tails_b + tails_c
        gap = jnp.zeros((1, STATE), F32)
        if plan.packed:
            gap = jnp.concatenate([gap, c_last[2:]], axis=0)
            unused = jnp.zeros((heads, STATE - 2 * FACTORS), F32)
            high = jnp.concatenate([high[:, :FACTORS], low[:, :FACTORS], unused], axis=1)
        else:
            gap = jnp.concatenate([gap, gap], axis=0)
            foot.append(c_last[2:])
        if plan.rows > plan.used:
            foot.append(jnp.zeros((plan.rows - plan.used, STATE), F32))
        foot = jnp.concatenate(foot, axis=0)
        tile_row = iota((8, STATE), 0)
        for c in range(chans // STATE):
            lanes = slice(c * STATE, (c + 1) * STATE)
            x_tile = jnp.concatenate([x[:LAGS, lanes], gap, x[TOK - LAGS :, lanes]], axis=0)
            part = jnp.concatenate([b_tile, at_start[:, lanes], tails[:, lanes], foot], axis=0).astype(BF)
            for k in range(c * STATE // rows, (c + 1) * STATE // rows):
                h = k * rows // WIDTH
                tile = jnp.where(tile_row == LAGS, high[h : h + 1], x_tile)
                if not plan.packed:
                    tile = jnp.where(tile_row == LAGS + 1, low[h : h + 1], tile)
                out_ref[k, plan.xb : plan.bb, :] = tile.astype(BF)
                out_ref[k, plan.bb :, :] = part

    finish(PLANS[0], out_refs[0], x, b_raw, high, low)
    copies[-1].wait()
    out_refs[0][:, rows : 2 * rows, :] = prefix_ref[used]

    tell.wait()

    @pl.when(number > 0)
    def _():
        for n, plan in list(enumerate(PLANS))[1:]:

            @pl.when(number == n)
            def _():
                out_refs[n][:, :rows, :] = out_refs[0][:, :rows, :]
                for s in range(plan.slots):
                    at = plan.prefix + s * rows
                    out_refs[n][:, at : at + rows, :] = prefix_ref[used if plan.slots == 1 else s]
                finish(plan, out_refs[n], x_scr[8:, :chans], x_scr[8:, chans:], vals_scr[0], vals_scr[1])


def tail_of(plan, got_ref, slot, tail_at):
    owner = got_ref[slot // SLOTS_HERE, plan.xb :, :].astype(F32)
    place = tail_at - plan.xb
    tail = owner[place : place + LAGS]
    if plan.slots > 1:
        tail = jnp.where(slot % SLOTS_HERE == 1, owner[place + LAGS : place + 2 * LAGS], tail)
    return tail


def scan_kernel(plan, len_ref, slot_ref, got_ref, taps_ref, out_ref, x_scr, b_scr, in_scr, mix_scr):
    devices = got_ref.shape[0]
    rows = plan.prefix
    ctx = lax.axis_index("ctx")
    at = ctx * rows % STATE
    starts = starts_of(len_ref)
    blocks = [s // TOK for s in starts]

    x_scr[...] = got_ref[:, plan.xb : plan.xb + 8, :].astype(F32).reshape(devices * 8, STATE)
    b_scr[...] = got_ref[:, plan.bb : plan.bb + 8, :].astype(F32).reshape(devices * 8, STATE)
    factors = x_scr[pl.ds(LAGS, devices, stride=8), :]
    if plan.packed:
        factors = factors[:, :FACTORS] + factors[:, FACTORS : 2 * FACTORS]
    else:
        factors = factors + x_scr[pl.ds(LAGS + 1, devices, stride=8), :]
    prompt_factors = jnp.sum(factors, axis=0, keepdims=True)

    def windows(scr, start_at, tail_at):
        before, now = [], []
        for p in range(PROMPTS):
            own = got_ref[blocks[p], plan.xb :, :].astype(F32)
            place = start_at - plan.xb + p % plan.begun * LAGS
            found = []
            for i in range(LAGS):
                row = (starts[p] + i) % TOK
                block = jnp.minimum((starts[p] + i) // TOK, devices - 1)
                early = scr[pl.ds(8 * block + jnp.minimum(row, LAGS - 1), 1), :]
                found.append(jnp.where(row < LAGS, early, own[place + i : place + i + 1]))
            now.append(found)
            before.append(tail_of(plan, got_ref, slot_ref[p], tail_at))
        pad = jnp.zeros((WINDOWS - devices - PROMPTS, STATE), F32)
        found = []
        for i in range(LAGS):
            last = scr[pl.ds(8 - LAGS + i, devices, stride=8), :]
            last = jnp.concatenate([last[devices - 1 :], last[: devices - 1]], axis=0)
            found.append(jnp.concatenate([last] + [b[i : i + 1] for b in before] + [pad], axis=0))
        for i in range(LAGS):
            fresh = scr[pl.ds(i, devices, stride=8), :]
            found.append(jnp.concatenate([fresh] + [n[i] for n in now] + [pad], axis=0))
        return found

    def activation(rows6, taps, i):
        conv = taps[LAGS : LAGS + 1] * rows6[LAGS + i]
        for k in range(1, LAGS + 1):
            conv = conv + taps[LAGS - k : LAGS - k + 1] * rows6[LAGS + i - k]
        return silu(conv).astype(BF).astype(F32)

    x_rows = windows(x_scr, plan.xp, plan.xt)
    b_rows = windows(b_scr, plan.bp, plan.bt)
    x_act = [activation(x_rows, taps_ref[0], i) for i in range(LAGS)]
    b_act = [activation(b_rows, taps_ref[1], i) for i in range(LAGS)]
    scaled = []
    for i in range(LAGS):
        column = [factors[:, i : i + 1]]
        for p in range(PROMPTS):
            lane = LAGS + p * LAGS + i
            column.append(prompt_factors[:, lane : lane + 1])
        column.append(jnp.zeros((WINDOWS - devices - PROMPTS, 1), F32))
        scaled.append(x_act[i] * jnp.concatenate(column, axis=0))
    spare = jnp.zeros((STATE - LAGS * WINDOWS, STATE), F32)
    in_scr[...] = jnp.concatenate(scaled + [spare], axis=0).T
    mine = in_scr[pl.ds(pl.multiple_of(at, rows), rows), :]
    lane = iota((rows, STATE), 1)
    target = lane % WINDOWS
    for p in range(PROMPTS):
        for i in range(LAGS):
            target = jnp.where(lane == i * WINDOWS + devices + p, (starts[p] + i) // TOK, target)
    for d in range(devices):
        mix_scr[d * rows : (d + 1) * rows, :] = jnp.where(target == d, mine, 0.0).astype(BF)
    b_all = jnp.concatenate(b_act + [spare], axis=0).astype(BF)
    extra = jnp.dot(mix_scr[...], b_all, preferred_element_type=F32)

    turn = at // rows
    from_prompts = jnp.where(
        turn == 0, x_act[0][devices:], jnp.where(turn == 1, x_act[1][devices:], x_act[2][devices:])
    )
    for i in range(LAGS):
        x_scr[pl.ds(i, devices, stride=8), :] = x_act[i][:devices]
    from_blocks = x_scr[...].reshape(devices, 8, STATE)
    out_ref[:, plan.prompts * rows :, :] = jnp.where(turn == LAGS, from_blocks, from_prompts[None]).astype(BF)

    prefixes = []
    for p in range(PROMPTS):
        slot = slot_ref[p]
        place = plan.prefix
        if plan.slots > 1:
            place = pl.multiple_of(place + (slot % SLOTS_HERE) * rows, rows)
        prefixes.append(got_ref[slot // SLOTS_HERE, pl.ds(place, rows), :])
    wide = [piece.astype(F32) for piece in prefixes]
    state = jnp.zeros((rows, STATE), F32)
    states = plan.prompts * rows
    for d in range(devices):
        out_ref[d, :rows, :] = state.astype(BF)
        out_ref[d, rows:states, :] = jnp.zeros((states - rows, STATE), BF)
        base = state
        for p in range(PROMPTS):
            base = jnp.where(blocks[p] == d, wide[p], base)
        decay = factors[d : d + 1, DECAY_LANE : DECAY_LANE + 1]
        state = decay * base + (got_ref[d, :rows, :].astype(F32) + extra[d * rows : (d + 1) * rows])
    for p in range(PROMPTS):
        place = jnp.int32(0)
        for q in range(p + 1):
            place = place + (starts[q] > blocks[p] * TOK).astype(jnp.int32)
        place = jnp.minimum(place, plan.prompts - 1)
        out_ref[blocks[p], pl.ds(pl.multiple_of(place * rows, rows), rows), :] = prefixes[p]


def read_kernel(
    plan,
    len_ref,
    slot_ref,
    sent_ref,
    got_ref,
    act_ref,
    bc_ref,
    taps_ref,
    within_ref,
    delta_ref,
    skip_ref,
    gate_ref,
    gated_ref,
    sq_ref,
    bc_scr,
):
    ctx = lax.axis_index("ctx")
    devices = got_ref.shape[0]
    heads = delta_ref.shape[0]
    chans = heads * WIDTH
    rows = chans // devices
    locs = [s - ctx * TOK for s in starts_of(len_ref)]

    token = iota((TOK, 16), 0)
    entry = iota((TOK, 16), 1)
    first = row_starts(locs, token)
    prompt = sum((token >= loc).astype(jnp.int32) for loc in locs) - 1

    bc_scr[8:, :] = jnp.concatenate([bc_ref[0], bc_ref[1]], axis=1).astype(F32)
    before = sent_ref[(ctx + devices - 1) % devices, plan.xb :, :].astype(F32)
    bc_scr[8 - LAGS : 8, :STATE] = before[16 - LAGS : 16]
    c_last = LAGS + 1 if plan.packed else plan.cp - plan.xb
    bc_scr[8 - LAGS : 8, STATE:] = jnp.concatenate(
        [before[8 + LAGS : 10 + LAGS], before[c_last : c_last + 1]], axis=0
    )
    tails = []
    for p in range(PROMPTS):
        pair = [tail_of(plan, sent_ref, slot_ref[p], at) for at in (plan.bt, plan.ct)]
        tails.append(jnp.concatenate(pair, axis=1))
    tails.append(jnp.zeros((16 - PROMPTS * LAGS, 2 * STATE), F32))
    tails = jnp.concatenate(tails, axis=0).astype(BF)
    taps = jnp.concatenate([taps_ref[1], taps_ref[2]], axis=1)
    conv = taps[LAGS : LAGS + 1] * bc_scr[8:, :]
    for k in range(1, LAGS + 1):
        outside = token - k < first
        pick = outside & (entry == prompt * LAGS + token - k - first + LAGS)
        tail_rows = jnp.dot(pick.astype(BF), tails, preferred_element_type=F32)
        value = jnp.where(outside[:, :1], tail_rows, bc_scr[8 - k : 8 + TOK - k, :])
        conv = conv + taps[LAGS - k : LAGS - k + 1] * value
    bc_act = silu(conv).astype(BF)
    b_act, c_act = bc_act[:, :STATE], bc_act[:, STATE:]

    near = token - first < LAGS
    by_prompt = (prompt == entry % PROMPTS) & (token - first == entry // PROMPTS) & near
    by_block = (token == entry - LAGS * PROMPTS) & (token < LAGS) & jnp.logical_not(near)
    pick = by_prompt | by_block
    other = (near | (token < LAGS))[:, :1]
    per = STATE // rows
    states = plan.prompts * rows
    spec = []
    for c in range(chans // STATE):
        spec.append(
            jnp.concatenate(
                [got_ref[c * per + j, states:, :].astype(F32)[:PROMPTS] for j in range(per)], axis=0
            )
        )
    spec = jnp.concatenate(spec, axis=1).astype(BF)
    patch = jnp.dot(pick.astype(BF), spec, preferred_element_type=F32)
    x_wide = jnp.where(other, patch, act_ref[...].astype(F32))

    live = live_matrix(locs)
    delta = delta_ref[...]
    within = within_ref[...]
    within_c = within.T
    scores = nt_dot(c_act, b_act)
    place = iota((TOK, STATE), 0)
    place = sum(((loc > 0) & (place >= loc)).astype(jnp.int32) for loc in locs)
    c_wide = c_act.astype(F32)
    reads = jnp.zeros((TOK, chans), F32)
    for j in range(plan.prompts):
        state = got_ref[:, j * rows : (j + 1) * rows, :].reshape(chans, STATE)
        reads = reads + nt_dot(jnp.where(place == j, c_wide, 0.0).astype(BF), state)
    y = widen(jnp.exp(within)) * reads
    skip = jnp.dot(terms(skip_ref[...], 1).astype(BF), spread_terms(heads), preferred_element_type=F32)
    left = iota((TOK, 2 * WIDTH), 1) < WIDTH
    part = jnp.zeros((TOK, TOK), F32)
    for j in range(heads // 2):
        pair = []
        for h in (2 * j, 2 * j + 1):
            fade = jnp.exp(jnp.where(live, within_c[:, h : h + 1] - within[h : h + 1, :], FAR))
            pair.append((scores * fade * delta[h : h + 1, :]).astype(BF))
        at = slice(2 * j * WIDTH, 2 * (j + 1) * WIDTH)
        x_pair = x_wide[:, at]
        both = jnp.concatenate([jnp.where(left, x_pair, 0.0), jnp.where(left, 0.0, x_pair)], axis=0)
        intra = jnp.dot(jnp.concatenate(pair, axis=1), both.astype(BF), preferred_element_type=F32)
        total = y[:, at] + (intra + skip[:, at] * x_pair)
        gated = total * silu(gate_ref[:, at].astype(F32))
        gated_ref[:, at] = gated
        part = part + gated * gated
    sq_ref[...] = jnp.sum(part.T, axis=0, keepdims=True)


def norm_kernel(gated_ref, sq_ref, gain_ref, out_hbm, out_scr, sems):
    inverse = lax.rsqrt((sq_ref[0] + sq_ref[1]) / (HEADS_GROUP * WIDTH) + EPS)
    inverse = jnp.broadcast_to(inverse, (TOK, TOK)).T
    rows = TOK // NORM_PARTS
    copies = []
    for part in range(NORM_PARTS):
        at = slice(part * rows, (part + 1) * rows)
        for c in range(out_scr.shape[1] // TOK):
            cols = slice(c * TOK, (c + 1) * TOK)
            out_scr[at, cols] = (gated_ref[at, cols] * inverse[at] * gain_ref[:, cols]).astype(BF)
        copies.append(pltpu.make_async_copy(out_scr.at[at], out_hbm.at[at], sems.at[part]))
        copies[-1].start()
    for copy in copies:
        copy.wait()


def on_device(
    x_mant,
    x_codes,
    bc_raw,
    gate_z,
    conv_x,
    conv_bc,
    dt_raw,
    a_log,
    d_skip,
    norm_gain,
    prompt_lengths,
    cache_slot,
    prefix_state,
    tail_x,
    tail_bc,
):
    devices = lax.axis_size("ctx")
    head_devices = lax.axis_size("head")
    heads = a_log.shape[0]
    chans = heads * WIDTH
    rows = chans // devices
    dt_t = dt_raw.T
    a_row = a_log.reshape(1, heads)
    skip_row = d_skip.reshape(1, heads)
    tail_x = jnp.transpose(tail_x, (1, 0, 2))
    tail_bc = jnp.transpose(tail_bc, (1, 0, 2))
    prefixes = prefix_state.reshape(SLOTS_HERE, devices, rows, STATE)

    sources = [
        prompt_lengths,
        cache_slot,
        dt_t,
        a_row,
        x_codes.T,
        x_mant,
        bc_raw,
        tail_x,
        tail_bc,
        conv_x,
        conv_bc,
    ]
    found = call(
        block_kernel,
        tuple(jax.ShapeDtypeStruct((devices, plan.rows, STATE), BF) for plan in PLANS)
        + (
            jax.ShapeDtypeStruct((TOK, chans), BF),
            jax.ShapeDtypeStruct((heads, TOK), F32),
            jax.ShapeDtypeStruct((heads, TOK), F32),
            jax.ShapeDtypeStruct((2, TOK, STATE), BF),
            jax.ShapeDtypeStruct((3, conv_x.shape[0], STATE), F32),
            jax.ShapeDtypeStruct((1,), jnp.int32),
        ),
        in_specs=[hbm()] * 12,
        out_specs=(vmem(),) * (5 + len(PLANS)) + (hbm(),),
        scratch_shapes=[pltpu.SMEM((PROMPTS,), jnp.int32)] * 2
        + [pltpu.VMEM(source.shape, source.dtype) for source in sources[2:6]]
        + [
            pltpu.VMEM(tail_x.shape, BF),
            pltpu.VMEM((2,) + tail_x.shape[:2] + (STATE,), BF),
            pltpu.VMEM(conv_x.shape, F32),
            pltpu.VMEM(prefixes.shape, BF),
            pltpu.VMEM((TOK + 8, chans + STATE), F32),
            pltpu.VMEM((2, heads, STATE), F32),
            pltpu.SMEM((1,), jnp.int32),
            pltpu.SemaphoreType.DMA((17,)),
        ],
    )(*[pinned(source) for source in sources + [prefixes]])
    messages, rest, number = found[: len(PLANS)], found[len(PLANS) : -1], found[-1]

    def second_part(plan, send1, act, within, delta, bc_here, taps):
        got1 = lax.all_to_all(send1, "ctx", 0, 0)
        send2 = call(
            functools.partial(scan_kernel, plan),
            jax.ShapeDtypeStruct((devices, plan.prompts * rows + 8, STATE), BF),
            in_specs=[smem(), smem()] + [vmem()] * 2,
            out_specs=vmem(),
            scratch_shapes=[
                pltpu.VMEM((devices * 8, STATE), F32),
                pltpu.VMEM((devices * 8, STATE), F32),
                pltpu.VMEM((STATE, STATE), F32),
                pltpu.VMEM((chans, STATE), BF),
            ],
        )(prompt_lengths, cache_slot, got1, taps)
        got2 = lax.all_to_all(send2, "ctx", 0, 0)
        return call(
            functools.partial(read_kernel, plan),
            (jax.ShapeDtypeStruct((TOK, chans), F32), jax.ShapeDtypeStruct((1, TOK), F32)),
            in_specs=[smem(), smem()] + [vmem()] * 9,
            out_specs=(vmem(), vmem()),
            scratch_shapes=[pltpu.VMEM((TOK + 8, 2 * STATE), F32)],
        )(
            prompt_lengths,
            cache_slot,
            got1,
            got2,
            act,
            bc_here,
            taps,
            within,
            delta,
            skip_row,
            gate_z,
        )

    gated, squares = lax.switch(
        number[0],
        [
            lambda plan=plan, message=message: second_part(plan, message, *rest)
            for plan, message in zip(PLANS, messages)
        ],
    )
    pairs = [[i, i + 1] for i in range(0, head_devices, 2)]
    both = lax.all_gather(squares, "head", axis_index_groups=pairs)
    return call(
        norm_kernel,
        jax.ShapeDtypeStruct((TOK, chans), BF),
        in_specs=[vmem()] * 3,
        out_specs=hbm(),
        scratch_shapes=[pltpu.VMEM((TOK, chans), BF), pltpu.SemaphoreType.DMA((NORM_PARTS,))],
    )(gated, both, norm_gain.reshape(1, chans))


def solution(mesh):
    in_specs = (
        P("ctx", "head"),
        P("ctx", "head"),
        P("ctx", None),
        P("ctx", "head"),
        P(None, "head"),
        P(),
        P("ctx", "head"),
        P("head"),
        P("head"),
        P("head"),
        P(),
        P(),
        P("ctx", "head", None),
        P("ctx", None, "head"),
        P("ctx", None, None),
    )
    out_specs = P("ctx", "head")
    return jax.shard_map(
        on_device, mesh=mesh, in_specs=in_specs, out_specs=out_specs, check_vma=False
    )
```

```python
import functools

import jax
import jax.numpy as jnp
from jax import lax
from jax.experimental import pallas as pl
from jax.experimental.pallas import tpu as pltpu
from jax.sharding import PartitionSpec as P

BF = jnp.bfloat16
F32 = jnp.float32
INTERPRET = False

TOK = 128
WIDTH = 64
STATE = 128
MXB = 32
LAGS = 3
PROMPTS = 4
HEADS_GROUP = 32
SLOTS_HERE = 2
EPS = 1e-05
FAR = -1e30
NORM_PARTS = 4


class Plan:
    def __init__(self, slots, prompts):
        self.slots, self.prompts = slots, prompts
        self.begun = prompts - 1
        at = 32
        self.prefix, at = at, at + 32 * slots
        self.xb, at = at, at + 8
        self.bb, at = at, at + 8
        self.xp, at = at, at + LAGS * self.begun
        self.xt, at = at, at + LAGS * slots
        self.bp, at = at, at + LAGS * self.begun
        self.bt, at = at, at + LAGS * slots
        self.ct, at = at, at + LAGS * slots
        self.packed = slots > 1
        if not self.packed:
            self.cp, at = at, at + 1
        self.used = at
        self.rows = (at + 7) // 8 * 8


PLANS = (Plan(1, 2), Plan(SLOTS_HERE, 2), Plan(1, 3), Plan(SLOTS_HERE, PROMPTS))
DECAY_LANE = LAGS + PROMPTS * LAGS
FACTORS = 16
WINDOWS = 40


def call(kernel, out_shape, **kw):
    return pl.pallas_call(
        kernel,
        out_shape=out_shape,
        interpret=INTERPRET,
        compiler_params=pltpu.CompilerParams(vmem_limit_bytes=48 * 1024 * 1024),
        **kw,
    )


def vmem():
    return pl.BlockSpec(memory_space=pltpu.VMEM)


def hbm():
    return pl.BlockSpec(memory_space=pltpu.HBM)


def pinned(array):
    return array if INTERPRET else pltpu.with_memory_space_constraint(array, pltpu.HBM)


def smem():
    return pl.BlockSpec(memory_space=pltpu.SMEM)


def starts_of(len_ref):
    found = [jnp.int32(0)]
    for p in range(PROMPTS - 1):
        found.append(found[-1] + len_ref[p])
    return found


def iota(shape, axis):
    return lax.broadcasted_iota(jnp.int32, shape, axis)


def row_starts(locs, token):
    first = jnp.full(token.shape, locs[0], jnp.int32)
    for p in range(1, PROMPTS):
        first = jnp.where(token >= locs[p], locs[p], first)
    return first


def softplus(v):
    return jnp.maximum(v, 0.0) + jnp.log1p(jnp.exp(-jnp.abs(v)))


def silu(v):
    half = 0.5 * v
    return half + half * jnp.tanh(half)


def terms(v, axis):
    high = v.astype(BF).astype(F32)
    mid = (v - high).astype(BF).astype(F32)
    return jnp.concatenate([high, mid, v - high - mid], axis=axis)


def spread(per, count):
    shape = (count, count * per)
    return (iota(shape, 1) // per == iota(shape, 0)).astype(BF)


def nt_dot(a, b, **kw):
    return lax.dot_general(a, b, (((1,), (1,)), ((), ())), preferred_element_type=F32, **kw)


def live_matrix(locs):
    row, col = iota((TOK, TOK), 0), iota((TOK, TOK), 1)
    return (col <= row) & (col >= row_starts(locs, row))


def spread_terms(heads):
    shape = (3 * heads, heads * WIDTH)
    return (iota(shape, 1) // WIDTH == iota(shape, 0) % heads).astype(BF)


def widen(per_head_t):
    columns = terms(per_head_t, 0).T.astype(BF)
    return jnp.dot(columns, spread_terms(per_head_t.shape[0]), preferred_element_type=F32)


def exact_nt(v, zero_one):
    rows = v.shape[0]
    parts = nt_dot(terms(v, 0).astype(BF), zero_one.astype(BF))
    return parts[:rows] + parts[rows : 2 * rows] + parts[2 * rows :]


def plan_number(starts, slot_ref):
    crowd = jnp.int32(2)
    for p in range(PROMPTS - 2):
        crowd = jnp.where((starts[p + 1] - 1) // TOK == starts[p + 2] // TOK, 3, crowd)
    crowd = jnp.where((starts[1] - 1) // TOK == starts[3] // TOK, 4, crowd)
    shared = jnp.int32(0)
    for p in range(PROMPTS):
        for q in range(p):
            one, two = slot_ref[p], slot_ref[q]
            both = (one // SLOTS_HERE == two // SLOTS_HERE) & (one != two)
            shared = jnp.where(both, 1, shared)
    return jnp.where(crowd == 2, shared, jnp.where((crowd == 3) & (shared == 0), 2, 3))


def block_kernel(*refs):
    (
        len_hbm,
        slot_hbm,
        dt_hbm,
        alog_hbm,
        xc_hbm,
        xm_hbm,
        bc_hbm,
        tx_hbm,
        tbc_hbm,
        wx_hbm,
        wbc_hbm,
        prefix_hbm,
    ) = refs[:12]
    out_refs, refs = refs[12 : 12 + len(PLANS)], refs[12 + len(PLANS) :]
    act_ref, within_ref, delta_ref, bc_ref, taps_ref, number_hbm = refs[:6]
    (len_ref, slot_ref, dt_ref, alog_ref, xc_ref, xm_ref, tx_ref, tbc_ref, wx_ref) = refs[6:15]
    prefix_ref, x_scr, vals_scr, number_ref, sems = refs[15:]
    rows = PLANS[0].prefix
    ctx = lax.axis_index("ctx")
    heads = dt_ref.shape[0]
    chans = heads * WIDTH
    devices = out_refs[0].shape[0]
    group = lax.axis_index("head") * heads // HEADS_GROUP
    groups = bc_hbm.shape[1] // (2 * STATE)
    b_cols = pl.ds(pl.multiple_of(group * STATE, STATE), STATE)
    c_cols = pl.ds(pl.multiple_of((groups + group) * STATE, STATE), STATE)
    x_cols = pl.ds(pl.multiple_of(ctx * rows // STATE * STATE, STATE), STATE)
    copies = [
        pltpu.make_async_copy(src, dst, sems.at[n])
        for n, (src, dst) in enumerate(
            [
                (len_hbm, len_ref),
                (slot_hbm, slot_ref),
                (dt_hbm, dt_ref),
                (alog_hbm, alog_ref),
                (xc_hbm, xc_ref),
                (xm_hbm, xm_ref),
                (bc_hbm.at[:, b_cols], bc_ref.at[0]),
                (bc_hbm.at[:, c_cols], bc_ref.at[1]),
                (wx_hbm, wx_ref),
                (wbc_hbm.at[:, b_cols], taps_ref.at[1]),
                (wx_hbm.at[:, x_cols], taps_ref.at[0]),
                (wbc_hbm.at[:, c_cols], taps_ref.at[2]),
                (tx_hbm, tx_ref),
                (tbc_hbm.at[:, :, b_cols], tbc_ref.at[0]),
                (tbc_hbm.at[:, :, c_cols], tbc_ref.at[1]),
                (prefix_hbm, prefix_ref),
            ]
        )
    ]
    for copy in copies:
        copy.start()
    copies[0].wait()
    copies[1].wait()
    used = jnp.int32(0)
    for p in range(PROMPTS):
        used = jnp.where(slot_ref[p] // SLOTS_HERE == ctx, slot_ref[p] % SLOTS_HERE, used)
    starts = starts_of(len_ref)
    locs = [s - ctx * TOK for s in starts]
    number = plan_number(starts, slot_ref)
    number_ref[0] = number
    tell = pltpu.make_async_copy(number_ref, number_hbm, sems.at[len(copies)])
    tell.start()

    for copy in copies[2:-1]:
        copy.wait()
    scale = jnp.exp2(xc_ref[...].astype(F32)).T.astype(BF)
    wide = jnp.dot(scale, spread(MXB, xc_ref.shape[0]), preferred_element_type=F32)
    x = xm_ref[...].astype(F32) * wide
    b_raw = bc_ref[0].astype(F32)
    x_scr[8:, :chans] = x
    x_scr[8:, chans:] = b_raw
    x_scr[:8, :] = jnp.zeros((8, chans + STATE), F32)

    live = live_matrix(locs)
    delta = softplus(dt_ref[...])
    delta_ref[...] = delta
    log_decay = -jnp.exp(alog_ref[...].T) * delta
    within = exact_nt(log_decay, live)
    within_ref[...] = within
    token = iota((heads, TOK), 1)
    first = row_starts(locs, token)
    last_start = row_starts(locs, jnp.full((heads, TOK), TOK - 1, jnp.int32))
    to_end = delta * jnp.exp(jnp.where(token >= last_start, within[:, TOK - 1 :] - within, FAR))
    regular = (token >= LAGS) & (token - first >= LAGS)
    factor = widen(jnp.where(regular, to_end, 0.0))

    def chosen_rows(modulus, lowest):
        entry = iota((16, TOK), 0)
        begin = jnp.full((16, TOK), -TOK, jnp.int32)
        for p in range(PROMPTS):
            for i in range(LAGS):
                at = locs[p] + i
                inside = (len_ref[p] > i) & (at >= lowest) & (at < TOK)
                begin = jnp.where((entry == p % modulus * LAGS + i) & inside, at, begin)
        return iota((16, TOK), 1) == begin

    at_block = jnp.where((token < LAGS) & (token - first >= LAGS), to_end, 0.0)
    vals = exact_nt(to_end, chosen_rows(PROMPTS, 0))[:, : PROMPTS * LAGS]
    vals = jnp.concatenate(
        [at_block[:, :LAGS], vals, jnp.exp(within[:, TOK - 1 :]), jnp.zeros((heads, TOK - 16), F32)], axis=1
    )
    high = vals.astype(BF).astype(F32)
    low = vals - high
    vals_scr[0] = high
    vals_scr[1] = low

    taps = jnp.concatenate([wx_ref[...], taps_ref[1]], axis=1)
    conv = taps[LAGS : LAGS + 1] * x_scr[8:, :]
    for k in range(1, LAGS + 1):
        conv = conv + taps[LAGS - k : LAGS - k + 1] * x_scr[8 - k : 8 + TOK - k, :]
    act = silu(conv).astype(BF)
    act_ref[...] = act[:, :chans]
    inputs = (act[:, :chans].astype(F32) * factor).astype(BF)
    ends = lax.dot_general(
        inputs, act[:, chans:], (((0,), (0,)), ((), ())), preferred_element_type=F32
    ).astype(BF)
    for k in range(devices):
        out_refs[0][k, :rows, :] = ends[k * rows : (k + 1) * rows]

    def finish(plan, out_ref, x, b_raw, high, low):
        raw = jnp.concatenate([x, b_raw], axis=1).astype(BF)
        at_start = jnp.dot(chosen_rows(plan.begun, LAGS).astype(BF), raw, preferred_element_type=F32)
        at_start = at_start[: plan.begun * LAGS]
        tails_x, tails_b, tails_c = [], [], []
        for s in range(plan.slots):
            for i in range(LAGS):
                for found, two in ((tails_x, tx_ref[i]), (tails_b, tbc_ref[0, i]), (tails_c, tbc_ref[1, i])):
                    two = two.astype(F32)
                    found.append(jnp.where(used == 1, two[1:], two[:1]) if plan.slots == 1 else two[s : s + 1])
        tails = jnp.concatenate(tails_x, axis=0)
        c_last = bc_ref[1].astype(F32)[TOK - LAGS :]
        b_tile = jnp.concatenate([b_raw[:LAGS], c_last[:2], b_raw[TOK - LAGS :]], axis=0)
        foot = [at_start[:, chans:]] + tails_b + tails_c
        gap = jnp.zeros((1, STATE), F32)
        if plan.packed:
            gap = jnp.concatenate([gap, c_last[2:]], axis=0)
            unused = jnp.zeros((heads, STATE - 2 * FACTORS), F32)
            high = jnp.concatenate([high[:, :FACTORS], low[:, :FACTORS], unused], axis=1)
        else:
            gap = jnp.concatenate([gap, gap], axis=0)
            foot.append(c_last[2:])
        if plan.rows > plan.used:
            foot.append(jnp.zeros((plan.rows - plan.used, STATE), F32))
        foot = jnp.concatenate(foot, axis=0)
        tile_row = iota((8, STATE), 0)
        for c in range(chans // STATE):
            lanes = slice(c * STATE, (c + 1) * STATE)
            x_tile = jnp.concatenate([x[:LAGS, lanes], gap, x[TOK - LAGS :, lanes]], axis=0)
            part = jnp.concatenate([b_tile, at_start[:, lanes], tails[:, lanes], foot], axis=0).astype(BF)
            for k in range(c * STATE // rows, (c + 1) * STATE // rows):
                h = k * rows // WIDTH
                tile = jnp.where(tile_row == LAGS, high[h : h + 1], x_tile)
                if not plan.packed:
                    tile = jnp.where(tile_row == LAGS + 1, low[h : h + 1], tile)
                out_ref[k, plan.xb : plan.bb, :] = tile.astype(BF)
                out_ref[k, plan.bb :, :] = part

    finish(PLANS[0], out_refs[0], x, b_raw, high, low)
    copies[-1].wait()
    out_refs[0][:, rows : 2 * rows, :] = prefix_ref[used]

    tell.wait()

    @pl.when(number > 0)
    def _():
        for n, plan in list(enumerate(PLANS))[1:]:

            @pl.when(number == n)
            def _():
                out_refs[n][:, :rows, :] = out_refs[0][:, :rows, :]
                for s in range(plan.slots):
                    at = plan.prefix + s * rows
                    out_refs[n][:, at : at + rows, :] = prefix_ref[used if plan.slots == 1 else s]
                finish(plan, out_refs[n], x_scr[8:, :chans], x_scr[8:, chans:], vals_scr[0], vals_scr[1])


def tail_of(plan, got_ref, slot, tail_at):
    owner = got_ref[slot // SLOTS_HERE, plan.xb :, :].astype(F32)
    place = tail_at - plan.xb
    tail = owner[place : place + LAGS]
    if plan.slots > 1:
        tail = jnp.where(slot % SLOTS_HERE == 1, owner[place + LAGS : place + 2 * LAGS], tail)
    return tail


def scan_kernel(plan, len_ref, slot_ref, got_ref, taps_ref, out_ref, x_scr, b_scr, in_scr, mix_scr, begin_scr):
    devices = got_ref.shape[0]
    rows = plan.prefix
    ctx = lax.axis_index("ctx")
    at = ctx * rows % STATE
    starts = starts_of(len_ref)
    blocks = [s // TOK for s in starts]

    x_scr[...] = got_ref[:, plan.xb : plan.xb + 8, :].astype(F32).reshape(devices * 8, STATE)
    b_scr[...] = got_ref[:, plan.bb : plan.bb + 8, :].astype(F32).reshape(devices * 8, STATE)
    factors = x_scr[pl.ds(LAGS, devices, stride=8), :]
    if plan.packed:
        factors = factors[:, :FACTORS] + factors[:, FACTORS : 2 * FACTORS]
    else:
        factors = factors + x_scr[pl.ds(LAGS + 1, devices, stride=8), :]
    prompt_factors = jnp.sum(factors, axis=0, keepdims=True)

    def windows(scr, start_at, tail_at):
        before, now = [], []
        for p in range(PROMPTS):
            own = got_ref[blocks[p], plan.xb :, :].astype(F32)
            place = start_at - plan.xb + p % plan.begun * LAGS
            found = []
            for i in range(LAGS):
                row = (starts[p] + i) % TOK
                block = jnp.minimum((starts[p] + i) // TOK, devices - 1)
                early = scr[pl.ds(8 * block + jnp.minimum(row, LAGS - 1), 1), :]
                found.append(jnp.where(row < LAGS, early, own[place + i : place + i + 1]))
            now.append(found)
            before.append(tail_of(plan, got_ref, slot_ref[p], tail_at))
        pad = jnp.zeros((WINDOWS - devices - PROMPTS, STATE), F32)
        found = []
        for i in range(LAGS):
            last = scr[pl.ds(8 - LAGS + i, devices, stride=8), :]
            last = jnp.concatenate([last[devices - 1 :], last[: devices - 1]], axis=0)
            found.append(jnp.concatenate([last] + [b[i : i + 1] for b in before] + [pad], axis=0))
        for i in range(LAGS):
            fresh = scr[pl.ds(i, devices, stride=8), :]
            found.append(jnp.concatenate([fresh] + [n[i] for n in now] + [pad], axis=0))
        return found

    def activation(rows6, taps, i):
        conv = taps[LAGS : LAGS + 1] * rows6[LAGS + i]
        for k in range(1, LAGS + 1):
            conv = conv + taps[LAGS - k : LAGS - k + 1] * rows6[LAGS + i - k]
        return silu(conv).astype(BF).astype(F32)

    x_rows = windows(x_scr, plan.xp, plan.xt)
    b_rows = windows(b_scr, plan.bp, plan.bt)
    x_act = [activation(x_rows, taps_ref[0], i) for i in range(LAGS)]
    b_act = [activation(b_rows, taps_ref[1], i) for i in range(LAGS)]
    scaled = []
    for i in range(LAGS):
        column = [factors[:, i : i + 1]]
        for p in range(PROMPTS):
            lane = LAGS + p * LAGS + i
            column.append(prompt_factors[:, lane : lane + 1])
        column.append(jnp.zeros((WINDOWS - devices - PROMPTS, 1), F32))
        scaled.append(x_act[i] * jnp.concatenate(column, axis=0))
    spare = jnp.zeros((STATE - LAGS * WINDOWS, STATE), F32)
    in_scr[...] = jnp.concatenate(scaled + [spare], axis=0).T
    mine = in_scr[pl.ds(pl.multiple_of(at, rows), rows), :]
    lane = iota((rows, STATE), 1)
    target = lane % WINDOWS
    for p in range(PROMPTS):
        for i in range(LAGS):
            target = jnp.where(lane == i * WINDOWS + devices + p, (starts[p] + i) // TOK, target)
    for d in range(devices):
        mix_scr[d * rows : (d + 1) * rows, :] = jnp.where(target == d, mine, 0.0).astype(BF)
    b_all = jnp.concatenate(b_act + [spare], axis=0).astype(BF)
    extra = jnp.dot(mix_scr[...], b_all, preferred_element_type=F32)

    turn = at // rows
    from_prompts = jnp.where(
        turn == 0, x_act[0][devices:], jnp.where(turn == 1, x_act[1][devices:], x_act[2][devices:])
    )
    for i in range(LAGS):
        x_scr[pl.ds(i, devices, stride=8), :] = x_act[i][:devices]
    from_blocks = x_scr[...].reshape(devices, 8, STATE)
    out_ref[:, plan.prompts * rows :, :] = jnp.where(turn == LAGS, from_blocks, from_prompts[None]).astype(BF)

    prefixes = []
    for p in range(PROMPTS):
        slot = slot_ref[p]
        place = plan.prefix
        if plan.slots > 1:
            place = pl.multiple_of(place + (slot % SLOTS_HERE) * rows, rows)
        prefixes.append(got_ref[slot // SLOTS_HERE, pl.ds(place, rows), :])
    for p in range(PROMPTS):
        begin_scr[blocks[p]] = prefixes[p].astype(F32)
    state = jnp.zeros((rows, STATE), F32)
    states = plan.prompts * rows
    for d in range(devices):
        out_ref[d, :rows, :] = state.astype(BF)
        out_ref[d, rows:states, :] = jnp.zeros((states - rows, STATE), BF)
        begins = functools.reduce(jnp.logical_or, [block == d for block in blocks])
        base = jnp.where(begins, begin_scr[d], state)
        decay = factors[d : d + 1, DECAY_LANE : DECAY_LANE + 1]
        state = decay * base + (got_ref[d, :rows, :].astype(F32) + extra[d * rows : (d + 1) * rows])
    for p in range(PROMPTS):
        place = jnp.int32(0)
        for q in range(p + 1):
            place = place + (starts[q] > blocks[p] * TOK).astype(jnp.int32)
        place = jnp.minimum(place, plan.prompts - 1)
        out_ref[blocks[p], pl.ds(pl.multiple_of(place * rows, rows), rows), :] = prefixes[p]


def read_kernel(
    plan,
    len_ref,
    slot_ref,
    sent_ref,
    got_ref,
    act_ref,
    bc_ref,
    taps_ref,
    within_ref,
    delta_ref,
    skip_ref,
    gate_ref,
    gated_ref,
    sq_ref,
    bc_scr,
):
    ctx = lax.axis_index("ctx")
    devices = got_ref.shape[0]
    heads = delta_ref.shape[0]
    chans = heads * WIDTH
    rows = chans // devices
    locs = [s - ctx * TOK for s in starts_of(len_ref)]

    token = iota((TOK, 16), 0)
    entry = iota((TOK, 16), 1)
    first = row_starts(locs, token)
    prompt = sum((token >= loc).astype(jnp.int32) for loc in locs) - 1

    bc_scr[8:, :] = jnp.concatenate([bc_ref[0], bc_ref[1]], axis=1).astype(F32)
    before = sent_ref[(ctx + devices - 1) % devices, plan.xb :, :].astype(F32)
    bc_scr[8 - LAGS : 8, :STATE] = before[16 - LAGS : 16]
    c_last = LAGS + 1 if plan.packed else plan.cp - plan.xb
    bc_scr[8 - LAGS : 8, STATE:] = jnp.concatenate(
        [before[8 + LAGS : 10 + LAGS], before[c_last : c_last + 1]], axis=0
    )
    tails = []
    for p in range(PROMPTS):
        pair = [tail_of(plan, sent_ref, slot_ref[p], at) for at in (plan.bt, plan.ct)]
        tails.append(jnp.concatenate(pair, axis=1))
    tails.append(jnp.zeros((16 - PROMPTS * LAGS, 2 * STATE), F32))
    tails = jnp.concatenate(tails, axis=0).astype(BF)
    taps = jnp.concatenate([taps_ref[1], taps_ref[2]], axis=1)
    conv = taps[LAGS : LAGS + 1] * bc_scr[8:, :]
    for k in range(1, LAGS + 1):
        outside = token - k < first
        pick = outside & (entry == prompt * LAGS + token - k - first + LAGS)
        tail_rows = jnp.dot(pick.astype(BF), tails, preferred_element_type=F32)
        value = jnp.where(outside[:, :1], tail_rows, bc_scr[8 - k : 8 + TOK - k, :])
        conv = conv + taps[LAGS - k : LAGS - k + 1] * value
    bc_act = silu(conv).astype(BF)
    b_act, c_act = bc_act[:, :STATE], bc_act[:, STATE:]

    near = token - first < LAGS
    by_prompt = (prompt == entry % PROMPTS) & (token - first == entry // PROMPTS) & near
    by_block = (token == entry - LAGS * PROMPTS) & (token < LAGS) & jnp.logical_not(near)
    pick = by_prompt | by_block
    other = (near | (token < LAGS))[:, :1]
    per = STATE // rows
    states = plan.prompts * rows
    spec = []
    for c in range(chans // STATE):
        spec.append(
            jnp.concatenate(
                [got_ref[c * per + j, states:, :].astype(F32)[:PROMPTS] for j in range(per)], axis=0
            )
        )
    spec = jnp.concatenate(spec, axis=1).astype(BF)
    patch = jnp.dot(pick.astype(BF), spec, preferred_element_type=F32)
    x_wide = jnp.where(other, patch, act_ref[...].astype(F32))

    live = live_matrix(locs)
    delta = delta_ref[...]
    within = within_ref[...]
    within_c = within.T
    scores = nt_dot(c_act, b_act)
    place = iota((TOK, STATE), 0)
    place = sum(((loc > 0) & (place >= loc)).astype(jnp.int32) for loc in locs)
    c_wide = c_act.astype(F32)
    reads = jnp.zeros((TOK, chans), F32)
    for j in range(plan.prompts):
        state = got_ref[:, j * rows : (j + 1) * rows, :].reshape(chans, STATE)
        reads = reads + nt_dot(jnp.where(place == j, c_wide, 0.0).astype(BF), state)
    y = widen(jnp.exp(within)) * reads
    skip = jnp.dot(terms(skip_ref[...], 1).astype(BF), spread_terms(heads), preferred_element_type=F32)
    left = iota((TOK, 2 * WIDTH), 1) < WIDTH
    part = jnp.zeros((TOK, TOK), F32)
    for j in range(heads // 2):
        pair = []
        for h in (2 * j, 2 * j + 1):
            fade = jnp.exp(jnp.where(live, within_c[:, h : h + 1] - within[h : h + 1, :], FAR))
            pair.append((scores * fade * delta[h : h + 1, :]).astype(BF))
        at = slice(2 * j * WIDTH, 2 * (j + 1) * WIDTH)
        x_pair = x_wide[:, at]
        both = jnp.concatenate([jnp.where(left, x_pair, 0.0), jnp.where(left, 0.0, x_pair)], axis=0)
        intra = jnp.dot(jnp.concatenate(pair, axis=1), both.astype(BF), preferred_element_type=F32)
        total = y[:, at] + (intra + skip[:, at] * x_pair)
        gated = total * silu(gate_ref[:, at].astype(F32))
        gated_ref[:, at] = gated
        part = part + gated * gated
    sq_ref[...] = jnp.sum(part.T, axis=0, keepdims=True)


def norm_kernel(gated_ref, sq_ref, gain_ref, out_hbm, out_scr, sems):
    inverse = lax.rsqrt((sq_ref[0] + sq_ref[1]) / (HEADS_GROUP * WIDTH) + EPS)
    inverse = jnp.broadcast_to(inverse, (TOK, TOK)).T
    rows = TOK // NORM_PARTS
    copies = []
    for part in range(NORM_PARTS):
        at = slice(part * rows, (part + 1) * rows)
        for c in range(out_scr.shape[1] // TOK):
            cols = slice(c * TOK, (c + 1) * TOK)
            out_scr[at, cols] = (gated_ref[at, cols] * inverse[at] * gain_ref[:, cols]).astype(BF)
        copies.append(pltpu.make_async_copy(out_scr.at[at], out_hbm.at[at], sems.at[part]))
        copies[-1].start()
    for copy in copies:
        copy.wait()


def on_device(
    x_mant,
    x_codes,
    bc_raw,
    gate_z,
    conv_x,
    conv_bc,
    dt_raw,
    a_log,
    d_skip,
    norm_gain,
    prompt_lengths,
    cache_slot,
    prefix_state,
    tail_x,
    tail_bc,
):
    devices = lax.axis_size("ctx")
    head_devices = lax.axis_size("head")
    heads = a_log.shape[0]
    chans = heads * WIDTH
    rows = chans // devices
    dt_t = dt_raw.T
    a_row = a_log.reshape(1, heads)
    skip_row = d_skip.reshape(1, heads)
    tail_x = jnp.transpose(tail_x, (1, 0, 2))
    tail_bc = jnp.transpose(tail_bc, (1, 0, 2))
    prefixes = prefix_state.reshape(SLOTS_HERE, devices, rows, STATE)

    sources = [
        prompt_lengths,
        cache_slot,
        dt_t,
        a_row,
        x_codes.T,
        x_mant,
        bc_raw,
        tail_x,
        tail_bc,
        conv_x,
        conv_bc,
    ]
    found = call(
        block_kernel,
        tuple(jax.ShapeDtypeStruct((devices, plan.rows, STATE), BF) for plan in PLANS)
        + (
            jax.ShapeDtypeStruct((TOK, chans), BF),
            jax.ShapeDtypeStruct((heads, TOK), F32),
            jax.ShapeDtypeStruct((heads, TOK), F32),
            jax.ShapeDtypeStruct((2, TOK, STATE), BF),
            jax.ShapeDtypeStruct((3, conv_x.shape[0], STATE), F32),
            jax.ShapeDtypeStruct((1,), jnp.int32),
        ),
        in_specs=[hbm()] * 12,
        out_specs=(vmem(),) * (5 + len(PLANS)) + (hbm(),),
        scratch_shapes=[pltpu.SMEM((PROMPTS,), jnp.int32)] * 2
        + [pltpu.VMEM(source.shape, source.dtype) for source in sources[2:6]]
        + [
            pltpu.VMEM(tail_x.shape, BF),
            pltpu.VMEM((2,) + tail_x.shape[:2] + (STATE,), BF),
            pltpu.VMEM(conv_x.shape, F32),
            pltpu.VMEM(prefixes.shape, BF),
            pltpu.VMEM((TOK + 8, chans + STATE), F32),
            pltpu.VMEM((2, heads, STATE), F32),
            pltpu.SMEM((1,), jnp.int32),
            pltpu.SemaphoreType.DMA((17,)),
        ],
    )(*[pinned(source) for source in sources + [prefixes]])
    messages, rest, number = found[: len(PLANS)], found[len(PLANS) : -1], found[-1]

    def second_part(plan, send1, act, within, delta, bc_here, taps):
        got1 = lax.all_to_all(send1, "ctx", 0, 0)
        send2 = call(
            functools.partial(scan_kernel, plan),
            jax.ShapeDtypeStruct((devices, plan.prompts * rows + 8, STATE), BF),
            in_specs=[smem(), smem()] + [vmem()] * 2,
            out_specs=vmem(),
            scratch_shapes=[
                pltpu.VMEM((devices * 8, STATE), F32),
                pltpu.VMEM((devices * 8, STATE), F32),
                pltpu.VMEM((STATE, STATE), F32),
                pltpu.VMEM((chans, STATE), BF),
                pltpu.VMEM((devices, rows, STATE), F32),
            ],
        )(prompt_lengths, cache_slot, got1, taps)
        got2 = lax.all_to_all(send2, "ctx", 0, 0)
        return call(
            functools.partial(read_kernel, plan),
            (jax.ShapeDtypeStruct((TOK, chans), F32), jax.ShapeDtypeStruct((1, TOK), F32)),
            in_specs=[smem(), smem()] + [vmem()] * 9,
            out_specs=(vmem(), vmem()),
            scratch_shapes=[pltpu.VMEM((TOK + 8, 2 * STATE), F32)],
        )(
            prompt_lengths,
            cache_slot,
            got1,
            got2,
            act,
            bc_here,
            taps,
            within,
            delta,
            skip_row,
            gate_z,
        )

    gated, squares = lax.switch(
        number[0],
        [
            lambda plan=plan, message=message: second_part(plan, message, *rest)
            for plan, message in zip(PLANS, messages)
        ],
    )
    pairs = [[i, i + 1] for i in range(0, head_devices, 2)]
    both = lax.all_gather(squares, "head", axis_index_groups=pairs)
    return call(
        norm_kernel,
        jax.ShapeDtypeStruct((TOK, chans), BF),
        in_specs=[vmem()] * 3,
        out_specs=hbm(),
        scratch_shapes=[pltpu.VMEM((TOK, chans), BF), pltpu.SemaphoreType.DMA((NORM_PARTS,))],
    )(gated, both, norm_gain.reshape(1, chans))


def solution(mesh):
    in_specs = (
        P("ctx", "head"),
        P("ctx", "head"),
        P("ctx", None),
        P("ctx", "head"),
        P(None, "head"),
        P(),
        P("ctx", "head"),
        P("head"),
        P("head"),
        P("head"),
        P(),
        P(),
        P("ctx", "head", None),
        P("ctx", None, "head"),
        P("ctx", None, None),
    )
    out_specs = P("ctx", "head")
    return jax.shard_map(
        on_device, mesh=mesh, in_specs=in_specs, out_specs=out_specs, check_vma=False
    )
```
